32 devices in a mesh: clip: 4 (over z), frame: 2 (over y), row: 4 (over x, core).
Axes of the slice: x: 2, y: 2, z: 4, core: 2. Of those that a mesh axis runs over, the one named last changes fastest.
Arguments:
- tokens: bfloat16 [16, 256, 8, 1024], P('frame', 'row', 'clip'), may hold values from -6 to 6
- context: int32 [8], P('clip'), may hold values from 1 to 15
- noise_mod: float32 [16, 8, 6, 1024], P('frame', 'clip'), may hold values from -4 to 4
- clean_mod: float32 [6, 1024], replicated, may hold values from -4 to 4
- w_qkv: bfloat16 [1024, 3072], replicated, may hold values from -0.1875 to 0.1875
- b_qkv: float32 [3072], replicated, may hold values from -3 to 3
- w_out: bfloat16 [1024, 1024], replicated, may hold values from -1.5 to 1.5
- b_out: float32 [1024], replicated, may hold values from -3 to 3
- w_up: bfloat16 [1024, 4096], replicated, may hold values from -0.1875 to 0.1875
- b_up: float32 [4096], replicated, may hold values from -3 to 3
- w_down: bfloat16 [4096, 1024], replicated, may hold values from -0.09375 to 0.09375
- b_down: float32 [1024], replicated, may hold values from -3 to 3
- cotangent: bfloat16 [16, 256, 8, 1024], P('frame', 'row', 'clip'), may hold values from -6 to 6
Outputs:
- output: bfloat16 [16, 256, 8, 1024], P('frame', 'row', 'clip')
- grad_tokens: float32 [16, 256, 8, 1024], P('frame', 'row', 'clip')
- grad_noise_mod: float32 [16, 8, 6, 1024], P('frame', 'clip', None, 'row')
- grad_clean_mod: float32 [6, 1024], P(None, ('clip', 'frame', 'row'))
- grad_w_qkv: float32 [1024, 3072], P(('clip', 'frame', 'row'))
- grad_b_qkv: float32 [3072], P(('clip', 'frame', 'row'))
- grad_w_out: float32 [1024, 1024], P(('clip', 'frame', 'row'))
- grad_b_out: float32 [1024], P(('clip', 'frame', 'row'))
- grad_w_up: float32 [1024, 4096], P(('clip', 'frame', 'row'))
- grad_b_up: float32 [4096], P(('clip', 'frame', 'row'))
- grad_w_down: float32 [4096, 1024], P(('clip', 'frame', 'row'))
- grad_b_down: float32 [1024], P(('clip', 'frame', 'row'))
The draws below stay inside these ranges and needn't reach their ends.
Inputs may be any that keep to these rules, and one draw needn't show every extreme that they name: The first context[c] frames of clip c are clean context.
All inputs are finite; a program needn't handle non-finite values.
Results may differ from the reference program's by a relative error of at most 0.017.
The reference program's roundings to bfloat16 on the way count: a program that leaves them out, or rounds other values in their place, can miss the bound.
Values may be sent and summed in bfloat16 or wider, within the bound.
A program may use at most 384 MiB of HBM per device.

```python
import jax
import jax.numpy as jnp
from jax import lax

D = 1024
HEADS = 16
HEAD_DIM = 64
FF = 4096
FRAMES = 16
GRID = 16
PATCHES = 256
CLIPS = 8


def set_ends(drawn, rng, low, largest):
    longest = drawn.shape.index(max(drawn.shape))
    spots = []
    for shift in (0, 1):
        where = [jax.random.randint(jax.random.fold_in(rng, axis), (), 0, length) for axis, length in enumerate(drawn.shape)]
        where[longest] = (where[longest] + shift) % drawn.shape[longest]
        spots.append(tuple(where))
    return drawn.at[spots[0]].set(low).at[spots[1]].set(largest)


def level_of(rng, shape, pieces, low, top_value):
    gain, own = 1.0, jax.random.fold_in(rng, 6)
    for dim, blocks in pieces:
        draws = jnp.exp(jax.random.uniform(jax.random.fold_in(own, dim), (blocks,), jnp.float32, low / len(pieces), top_value / len(pieces)))
        gain = gain * jnp.repeat(draws, shape[dim] // blocks).reshape([-1 if axis == dim else 1 for axis in range(len(shape))])
    return gain


def bell_draw(rng, extent, deviation, most, pieces=(), dtype=jnp.bfloat16):
    values = jax.random.normal(rng, extent, jnp.float32) * deviation
    if len(pieces) > 0:
        values = level_of(rng, extent, pieces, -0.22, 0.18) * values
    return jnp.clip(values, min=-most, max=most).astype(dtype)


def setup_inputs(seed: int = 0) -> dict:
    seeds = jax.random.split(jax.random.key(seed), 14)
    return {
        "tokens": bell_draw(seeds[0], (FRAMES, PATCHES, CLIPS, D), 1.0, 6.0, ((0, 2), (1, 4), (2, 4))),
        "context": set_ends(jax.random.randint(seeds[1], (CLIPS,), 1, FRAMES), jax.random.fold_in(seeds[1], 1), 1, FRAMES - 1).astype(jnp.int32),
        "noise_mod": bell_draw(seeds[2], (FRAMES, CLIPS, 6, D), 1.0, 4.0, ((0, 2), (1, 4)), jnp.float32),
        "clean_mod": bell_draw(seeds[3], (6, D), 1.0, 4.0, (), jnp.float32),
        "w_qkv": bell_draw(seeds[4], (D, 3 * D), D ** -0.5, 0.1875),
        "b_qkv": bell_draw(seeds[5], (3 * D,), 0.5, 3.0, (), jnp.float32),
        "w_out": bell_draw(seeds[6], (D, D), (D // 64) ** -0.5, 1.5),
        "b_out": bell_draw(seeds[7], (D,), 0.5, 3.0, (), jnp.float32),
        "w_up": bell_draw(seeds[8], (D, FF), D ** -0.5, 0.1875),
        "b_up": bell_draw(seeds[9], (FF,), 0.5, 3.0, (), jnp.float32),
        "w_down": bell_draw(seeds[10], (FF, D), FF ** -0.5, 0.09375),
        "b_down": bell_draw(seeds[11], (D,), 0.5, 3.0, (), jnp.float32),
        "cotangent": bell_draw(seeds[12], (FRAMES, PATCHES, CLIPS, D), 1.0, 6.0, ((0, 2), (1, 4), (2, 4))),
    }


@jax.custom_vjp
def low(v):
    return lax.optimization_barrier(v.astype(jnp.bfloat16)).astype(jnp.float32)

@jax.custom_vjp
def low_back(v):
    return v

def low_keep(v):
    return (low(v), None)

def low_pass(kept, grad):
    return (grad,)

def back_keep(v):
    return (v, None)

def back_low(kept, grad):
    return (low(grad),)
low.defvjp(low_keep, low_pass)
low_back.defvjp(back_keep, back_low)

def rope_angles(frame_pos, patch_pos):
    pair_index = jnp.arange(32)
    is_time = pair_index < 8
    is_height = (pair_index >= 8) & (pair_index < 20)
    exponent = jnp.where(is_time, pair_index / 8.0, jnp.where(is_height, (pair_index - 8) / 12.0, (pair_index - 20) / 12.0)).astype(jnp.float32)
    frequency = jnp.power(jnp.float32(10000.0), -exponent)
    position = jnp.where(is_time[None, :], frame_pos[:, None], jnp.where(is_height[None, :], (patch_pos // GRID)[:, None], (patch_pos % GRID)[:, None])).astype(jnp.float32)
    angle = position * frequency[None, :]
    return (jnp.cos(angle), jnp.sin(angle))

def rotate(values_in, cosine, sine_table):
    half_dim = values_in.shape[-1] // 2
    shape_b = (cosine.shape[0],) + (1,) * (values_in.ndim - 2) + (half_dim,)
    cos_b = cosine.reshape(shape_b)
    sin_b = sine_table.reshape(shape_b)
    first_half = values_in[..., :half_dim]
    second_half = values_in[..., half_dim:]
    return jnp.concatenate([first_half * cos_b - second_half * sin_b, first_half * sin_b + second_half * cos_b], axis=-1)

def layer_norm(values_in):
    centre = values_in - lax.optimization_barrier(jnp.mean(values_in, axis=-1, keepdims=True))
    spread = lax.optimization_barrier(jnp.mean(centre * centre, axis=-1, keepdims=True))
    return centre * lax.rsqrt(spread + 1e-06)

def clip_forward(tokens_c, mod_c, param_set, flags_c):
    clean_mod, w_qkv, b_qkv, w_out, b_out, w_up, b_up, w_down, b_down = param_set
    highest = lax.Precision.HIGHEST
    token_count = FRAMES * PATCHES
    chosen = jnp.where(flags_c[:, None, None], clean_mod[None], mod_c)
    per_token = jnp.broadcast_to(chosen[:, None], (FRAMES, PATCHES, 6, D)).reshape(token_count, 6, D)
    flat_in = tokens_c.reshape(token_count, D)
    hidden_one = low(layer_norm(flat_in) * (1.0 + per_token[:, 1]) + per_token[:, 0])
    projected = low_back(jnp.dot(hidden_one, w_qkv, precision=highest) + b_qkv)
    token_ids = jnp.arange(token_count)
    cosine, sine_table = rope_angles(token_ids // PATCHES, token_ids % PATCHES)
    query_rot = low(rotate(projected[:, :D].reshape(token_count, HEADS, HEAD_DIM), cosine, sine_table))
    key_rot = low(rotate(projected[:, D:2 * D].reshape(token_count, HEADS, HEAD_DIM), cosine, sine_table))
    value_low = low(projected[:, 2 * D:].reshape(token_count, HEADS, HEAD_DIM))
    frame_ids = token_ids // PATCHES
    allowed = frame_ids[None, :] <= frame_ids[:, None]

    def one_head(triple):
        query_h, key_h, value_h = triple
        scores = low_back(HEAD_DIM ** (-0.5) * jnp.dot(query_h, key_h.T, precision=highest))
        scores = jnp.where(allowed, scores, -jnp.inf)
        weights = jax.nn.softmax(scores, axis=-1)
        return jnp.dot(low(weights), value_h, precision=highest)
    heads_out = lax.map(jax.checkpoint(one_head), (query_rot.transpose(1, 0, 2), key_rot.transpose(1, 0, 2), value_low.transpose(1, 0, 2)))
    attn = low(low_back(heads_out.transpose(1, 0, 2).reshape(token_count, D)))
    branch = low_back(jnp.dot(attn, w_out, precision=highest) + b_out)
    mixed = flat_in + per_token[:, 2] * branch
    hidden_two = low(layer_norm(mixed) * (1.0 + per_token[:, 4]) + per_token[:, 3])
    pre_act = low_back(jnp.dot(hidden_two, w_up, precision=highest) + b_up)
    act_low = low(jax.nn.gelu(pre_act, approximate=True))
    down_out = low_back(jnp.dot(act_low, w_down, precision=highest) + b_down)
    result = mixed + per_token[:, 5] * down_out
    return result.reshape(FRAMES, PATCHES, D)

def reference(tokens, context, noise_mod, clean_mod, w_qkv, b_qkv, w_out, b_out, w_up, b_up, w_down, b_down, cotangent):
    param_set = tuple((item.astype(jnp.float32) for item in (clean_mod, w_qkv, b_qkv, w_out, b_out, w_up, b_up, w_down, b_down)))
    clip_tokens = jnp.moveaxis(tokens.astype(jnp.float32), 2, 0)
    clip_cots = jnp.moveaxis(cotangent.astype(jnp.float32), 2, 0)
    clip_mods = jnp.moveaxis(noise_mod.astype(jnp.float32), 1, 0)
    clean_flags = jnp.arange(FRAMES)[None, :] < context[:, None]

    def one_clip(totals, item):
        tokens_c, cot_c, mod_c, flags_c = item

        def forward_c(tok_in, mod_in, par_in):
            return clip_forward(tok_in, mod_in, par_in, flags_c)
        output_c, pull_back = jax.vjp(forward_c, tokens_c, mod_c, param_set)
        grad_tok, grad_mod, grad_par = pull_back(cot_c)
        totals = jax.tree.map(lambda acc_in, new_in: acc_in + new_in, totals, grad_par)
        return (totals, (output_c, grad_tok, grad_mod))
    zero_set = jax.tree.map(jnp.zeros_like, param_set)
    totals, (outputs, grads_tok, grads_mod) = lax.scan(one_clip, zero_set, (clip_tokens, clip_cots, clip_mods, clean_flags))
    return (jnp.moveaxis(outputs, 0, 2).astype(jnp.bfloat16), jnp.moveaxis(grads_tok, 0, 2), jnp.moveaxis(grads_mod, 0, 1), totals[0], totals[1], totals[2], totals[3], totals[4], totals[5], totals[6], totals[7], totals[8])
```

```python
import functools
import jax, jax.numpy as jnp
from jax import lax
from jax.experimental import pallas as pl
from jax.experimental.pallas import tpu as pltpu
from jax.sharding import PartitionSpec as P
HD = 64
NN = (((1,), (0,)), ((), ()))
NT = (((1,), (1,)), ((), ()))
def dot(a, b, dims):
    return lax.dot_general(a, b, dims, preferred_element_type=jnp.float32)

def head_mask(values, head, heads):
    if heads == 1:
        return values
    lane = lax.broadcasted_iota(jnp.int32, values.shape, 1)
    return jnp.where(lane // HD == head, values, jnp.zeros_like(values))


def fwd_kernel(x_ref, o_ref, ot_ref, lse_ref, qm, kf, vt, sb, acc, mrow):
    nf, nr, fl, pt, width = x_ref.shape
    lw = width // 3
    nh = lw // HD
    tok = nr * pt
    frames = nf * fl
    blk = 2 * tok
    nblk = frames // 2
    def load(f, _):
        part = x_ref[f // fl, :, f % fl].reshape(tok, width)
        rows = pl.ds(pl.multiple_of(f * tok, tok), tok)
        q = part[:, :lw] * jnp.bfloat16(HD ** -0.5)
        for h in range(nh):
            qm[h, rows, :] = head_mask(q, h, nh)
        kf[rows, :] = part[:, lw:2 * lw]
        vt[:, rows] = part[:, 2 * lw:].T
        return 0
    lax.fori_loop(0, frames, load, 0)

    def fold(v, op):
        return op(v.reshape(v.shape[0] // 8, 8, v.shape[1]), axis=0)

    def stage(cur, nxt, grow):
        zero8 = jnp.zeros((8, blk), jnp.float32)
        if nxt is not None:
            na, nhd, ns = nxt
            n0 = pl.multiple_of(na * blk, blk)
            n1 = pl.multiple_of(na * blk + tok, tok)
            ncols = pl.ds(n0, blk)
            s0 = dot(kf[pl.ds(n0, tok), :], qm[nhd, ncols, :], NT)
            s1 = dot(kf[pl.ds(n1, tok), :], qm[nhd, pl.ds(n1, tok), :], NT)
            sb[ns, pl.ds(n0, tok), :] = s0
            sb[ns, pl.ds(n1, tok), tok:] = s1
            m0 = fold(s0, jnp.max)
            mm = jnp.concatenate([m0[:, :tok], jnp.maximum(m0[:, tok:], fold(s1, jnp.max))], axis=1)
        else:
            mm = zero8
        if cur is not None:
            ca, chd, cs = cur
            hs = slice(chd * HD, (chd + 1) * HD)
            c0 = pl.multiple_of(ca * blk, blk)
            c1 = pl.multiple_of(ca * blk + tok, tok)
            m = mrow[cs]
            p0 = jnp.exp(sb[cs, pl.ds(c0, tok), :] - m)
            p1 = jnp.exp(sb[cs, pl.ds(c1, tok), tok:] - m[:, tok:])
            l0 = fold(p0, jnp.sum)
            ll = jnp.concatenate([l0[:, :tok], l0[:, tok:] + fold(p1, jnp.sum)], axis=1)
            a0 = dot(vt[hs, pl.ds(c0, tok)], p0.astype(jnp.bfloat16), NN)
            a1 = dot(vt[hs, pl.ds(c1, tok)], p1.astype(jnp.bfloat16), NN)
            acc[hs, :tok] = a0[:, :tok]
            acc[hs, tok:] = a0[:, tok:] + a1
        else:
            ll = zero8
        def score(b, mm):
            rows = pl.ds(pl.multiple_of(b * blk, blk), blk)
            s = dot(kf[rows, :], qm[nhd, ncols, :], NT)
            sb[ns, rows, :] = s
            return jnp.maximum(mm, fold(s, jnp.max))
        def body(b, carry):
            mm, ll = carry
            if nxt is not None:
                mm = score(b, mm)
            if cur is not None:
                rows = pl.ds(pl.multiple_of(b * blk, blk), blk)
                p = jnp.exp(sb[cs, rows, :] - m)
                ll = ll + fold(p, jnp.sum)
                acc[hs, :] += dot(vt[hs, rows], p.astype(jnp.bfloat16), NN)
            return mm, ll
        trip = nxt[0] if cur is None else cur[0]
        mm, ll = lax.fori_loop(0, trip, body, (mm, ll))
        if grow and nxt is not None:
            mm = score(cur[0], mm)
        if nxt is not None:
            mrow[ns] = jnp.max(mm, axis=0, keepdims=True)
        if cur is not None:
            l = jnp.sum(ll, axis=0, keepdims=True)
            ot = acc[hs, :] / l
            acc[hs, :] = ot
            cols = pl.ds(c0, blk)
            ot_ref[hs, cols] = ot
            lse_ref[chd:chd + 1, cols] = m + jnp.log(l)

    def finish(a):
        o = acc[...].T.astype(jnp.bfloat16)
        for j in range(2):
            f = 2 * a + j
            o_ref[f // fl, :, f % fl] = o[j * tok:(j + 1) * tok].reshape(nr, pt, lw)

    slots = sb.shape[0]
    def q_block(a, last):
        par = (a * nh) % slots if nh % slots else 0
        for h in range(nh):
            cs = (par + h) % slots
            cur = (a, h, cs)
            ns = (par + h + 1) % slots
            if h + 1 < nh:
                stage(cur, (a, h + 1, ns), False)
            else:
                stage(cur, None if last else (a + 1, 0, ns), True)
        finish(a)
    stage(None, (0, 0, 0), False)
    def step(a, _):
        q_block(a, False)
        return 0
    lax.fori_loop(0, nblk - 1, step, 0)
    q_block(nblk - 1, True)

def attn_fwd(x):
    nf, nr, fl, pt, width = x.shape
    lw = width // 3
    nh = lw // HD
    seq = nf * nr * fl * pt
    blk = 2 * nr * pt
    return pl.pallas_call(
        fwd_kernel,
        out_shape=(jax.ShapeDtypeStruct((nf, nr, fl, pt, lw), jnp.bfloat16),
                   jax.ShapeDtypeStruct((lw, seq), jnp.float32),
                   jax.ShapeDtypeStruct((nh, seq), jnp.float32)),
        scratch_shapes=[pltpu.VMEM((nh, seq, lw), jnp.bfloat16), pltpu.VMEM((seq, lw), jnp.bfloat16),
                        pltpu.VMEM((lw, seq), jnp.bfloat16), pltpu.VMEM((2, seq, blk), jnp.float32),
                        pltpu.VMEM((lw, blk), jnp.float32), pltpu.VMEM((2, 1, blk), jnp.float32)],
        compiler_params=pltpu.CompilerParams(vmem_limit_bytes=48 << 20),
        cost_estimate=pl.CostEstimate(flops=seq * seq * lw * 2, bytes_accessed=seq * lw * 12, transcendentals=seq * seq * nh // 2),
        name="attn_fwd",
    )(x)

def rotate_back(t, cos, sin, nh):
    out = []
    for h in range(nh):
        a = t[h * HD:h * HD + HD // 2]
        b = t[h * HD + HD // 2:(h + 1) * HD]
        out += [a * cos + b * sin, b * cos - a * sin]
    return jnp.concatenate(out, axis=0)

def bwd_kernel(x_ref, go_ref, ot_ref, lse_ref, cos_ref, sin_ref, g_ref, qm, dom, kf, vf, kt, delta, dqt, dka, dva):
    nf, nr, fl, pt, width = x_ref.shape
    lw = width // 3
    nh = lw // HD
    tok = nr * pt
    frames = nf * fl
    blk = 2 * tok
    def load(f, _):
        part = x_ref[f // fl, :, f % fl].reshape(tok, width)
        go = go_ref[f // fl, :, f % fl].reshape(tok, lw)
        rows = pl.ds(pl.multiple_of(f * tok, tok), tok)
        q = part[:, :lw] * jnp.bfloat16(HD ** -0.5)
        k = part[:, lw:2 * lw]
        prod = go.T.astype(jnp.float32) * ot_ref[:, rows]
        for h in range(nh):
            qm[h, rows, :] = head_mask(q, h, nh)
            dom[h, rows, :] = head_mask(go, h, nh)
            delta[h:h + 1, rows] = jnp.sum(prod[h * HD:(h + 1) * HD], axis=0, keepdims=True)
        kf[rows, :] = k
        kt[:, rows] = k.T
        vf[rows, :] = part[:, 2 * lw:]
        dqt[:, rows] = jnp.zeros((lw, tok), jnp.float32)
        return 0
    lax.fori_loop(0, frames, load, 0)

    def work(k0, kn, q0, qn):
        rows, cols = pl.ds(k0, kn), pl.ds(q0, qn)
        dv, dk = [], []
        for h in range(nh):
            hs = slice(h * HD, (h + 1) * HD)
            qh, dh = qm[h, cols, :], dom[h, cols, :]
            p = jnp.exp(dot(kf[rows, :], qh, NT) - lse_ref[h:h + 1, cols])
            ds = (p * (dot(vf[rows, :], dh, NT) - delta[h:h + 1, cols])).astype(jnp.bfloat16)
            dv.append(dot(p.astype(jnp.bfloat16), dh, NN))
            dk.append(dot(ds, qh, NN))
            dqt[hs, cols] += dot(kt[hs, rows], ds, NN)
        return sum(dk[1:], dk[0]), sum(dv[1:], dv[0])

    def k_block(b, _):
        k0 = pl.multiple_of(b * blk, blk)
        k1 = pl.multiple_of(b * blk + tok, tok)
        dk, dv = work(k0, tok, k0, blk)
        dka[:tok, :] = dk
        dva[:tok, :] = dv
        dk, dv = work(k1, tok, k1, tok)
        dka[tok:, :] = dk
        dva[tok:, :] = dv
        def q_block(a, _):
            dk, dv = work(k0, blk, pl.multiple_of(a * blk, blk), blk)
            dka[...] += dk
            dva[...] += dv
            return 0
        lax.fori_loop(b + 1, frames // 2, q_block, 0)
        cols = pl.ds(k0, blk)
        dk = rotate_back(dka[...].T, cos_ref[:, cols], sin_ref[:, cols], nh).T.astype(jnp.bfloat16)
        dv = dva[...].astype(jnp.bfloat16)
        for j in range(2):
            f = 2 * b + j
            g_ref[f // fl, :, f % fl, :, lw:2 * lw] = dk[j * tok:(j + 1) * tok].reshape(nr, pt, lw)
            g_ref[f // fl, :, f % fl, :, 2 * lw:] = dv[j * tok:(j + 1) * tok].reshape(nr, pt, lw)
        return 0
    lax.fori_loop(0, frames // 2, k_block, 0)
    def store(f, _):
        cols = pl.ds(pl.multiple_of(f * tok, tok), tok)
        dq = rotate_back(dqt[:, cols] * HD ** -0.5, cos_ref[:, cols], sin_ref[:, cols], nh).T.astype(jnp.bfloat16)
        g_ref[f // fl, :, f % fl, :, :lw] = dq.reshape(nr, pt, lw)
        return 0
    lax.fori_loop(0, frames, store, 0)

def attn_bwd(x, go, ot, lse, cos, sin):
    nf, nr, fl, pt, width = x.shape
    lw = width // 3
    nh = lw // HD
    seq = nf * nr * fl * pt
    blk = 2 * nr * pt
    b16, f32 = jnp.bfloat16, jnp.float32
    return pl.pallas_call(
        bwd_kernel,
        out_shape=jax.ShapeDtypeStruct(x.shape, b16),
        scratch_shapes=[pltpu.VMEM((nh, seq, lw), b16), pltpu.VMEM((nh, seq, lw), b16), pltpu.VMEM((seq, lw), b16),
                        pltpu.VMEM((seq, lw), b16), pltpu.VMEM((lw, seq), b16), pltpu.VMEM((nh, seq), f32),
                        pltpu.VMEM((lw, seq), f32), pltpu.VMEM((blk, lw), f32), pltpu.VMEM((blk, lw), f32)],
        compiler_params=pltpu.CompilerParams(vmem_limit_bytes=52 << 20),
        cost_estimate=pl.CostEstimate(flops=seq * seq * lw * 5, bytes_accessed=seq * lw * 24, transcendentals=seq * seq * nh // 2),
        name="attn_bwd",
    )(x, go, ot, lse, cos, sin)

ALL = ("clip", "frame", "row")
B16, F32 = jnp.bfloat16, jnp.float32


def rope_angles(frame_pos, patch_pos, grid):
    pair_index = jnp.arange(32)
    is_time = pair_index < 8
    is_height = (pair_index >= 8) & (pair_index < 20)
    exponent = jnp.where(
        is_time,
        pair_index / 8.0,
        jnp.where(is_height, (pair_index - 8) / 12.0, (pair_index - 20) / 12.0),
    ).astype(F32)
    frequency = jnp.power(F32(10000.0), -exponent)
    position = jnp.where(
        is_time[None, :],
        frame_pos[:, None],
        jnp.where(is_height[None, :], (patch_pos // grid)[:, None], (patch_pos % grid)[:, None]),
    ).astype(F32)
    angle = position * frequency[None, :]
    return (jnp.cos(angle), jnp.sin(angle))


def rotate(values_in, cosine, sine):
    half = values_in.shape[-1] // 2
    cos_b, sin_b = cosine[:, None, :], sine[:, None, :]
    a, b = values_in[..., :half], values_in[..., half:]
    return jnp.concatenate([a * cos_b - b * sin_b, a * sin_b + b * cos_b], axis=-1)


def normalize(values_in):
    centre = values_in - jnp.mean(values_in, axis=-1, keepdims=True)
    inverse = lax.rsqrt(jnp.mean(centre * centre, axis=-1, keepdims=True) + 1e-06)
    return (centre * inverse, inverse)


def norm_back(grad_in, normed, inverse):
    first_mean = jnp.mean(grad_in, axis=-1, keepdims=True)
    second_mean = jnp.mean(grad_in * normed, axis=-1, keepdims=True)
    return inverse * (grad_in - first_mean - normed * second_mean)


def swap(block, axis, bit):
    size = lax.axis_size(axis)
    return lax.ppermute(block, axis, [(i, i ^ bit) for i in range(size)])


def half_step(array, dim, axis, bit):
    mine = (lax.axis_index(axis) // bit) % 2
    send = lax.dynamic_index_in_dim(array, 1 - mine, dim, keepdims=False)
    keep = lax.dynamic_index_in_dim(array, mine, dim, keepdims=False)
    got = swap(send, axis, bit)
    return (keep.astype(F32) + got.astype(F32)).astype(array.dtype)


def bits_of(size):
    out, bit = [], 1
    while bit < size:
        out.append(bit)
        bit *= 2
    return out


def scatter_sum(grad):
    rows, cols = grad.shape
    nc, nf, nr = (lax.axis_size(a) for a in ALL)
    sizes = {"clip": nc, "frame": nf, "row": nr // 2}
    array = half_step(grad.reshape(rows, 2, cols // 2), 1, "row", 1)
    left = rows
    shape = [nc, nf, nr // 2]
    array = array.reshape(shape + [rows // (nc * nf * (nr // 2)), cols // 2])
    for position, axis in ((0, "clip"), (2, "row"), (1, "frame")):
        base = 2 if axis == "row" else 1
        for bit in bits_of(sizes[axis]):
            now = list(array.shape)
            rest = now[position] // 2
            view = array.reshape(now[:position] + [rest, 2] + now[position + 1:])
            array = half_step(view, position + 1, axis, bit * base)
            array = array.reshape(now[:position] + [rest] + now[position + 1:])
    per = array.shape[3]
    array = array.reshape(2, per // 2, cols // 2)
    mine = lax.axis_index("row") % 2
    keep = lax.dynamic_index_in_dim(array, mine, 0, keepdims=False)
    got = swap(lax.dynamic_index_in_dim(array, 1 - mine, 0, keepdims=False), "row", 1)
    return jnp.where(mine == 0, jnp.concatenate([keep, got], axis=1), jnp.concatenate([got, keep], axis=1)).astype(F32)


def on_device(tokens, context, noise_mod, clean_mod, w_qkv, b_qkv, w_out, b_out, w_up, b_up, w_down, b_down, cotangent):
    frames, patches, clips, width = tokens.shape
    count = frames * patches
    heads = width // HD
    nf, nr = lax.axis_size("frame"), lax.axis_size("row")
    group = nf * nr
    nh = max(1, heads // group)
    lw = nh * HD
    hg = heads // nh
    cs = group // hg
    calls = clips // cs
    grid = round((patches * nr) ** 0.5)
    fi, ri = lax.axis_index("frame"), lax.axis_index("row")

    is_clean = (fi * frames + jnp.arange(frames))[None, :] < context[:, None]
    mods = jnp.where(is_clean[:, :, None, None], clean_mod[None, None], noise_mod.transpose(1, 0, 2, 3))
    mods = mods[:, :, :, None]
    shift1, scale1, gate1, shift2, scale2, gate2 = (mods[:, :, i] for i in range(6))
    full = (clips, frames, patches, width)
    inputs = tokens.transpose(2, 0, 1, 3).astype(F32)
    normed1, inv1 = normalize(inputs)
    h1 = (normed1 * (1.0 + scale1) + shift1).astype(B16).reshape(clips, count, width)

    tok = jnp.arange(count)
    cos, sin = rope_angles(fi * frames + tok // patches, ri * patches + tok % patches, grid)
    every = jnp.arange(nf * frames * nr * patches)
    cos_all, sin_all = rope_angles(every // (nr * patches), every % (nr * patches), grid)
    cos_t, sin_t = cos_all.T, sin_all.T

    def exchange(blocks):
        return lax.all_to_all(blocks, ("frame", "row"), 0, 0, tiled=True)

    def to_heads(parts):
        m = parts[0].shape[1]
        return jnp.concatenate(
            [p.reshape(count, m, hg, lw).transpose(2, 0, 1, 3).reshape(hg, count, m * lw) for p in parts], axis=0)

    def from_heads(blocks, m):
        v = blocks.reshape(cs, hg, count, m, lw).transpose(0, 2, 3, 1, 4).reshape(cs, count, m, width)
        return [v[i] for i in range(cs)]

    lead = (nf, nr, frames, patches)
    saved = []
    attn = []
    for i in range(calls):
        parts = []
        for c in range(i * cs, (i + 1) * cs):
            proj = jnp.dot(h1[c], w_qkv, preferred_element_type=F32) + b_qkv
            four = proj.reshape(count, 3 * heads, HD)
            q = rotate(four[:, :heads], cos, sin)
            k = rotate(four[:, heads:2 * heads], cos, sin)
            parts.append(jnp.concatenate([q, k, four[:, 2 * heads:]], axis=1).astype(B16).reshape(count, 3, width))
        x = exchange(to_heads(parts)).reshape(lead + (3 * lw,))
        o, ot, lse = attn_fwd(x)
        saved.append((x, ot, lse))
        attn += from_heads(exchange(o.reshape(group, count, lw)), 1)
    attn = jnp.concatenate(attn, axis=0).reshape(clips * count, width)

    branch = (jnp.dot(attn, w_out, preferred_element_type=F32) + b_out).reshape(full)
    mixed = inputs + gate1 * branch
    normed2, inv2 = normalize(mixed)
    h2 = (normed2 * (1.0 + scale2) + shift2).astype(B16).reshape(clips * count, width)
    pre = jnp.dot(h2, w_up, preferred_element_type=F32) + b_up
    act = jax.nn.gelu(pre, approximate=True).astype(B16)
    down = (jnp.dot(act, w_down, preferred_element_type=F32) + b_down).reshape(full)
    result = mixed + gate2 * down
    g = cotangent.transpose(2, 0, 1, 3).astype(F32)
    gdown = (g * gate2).astype(B16).reshape(clips * count, width)
    tn = (((0,), (0,)), ((), ()))
    dw_down = dot(act, gdown, tn).astype(B16)
    db_down = jnp.sum(gdown, axis=0, dtype=F32)
    gact = dot(gdown, w_down, NT)
    _, pull = jax.vjp(functools.partial(jax.nn.gelu, approximate=True), pre)
    gpre = pull(gact)[0].astype(B16)
    dw_up = dot(h2, gpre, tn).astype(B16)
    db_up = jnp.sum(gpre, axis=0, dtype=F32)
    gh2 = dot(gpre, w_up, NT).reshape(full)
    gmixed = g + norm_back(gh2 * (1.0 + scale2), normed2, inv2)
    gbranch = (gmixed * gate1).astype(B16).reshape(clips * count, width)
    dw_out = dot(attn, gbranch, tn).astype(B16)
    db_out = jnp.sum(gbranch, axis=0, dtype=F32)
    gattn = dot(gbranch, w_out, NT).astype(B16).reshape(clips, count, 1, width)

    gw_down, gw_up, gw_out = scatter_sum(dw_down), scatter_sum(dw_up), scatter_sum(dw_out)

    grads = []
    for i in range(calls):
        go = exchange(to_heads([gattn[c] for c in range(i * cs, (i + 1) * cs)])).reshape(lead + (lw,))
        x, ot, lse = saved[i]
        gx = attn_bwd(x, go, ot, lse, cos_t, sin_t)
        grads += from_heads(exchange(gx.reshape(group, count, 3 * lw)), 3)
    gproj = jnp.concatenate(grads, axis=0).reshape(clips * count, 3 * width)
    dw_qkv = dot(h1.reshape(clips * count, width), gproj, tn).astype(B16)
    db_qkv = jnp.sum(gproj, axis=0, dtype=F32)
    gh1 = dot(gproj, w_qkv, NT).reshape(full)
    gtokens = gmixed + norm_back(gh1 * (1.0 + scale1), normed1, inv1)
    gw_qkv = scatter_sum(dw_qkv)

    terms = [gh1, gh1 * normed1, gmixed * branch.reshape(full), gh2, gh2 * normed2, g * down]
    gmods = jnp.stack([jnp.sum(t, axis=2) for t in terms], axis=2)
    clean = is_clean[:, :, None, None]
    noise_part = jnp.where(clean, 0.0, gmods).transpose(1, 0, 2, 3).astype(B16)
    quarter = width // nr
    sent = noise_part.reshape(frames, clips, 6, nr, quarter).transpose(3, 0, 1, 2, 4)
    grad_noise = jnp.sum(lax.all_to_all(sent, "row", 0, 0, tiled=True).astype(F32), axis=0)
    clean_part = jnp.sum(jnp.where(clean, gmods, 0.0), axis=(0, 1))
    total = lax.axis_size(ALL)
    small = jnp.concatenate([v.reshape(total, -1) for v in (db_qkv, db_out, db_up, db_down)]
                            + [clean_part.reshape(6, total, -1).transpose(1, 0, 2).reshape(total, -1)], axis=1)
    small = jnp.sum(lax.all_to_all(small, ALL, 0, 0, tiled=True), axis=0)
    ends = []
    at = 0
    for size in (3 * width, width, 4 * width, width):
        ends.append(small[at:at + size // total])
        at += size // total
    gb_qkv, gb_out, gb_up, gb_down = ends
    grad_clean = small[at:].reshape(6, -1)
    back = lambda v: v.reshape(full).transpose(1, 2, 0, 3)
    return (back(result).astype(B16), back(gtokens), grad_noise, grad_clean, gw_qkv, gb_qkv, gw_out, gb_out, gw_up, gb_up, gw_down, gb_down)


def solution(mesh):
    token = P("frame", "row", "clip", None)
    rows = P(ALL, None)
    return jax.shard_map(
        on_device,
        mesh=mesh,
        in_specs=(token, P("clip"), P("frame", "clip", None, None)) + (P(),) * 9 + (token,),
        out_specs=(token, token, P("frame", "clip", None, "row"), P(None, ALL), rows, P(ALL), rows, P(ALL), rows, P(ALL), rows, P(ALL)),
        check_vma=False,
    )
```

```python
import functools
import jax, jax.numpy as jnp
from jax import lax
from jax.experimental import pallas as pl
from jax.experimental.pallas import tpu as pltpu
from jax.sharding import PartitionSpec as P
HD = 64
NN = (((1,), (0,)), ((), ()))
NT = (((1,), (1,)), ((), ()))
def dot(a, b, dims):
    return lax.dot_general(a, b, dims, preferred_element_type=jnp.float32)

def head_mask(values, head, heads):
    if heads == 1:
        return values
    lane = lax.broadcasted_iota(jnp.int32, values.shape, 1)
    return jnp.where(lane // HD == head, values, jnp.zeros_like(values))


def flash_forward(x_ref, o_ref, ot_ref, lse_ref, qm, kf, vt, sb, acc, mrow, done):
    nf, nr, fl, pt, width = x_ref.shape
    lw = width // 3
    nh = lw // HD
    tok = nr * pt
    frames = nf * fl
    blk = 2 * tok
    nblk = frames // 2
    def load(f, _):
        part = x_ref[f // fl, :, f % fl].reshape(tok, width)
        rows = pl.ds(pl.multiple_of(f * tok, tok), tok)
        q = part[:, :lw] * jnp.bfloat16(HD ** -0.5)
        for h in range(nh):
            qm[h, rows, :] = head_mask(q, h, nh)
        kf[rows, :] = part[:, lw:2 * lw]
        vt[:, rows] = part[:, 2 * lw:].T
        return 0
    lax.fori_loop(0, frames, load, 0)

    def fold(v, op):
        return op(v.reshape(v.shape[0] // 8, 8, v.shape[1]), axis=0)

    def stage(cur, nxt, grow):
        zero8 = jnp.zeros((8, blk), jnp.float32)
        if nxt is not None:
            na, nhd, ns = nxt
            n0 = pl.multiple_of(na * blk, blk)
            n1 = pl.multiple_of(na * blk + tok, tok)
            ncols = pl.ds(n0, blk)
            s0 = dot(kf[pl.ds(n0, tok), :], qm[nhd, ncols, :], NT)
            s1 = dot(kf[pl.ds(n1, tok), :], qm[nhd, pl.ds(n1, tok), :], NT)
            sb[ns, pl.ds(n0, tok), :] = s0
            sb[ns, pl.ds(n1, tok), tok:] = s1
            m0 = fold(s0, jnp.max)
            mm = jnp.concatenate([m0[:, :tok], jnp.maximum(m0[:, tok:], fold(s1, jnp.max))], axis=1)
        else:
            mm = zero8
        if cur is not None:
            ca, chd, cs = cur
            hs = slice(chd * HD, (chd + 1) * HD)
            c0 = pl.multiple_of(ca * blk, blk)
            c1 = pl.multiple_of(ca * blk + tok, tok)
            m = mrow[cs]
            p0 = jnp.exp(sb[cs, pl.ds(c0, tok), :] - m)
            p1 = jnp.exp(sb[cs, pl.ds(c1, tok), tok:] - m[:, tok:])
            l0 = fold(p0, jnp.sum)
            ll = jnp.concatenate([l0[:, :tok], l0[:, tok:] + fold(p1, jnp.sum)], axis=1)
            a0 = dot(vt[hs, pl.ds(c0, tok)], p0.astype(jnp.bfloat16), NN)
            a1 = dot(vt[hs, pl.ds(c1, tok)], p1.astype(jnp.bfloat16), NN)
            acc[hs, :tok] = a0[:, :tok]
            acc[hs, tok:] = a0[:, tok:] + a1
        else:
            ll = zero8
        def score(b, mm):
            rows = pl.ds(pl.multiple_of(b * blk, blk), blk)
            s = dot(kf[rows, :], qm[nhd, ncols, :], NT)
            sb[ns, rows, :] = s
            return jnp.maximum(mm, fold(s, jnp.max))
        def body(b, carry):
            mm, ll = carry
            if nxt is not None:
                mm = score(b, mm)
            if cur is not None:
                rows = pl.ds(pl.multiple_of(b * blk, blk), blk)
                p = jnp.exp(sb[cs, rows, :] - m)
                ll = ll + fold(p, jnp.sum)
                acc[hs, :] += dot(vt[hs, rows], p.astype(jnp.bfloat16), NN)
            return mm, ll
        trip = nxt[0] if cur is None else cur[0]
        mm, ll = lax.fori_loop(0, trip, body, (mm, ll))
        if grow and nxt is not None:
            mm = score(cur[0], mm)
        if nxt is not None:
            mrow[ns] = jnp.max(mm, axis=0, keepdims=True)
        if cur is not None:
            l = jnp.sum(ll, axis=0, keepdims=True)
            ot = acc[hs, :] / l
            acc[hs, :] = ot
            cols = pl.ds(c0, blk)
            ot_ref[hs, cols] = ot
            lse_ref[chd:chd + 1, cols] = m + jnp.log(l)

    def finish(a):
        o = acc[...].T.astype(jnp.bfloat16)
        for j in range(2):
            f = 2 * a + j
            o_ref[f // fl, :, f % fl] = o[j * tok:(j + 1) * tok].reshape(nr, pt, lw)
        done(a)

    slots = sb.shape[0]
    def q_block(a, last):
        par = (a * nh) % slots if nh % slots else 0
        for h in range(nh):
            cs = (par + h) % slots
            cur = (a, h, cs)
            ns = (par + h + 1) % slots
            if h + 1 < nh:
                stage(cur, (a, h + 1, ns), False)
            else:
                stage(cur, None if last else (a + 1, 0, ns), True)
        finish(a)
    stage(None, (0, 0, 0), False)
    def step(a, _):
        q_block(a, False)
        return 0
    lax.fori_loop(0, nblk - 1, step, 0)
    q_block(nblk - 1, True)


def rotate_back(t, cos, sin, nh):
    out = []
    for h in range(nh):
        a = t[h * HD:h * HD + HD // 2]
        b = t[h * HD + HD // 2:(h + 1) * HD]
        out += [a * cos + b * sin, b * cos - a * sin]
    return jnp.concatenate(out, axis=0)

def flash_backward(x_ref, go_ref, ot_ref, lse_ref, cos_ref, sin_ref, g_ref, qm, dom, kf, vf, kt, delta, dqt, dka, dva, done):
    nf, nr, fl, pt, width = x_ref.shape
    lw = width // 3
    nh = lw // HD
    tok = nr * pt
    frames = nf * fl
    blk = 2 * tok
    def load(f, _):
        part = x_ref[f // fl, :, f % fl].reshape(tok, width)
        go = go_ref[f // fl, :, f % fl].reshape(tok, lw)
        rows = pl.ds(pl.multiple_of(f * tok, tok), tok)
        q = part[:, :lw] * jnp.bfloat16(HD ** -0.5)
        k = part[:, lw:2 * lw]
        prod = go.T.astype(jnp.float32) * ot_ref[:, rows]
        for h in range(nh):
            qm[h, rows, :] = head_mask(q, h, nh)
            dom[h, rows, :] = head_mask(go, h, nh)
            delta[h:h + 1, rows] = jnp.sum(prod[h * HD:(h + 1) * HD], axis=0, keepdims=True)
        kf[rows, :] = k
        kt[:, rows] = k.T
        vf[rows, :] = part[:, 2 * lw:]
        dqt[:, rows] = jnp.zeros((lw, tok), jnp.float32)
        return 0
    lax.fori_loop(0, frames, load, 0)

    def work(k0, kn, q0, qn):
        rows, cols = pl.ds(k0, kn), pl.ds(q0, qn)
        dv, dk = [], []
        for h in range(nh):
            hs = slice(h * HD, (h + 1) * HD)
            qh, dh = qm[h, cols, :], dom[h, cols, :]
            p = jnp.exp(dot(kf[rows, :], qh, NT) - lse_ref[h:h + 1, cols])
            ds = (p * (dot(vf[rows, :], dh, NT) - delta[h:h + 1, cols])).astype(jnp.bfloat16)
            dv.append(dot(p.astype(jnp.bfloat16), dh, NN))
            dk.append(dot(ds, qh, NN))
            dqt[hs, cols] += dot(kt[hs, rows], ds, NN)
        return sum(dk[1:], dk[0]), sum(dv[1:], dv[0])

    def k_block(b, _):
        k0 = pl.multiple_of(b * blk, blk)
        k1 = pl.multiple_of(b * blk + tok, tok)
        dk, dv = work(k0, tok, k0, blk)
        dka[:tok, :] = dk
        dva[:tok, :] = dv
        dk, dv = work(k1, tok, k1, tok)
        dka[tok:, :] = dk
        dva[tok:, :] = dv
        def q_block(a, _):
            dk, dv = work(k0, blk, pl.multiple_of(a * blk, blk), blk)
            dka[...] += dk
            dva[...] += dv
            return 0
        lax.fori_loop(b + 1, frames // 2, q_block, 0)
        cols = pl.ds(k0, blk)
        dk = rotate_back(dka[...].T, cos_ref[:, cols], sin_ref[:, cols], nh).T.astype(jnp.bfloat16)
        dv = dva[...].astype(jnp.bfloat16)
        dq = rotate_back(dqt[:, cols] * HD ** -0.5, cos_ref[:, cols], sin_ref[:, cols], nh).T.astype(jnp.bfloat16)
        for j in range(2):
            f = 2 * b + j
            for n, part in enumerate((dq, dk, dv)):
                g_ref[f // fl, :, f % fl, :, n * lw:(n + 1) * lw] = part[j * tok:(j + 1) * tok].reshape(nr, pt, lw)
        done(b)
        return 0
    lax.fori_loop(0, frames // 2, k_block, 0)


ALL = ("clip", "frame", "row")
B16, F32 = jnp.bfloat16, jnp.float32


def rope_angles(frame_pos, patch_pos, grid):
    pair_index = jnp.arange(32)
    is_time = pair_index < 8
    is_height = (pair_index >= 8) & (pair_index < 20)
    exponent = jnp.where(
        is_time,
        pair_index / 8.0,
        jnp.where(is_height, (pair_index - 8) / 12.0, (pair_index - 20) / 12.0),
    ).astype(F32)
    frequency = jnp.power(F32(10000.0), -exponent)
    position = jnp.where(
        is_time[None, :],
        frame_pos[:, None],
        jnp.where(is_height[None, :], (patch_pos // grid)[:, None], (patch_pos % grid)[:, None]),
    ).astype(F32)
    angle = position * frequency[None, :]
    return (jnp.cos(angle), jnp.sin(angle))


def rotate_lanes(t, cos, sin):
    lane = lax.broadcasted_iota(jnp.int32, t.shape, 1)
    half = HD // 2
    lanes = t.shape[1]
    low = (lane % HD) < half
    part = jnp.where(low, pltpu.roll(t, lanes - half, 1), pltpu.roll(t, half, 1))
    return t * cos + part * sin


def stats(v):
    mean = jnp.mean(v, axis=1, keepdims=True)
    centre = v - mean
    inverse = lax.rsqrt(jnp.mean(centre * centre, axis=1, keepdims=True) + 1e-06)
    return centre * inverse, inverse


def qkv_kernel(x_ref, mod_ref, w_hbm, b_ref, cos_ref, sin_ref, o_ref, h_ref, w, sem):
    count, width = x_ref.shape
    hg, _, w3 = o_ref.shape
    lw = w3 // 3
    frames = mod_ref.shape[0]
    pt = count // frames
    copies = [pltpu.make_async_copy(w_hbm.at[:, pl.ds(j * width, width)], w.at[j], sem.at[j]) for j in range(3)]
    for c in copies:
        c.start()
    def one(f, _):
        rows = pl.ds(pl.multiple_of(f * pt, pt), pt)
        n, _inv = stats(x_ref[rows, :].astype(F32))
        h_ref[rows, :] = (n * (1.0 + mod_ref[f, 1:2, :]) + mod_ref[f, 0:1, :]).astype(B16)
        return 0
    lax.fori_loop(0, frames, one, 0)
    step = max(256, lw)
    for j in range(3):
        copies[j].wait()
        for a in range(0, width, step):
            t = dot(h_ref[...], w[j, :, a:a + step], NN) + b_ref[0:1, j * width + a:j * width + a + step]
            for g in range(step // lw):
                v = t[:, g * lw:(g + 1) * lw]
                if j < 2:
                    v = rotate_lanes(v, cos_ref[...], sin_ref[...])
                o_ref[a // lw + g, :, j * lw:(j + 1) * lw] = v.astype(B16)


def qkv_forward(x, mods, w, b, cos, sin, hg, lw):
    count, width = x.shape
    return pl.pallas_call(
        qkv_kernel,
        out_shape=(jax.ShapeDtypeStruct((hg, count, 3 * lw), B16), jax.ShapeDtypeStruct((count, width), B16)),
        in_specs=[pl.BlockSpec(memory_space=pltpu.VMEM)] * 2 + [pl.BlockSpec(memory_space=pl.ANY)]
        + [pl.BlockSpec(memory_space=pltpu.VMEM)] * 3,
        scratch_shapes=[pltpu.VMEM((3, width, width), B16), pltpu.SemaphoreType.DMA((3,))],
        compiler_params=pltpu.CompilerParams(vmem_limit_bytes=48 << 20),
        cost_estimate=pl.CostEstimate(flops=6 * count * width * width, bytes_accessed=10 * count * width + 6 * width * width, transcendentals=0),
        name="qkv",
    )(x, mods, w, b, cos, sin)


def mlp_kernel(a_ref, x_ref, g_ref, mod_ref, wo_ref, bo_ref, wu_ref, bu_ref, wd_ref, bd_ref,
               y_ref, gm_ref, ga_ref, gb_ref, an_ref, h_ref, gd_ref, act_ref, gp_ref, sums_ref, du_ref, db_ref,
               branch, mixed, n2, inv2, down, gh):
    hg, count, lw = a_ref.shape
    width = x_ref.shape[1]
    frames = mod_ref.shape[0]
    pt = count // frames
    step = pl.program_id(0)

    def each(fn):
        def one(f, _):
            fn(f, pl.ds(pl.multiple_of(f * pt, pt), pt))
            return 0
        lax.fori_loop(0, frames, one, 0)

    @pl.when(step == 0)
    def _():
        for g in range(hg):
            an_ref[:, g * lw:(g + 1) * lw] = a_ref[g]
        branch[...] = dot(an_ref[...], wo_ref[...], NN) + bo_ref[...]
        def fn(f, rows):
            m = x_ref[rows, :].astype(F32) + mod_ref[f, 2:3, :] * branch[rows, :]
            n, inv = stats(m)
            mixed[rows, :] = m
            n2[rows, :] = n
            inv2[rows, :] = jnp.broadcast_to(inv, (pt, 128))
            h_ref[rows, :] = (n * (1.0 + mod_ref[f, 4:5, :]) + mod_ref[f, 3:4, :]).astype(B16)
            gd_ref[rows, :] = (g_ref[rows, :].astype(F32) * mod_ref[f, 5:6, :]).astype(B16)
        each(fn)
        down[...] = jnp.zeros_like(down)
        gh[...] = jnp.zeros_like(gh)

    c0 = (2.0 / 3.141592653589793) ** 0.5
    c1 = 0.044715
    h, gd = h_ref[...], gd_ref[...]
    wu, wd = wu_ref[...], wd_ref[...]
    pre = dot(h, wu, NN) + bu_ref[...]
    gact = dot(gd, wd, NT)
    sq = pre * pre
    u = jnp.tanh(pre * (c0 + (c0 * c1) * sq))
    half = 0.5 * (1.0 + u)
    act = (pre * half).astype(B16)
    slope = half + (0.5 * pre) * (1.0 - u * u) * (c0 + (3.0 * c0 * c1) * sq)
    gp = (gact * slope).astype(B16)
    act_ref[...] = act
    gp_ref[...] = gp
    du_ref[...] = jnp.sum(gp.astype(F32), axis=0, keepdims=True)
    down[...] += dot(act, wd, NN)
    gh[...] += dot(gp, wu, NT)

    @pl.when(step == pl.num_programs(0) - 1)
    def _():
        db_ref[...] = jnp.zeros_like(db_ref)
        def fn(f, rows):
            g = g_ref[rows, :].astype(F32)
            d = down[rows, :] + bd_ref[...]
            y_ref[rows, :] = (mixed[rows, :] + mod_ref[f, 5:6, :] * d).astype(B16)
            ghf = gh[rows, :]
            n = n2[rows, :]
            t = ghf * (1.0 + mod_ref[f, 4:5, :])
            back = t - jnp.mean(t, axis=1, keepdims=True) - n * jnp.mean(t * n, axis=1, keepdims=True)
            gm = g + inv2[rows, 0:1] * back
            gm_ref[rows, :] = gm
            gbr = (gm * mod_ref[f, 2:3, :]).astype(B16)
            gb_ref[rows, :] = gbr
            s = lambda v: jnp.sum(v, axis=0, keepdims=True)
            sums_ref[f] = jnp.concatenate([s(gm * branch[rows, :]), s(ghf), s(ghf * n), s(g * d)], axis=0)
            db_ref[...] += jnp.concatenate([s(gbr.astype(F32)), s(gd_ref[rows, :].astype(F32))], axis=0)
        each(fn)
        ga = dot(gb_ref[...], wo_ref[...], NT).astype(B16)
        for i in range(hg):
            ga_ref[i] = ga[:, i * lw:(i + 1) * lw]


def mlp(c, attn, x, g, mods, w_out, b_out, w_up, b_up, w_down, b_down):
    _, hg, count, lw = attn.shape
    width = x.shape[1]
    ff = w_up.shape[1]
    frames = mods.shape[0]
    fc = min(512, ff)
    whole = lambda *shape: pl.BlockSpec(shape, lambda j: (0,) * len(shape), pipeline_mode=pl.Buffered(1))
    keep = lambda *shape: pl.BlockSpec(shape, lambda j: (0,) * len(shape))
    cols = lambda m: pl.BlockSpec((m, fc), lambda j: (0, j))
    s = jax.ShapeDtypeStruct
    return pl.pallas_call(
        mlp_kernel,
        grid=(ff // fc,),
        in_specs=[pl.BlockSpec((None, hg, count, lw), lambda j: (c, 0, 0, 0), pipeline_mode=pl.Buffered(1)), whole(count, width), whole(count, width), whole(frames, 6, width),
                  whole(width, width), whole(1, width), cols(width), cols(1),
                  pl.BlockSpec((fc, width), lambda j: (j, 0)), whole(1, width)],
        out_specs=(keep(count, width), keep(count, width), keep(hg, count, lw), keep(count, width), keep(count, width),
                   keep(count, width), keep(count, width), cols(count), cols(count), keep(frames, 4, width), cols(1), keep(2, width)),
        out_shape=(s((count, width), B16), s((count, width), F32), s((hg, count, lw), B16), s((count, width), B16),
                   s((count, width), B16), s((count, width), B16), s((count, width), B16), s((count, ff), B16),
                   s((count, ff), B16), s((frames, 4, width), F32), s((1, ff), F32), s((2, width), F32)),
        scratch_shapes=[pltpu.VMEM((count, width), F32)] * 3 + [pltpu.VMEM((count, 128), F32)]
        + [pltpu.VMEM((count, width), F32)] * 2,
        compiler_params=pltpu.CompilerParams(vmem_limit_bytes=60 << 20, dimension_semantics=("arbitrary",)),
        cost_estimate=pl.CostEstimate(flops=2 * count * width * (2 * width + 4 * ff), bytes_accessed=4 * width * ff + 40 * count * width, transcendentals=count * ff),
        name="mlp",
    )(attn, x, g, mods, w_out, b_out, w_up, b_up, w_down, b_down)


def qkv_back_kernel(gp_ref, x_ref, gm_ref, mod_ref, w_ref, o_ref, sums_ref, db_ref, full, gh):
    hg, count, w3 = gp_ref.shape
    lw = w3 // 3
    width = x_ref.shape[1]
    frames = mod_ref.shape[0]
    pt = count // frames
    for j in range(3):
        for g in range(hg):
            full[:, j * width + g * lw:j * width + (g + 1) * lw] = gp_ref[g, :, j * lw:(j + 1) * lw]
    gh[...] = dot(full[...], w_ref[...], NT)
    db_ref[...] = jnp.sum(full[...].astype(F32), axis=0, keepdims=True)
    def one(f, _):
        rows = pl.ds(pl.multiple_of(f * pt, pt), pt)
        n, inv = stats(x_ref[rows, :].astype(F32))
        ghf = gh[rows, :]
        t = ghf * (1.0 + mod_ref[f, 1:2, :])
        back = t - jnp.mean(t, axis=1, keepdims=True) - n * jnp.mean(t * n, axis=1, keepdims=True)
        o_ref[rows, :] = gm_ref[rows, :] + inv * back
        s = lambda v: jnp.sum(v, axis=0, keepdims=True)
        sums_ref[f] = jnp.concatenate([s(ghf), s(ghf * n)], axis=0)
        return 0
    lax.fori_loop(0, frames, one, 0)


def qkv_back(c, gproj, x, gmixed, mods, w):
    _, hg, count, w3 = gproj.shape
    width = x.shape[1]
    frames = mods.shape[0]
    s = jax.ShapeDtypeStruct
    whole = lambda *shape: pl.BlockSpec(shape, lambda i: (0,) * len(shape))
    return pl.pallas_call(
        qkv_back_kernel,
        grid=(1,),
        in_specs=[pl.BlockSpec((None, hg, count, w3), lambda i: (c, 0, 0, 0)), whole(count, width), whole(count, width),
                  whole(frames, 6, width), whole(width, 3 * width)],
        out_specs=(whole(count, width), whole(frames, 2, width), whole(1, 3 * width)),
        out_shape=(s((count, width), F32), s((frames, 2, width), F32), s((1, 3 * width), F32)),
        scratch_shapes=[pltpu.VMEM((count, 3 * width), B16), pltpu.VMEM((count, width), F32)],
        compiler_params=pltpu.CompilerParams(vmem_limit_bytes=48 << 20),
        cost_estimate=pl.CostEstimate(flops=6 * count * width * width, bytes_accessed=16 * count * width + 6 * width * width, transcendentals=0),
        name="qkv_back",
    )(gproj, x, gmixed, mods, w)


TN = (((0,), (0,)), ((), ()))


def outer_kernel(half_ref, *refs, clips, packed, received):
    a_refs, b_refs = refs[:clips], refs[clips:2 * clips]
    o_ref = refs[-1]
    total = None
    for a_ref, b_ref in zip(a_refs, b_refs):
        b = jnp.concatenate([b_ref[i] for i in range(packed)], axis=1) if packed else b_ref[...]
        part = dot(a_ref[...], b, TN)
        total = part if total is None else total + part
    if received:
        total = total + refs[2 * clips][...].astype(F32)
    o_ref[...] = total.astype(B16)


def outer(a_list, b_list, half, got=None):
    clips = len(a_list)
    count, rows = a_list[0].shape
    grouped = not isinstance(b_list, (list, tuple))
    if grouped:
        _, groups, _, w3 = b_list.shape
        packed = max(1, 128 * 3 // w3)
        ch = groups // 2 * w3
        cb, rb = packed * w3, rows
        b_specs = [pl.BlockSpec((None, packed, count, w3), lambda i, j, h, c=c: (c, h[0] * (groups // 2 // packed) + j, 0, 0)) for c in range(clips)]
        b_list = [b_list] * clips
    else:
        packed = 0
        ch = b_list[0].shape[1] // 2
        rb = min(rows, 1024)
        cb = min(ch, 512)
        b_specs = [pl.BlockSpec((count, cb), lambda i, j, h: (0, h[0] * (ch // cb) + j))] * clips
    out = pl.BlockSpec((rb, cb), lambda i, j, h: (i, j))
    return pl.pallas_call(
        functools.partial(outer_kernel, clips=clips, packed=packed, received=got is not None),
        grid_spec=pltpu.PrefetchScalarGridSpec(
            num_scalar_prefetch=1, grid=(rows // rb, ch // cb),
            in_specs=[pl.BlockSpec((count, rb), lambda i, j, h: (0, i))] * clips + b_specs + ([out] if got is not None else []),
            out_specs=out),
        out_shape=jax.ShapeDtypeStruct((rows, ch), B16),
        compiler_params=pltpu.CompilerParams(vmem_limit_bytes=40 << 20, dimension_semantics=("arbitrary", "arbitrary")),
        cost_estimate=pl.CostEstimate(flops=2 * clips * count * rows * ch, bytes_accessed=2 * clips * count * (rows + ch) + 2 * rows * ch, transcendentals=0),
        name="outer",
    )(half, *a_list, *b_list, *([got] if got is not None else []))


MESH = pl.DeviceIdType.MESH


class Plane:
    def __init__(self):
        self.nf, self.nr = lax.axis_size("frame"), lax.axis_size("row")
        self.f, self.r = lax.axis_index("frame"), lax.axis_index("row")
        self.size = self.nf * self.nr
        self.me = self.f * self.nr + self.r

    def peer(self, k):
        p = lax.rem(self.me + k, self.size)
        return p, p // self.nr, lax.rem(p, self.nr)


def greet(plane, with_clips):
    barrier = pltpu.get_barrier_semaphore()
    count = plane.size - 1
    for k in range(1, plane.size):
        _, f, r = plane.peer(k)
        pl.semaphore_signal(barrier, inc=1, device_id={"frame": f, "row": r}, device_id_type=MESH)
    if with_clips:
        nc = lax.axis_size("clip")
        c = lax.axis_index("clip")
        for k in range(1, nc):
            pl.semaphore_signal(barrier, inc=1, device_id={"clip": lax.rem(c + k, nc)}, device_id_type=MESH)
        count += nc - 1
    pl.semaphore_wait(barrier, count)


def remote(src, dst, send, recv, device):
    return pltpu.make_async_remote_copy(src_ref=src, dst_ref=dst, send_sem=send, recv_sem=recv, device_id=device, device_id_type=MESH)


def send_blocks(plane, i, a, buf, out, send, recv, local):
    fl = buf.shape[3]
    fh, at = 2 * a // fl, lax.rem(2 * a, fl)
    for r in range(plane.nr):
        src = buf.at[i, fh, r, pl.ds(at, 2)]
        dst = out.at[i, plane.me, pl.ds(at, 2)]
        own = jnp.logical_and(fh == plane.f, r == plane.r)
        dest = fh * plane.nr + r
        k = lax.rem(dest - plane.me + plane.size, plane.size)
        @pl.when(own)
        def _():
            pltpu.make_async_copy(src, dst, local.at[i]).start()
        @pl.when(jnp.logical_not(own))
        def _():
            remote(src, dst, send.at[i, k], recv.at[i, k], {"frame": fh, "row": r}).start()


def wait_blocks(plane, calls, buf, out, send, recv, local):
    for i in range(calls):
        pltpu.make_async_copy(buf.at[i, plane.f, plane.r], out.at[i, plane.me], local.at[i]).wait()
        for k in range(1, plane.size):
            p, f, r = plane.peer(k)
            copy = remote(buf.at[i, f, r], out.at[i, plane.me], send.at[i, k], recv.at[i, k], {"frame": f, "row": r})
            copy.wait_send()
            copy.wait_recv()


def fwd_all_kernel(*refs, calls):
    plane = Plane()
    x_send = refs[:calls]
    x_out, a_out, ot_ref, lse_ref = refs[calls:calls + 4]
    xv, ob, qm, kf, vt, sb, acc, mrow, xs, xr, xl, os, orr, ol, save = refs[calls + 4:]
    greet(plane, False)
    for i in range(calls):
        pltpu.make_async_copy(x_send[i].at[plane.me], xv.at[i, plane.f, plane.r], xl.at[i]).start()
        for k in range(1, plane.size):
            p, f, r = plane.peer(k)
            remote(x_send[i].at[p], xv.at[i, plane.f, plane.r], xs.at[i, k], xr.at[i, k], {"frame": f, "row": r}).start()

    def arrive(i, what):
        for k in range(1, plane.size):
            p, f, r = plane.peer(k)
            copy = remote(x_send[0].at[p], xv.at[i, plane.f, plane.r], xs.at[i, k], xr.at[i, k], {"frame": f, "row": r})
            copy.wait_recv() if what else copy.wait_send()

    def call(i, _):
        pltpu.make_async_copy(x_send[0].at[plane.me], xv.at[i, plane.f, plane.r], xl.at[i]).wait()
        arrive(i, True)
        pltpu.make_async_copy(xv.at[i], x_out.at[i], save.at[i]).start()
        flash_forward(xv.at[i], ob.at[i], ot_ref.at[i], lse_ref.at[i], qm, kf, vt, sb, acc, mrow,
                      lambda a: send_blocks(plane, i, a, ob, a_out, os, orr, ol))
        return 0
    lax.fori_loop(0, calls, call, 0)
    for i in range(calls):
        arrive(i, False)
        pltpu.make_async_copy(xv.at[i], x_out.at[i], save.at[i]).wait()
    wait_blocks(plane, calls, ob, a_out, os, orr, ol)


def attention_forward(sends, lead, lw):
    calls = len(sends)
    nf, nr, fl, pt = lead
    group = nf * nr
    nh = lw // HD
    seq = nf * nr * fl * pt
    blk = 2 * nr * pt
    hbm, vmem = pl.BlockSpec(memory_space=pl.ANY), pl.BlockSpec(memory_space=pltpu.VMEM)
    s, v, dma = jax.ShapeDtypeStruct, pltpu.VMEM, pltpu.SemaphoreType.DMA
    return pl.pallas_call(
        functools.partial(fwd_all_kernel, calls=calls),
        in_specs=[hbm] * calls,
        out_specs=(hbm, hbm, vmem, vmem),
        out_shape=(s((calls,) + lead + (3 * lw,), B16), s((calls, group, fl, pt, lw), B16),
                   s((calls, lw, seq), F32), s((calls, nh, seq), F32)),
        scratch_shapes=[v((calls,) + lead + (3 * lw,), B16), v((calls,) + lead + (lw,), B16), v((nh, seq, lw), B16),
                        v((seq, lw), B16), v((lw, seq), B16), v((2, seq, blk), F32), v((lw, blk), F32), v((2, 1, blk), F32),
                        dma((calls, group)), dma((calls, group)), dma((calls,)), dma((calls, group)), dma((calls, group)),
                        dma((calls,)), dma((calls,))],
        compiler_params=pltpu.CompilerParams(vmem_limit_bytes=56 << 20, collective_id=0, has_side_effects=True),
        cost_estimate=pl.CostEstimate(flops=calls * seq * seq * lw * 2, bytes_accessed=calls * seq * lw * 24, transcendentals=calls * seq * seq * nh // 2),
        name="attention_forward",
    )(*sends)


class Sum:
    def __init__(self, plane, plane_first, part, out, cols, out_cols, v1, s1, v2, s2, v3, sems):
        self.plane, self.plane_first, self.part, self.out = plane, plane_first, part, out
        self.cols, self.out_cols = cols, out_cols
        self.v1, self.s1, self.v2, self.s2, self.v3, self.sems = v1, s1, v2, s2, v3, sems
        self.bit = lax.rem(plane.r, 2)

    def place(self, stage):
        plane = self.plane
        if (stage == 1) == self.plane_first:
            half = plane.nr // 2
            return plane.nf * half, plane.f * half + plane.r // 2, lambda p: {"frame": p // half, "row": lax.rem(p, half) * 2 + self.bit}
        return lax.axis_size("clip"), lax.axis_index("clip"), lambda p: {"clip": p}

    def block(self, stage, p):
        if stage == 2:
            return self.s1.at[p]
        cols = pl.ds(*self.cols)
        return self.part.at[:, p, :, cols] if self.plane_first else self.part.at[p, :, :, cols]

    def copies(self, stage):
        count, me, device = self.place(stage)
        dst = self.v1 if stage == 1 else self.v2
        base = 0 if stage == 1 else self.v1.shape[0]
        out = []
        for k in range(1, count):
            p = lax.rem(me + k, count)
            out.append(remote(self.block(stage, p), dst.at[me], self.sems.at[0, base + k], self.sems.at[1, base + k], device(p)))
        return out, pltpu.make_async_copy(self.block(stage, me), dst.at[me], self.sems.at[0, base])

    def start(self, stage):
        copies, own = self.copies(stage)
        for c in copies:
            c.start()
        own.start()

    def wait(self, stage):
        copies, own = self.copies(stage)
        for c in copies:
            c.wait()
        own.wait()

    def middle(self):
        def one(j, _):
            total = self.v1[0, j].astype(F32)
            for c in range(1, self.v1.shape[0]):
                total = total + self.v1[c, j].astype(F32)
            self.s1[j] = total.astype(B16)
            return 0
        lax.fori_loop(0, self.s1.shape[0], one, 0)
        self.start(2)

    def third(self):
        return remote(self.s2.at[1 - self.bit], self.v3, self.sems.at[0, self.sems.shape[1] - 1], self.sems.at[1, self.sems.shape[1] - 1],
                      {"row": self.plane.r + 1 - 2 * self.bit})

    def columns(self, b):
        first, size = self.cols
        return pl.ds(b * self.out_cols + first, size)

    def last(self):
        total = self.v2[0].astype(F32)
        for c in range(1, self.v2.shape[0]):
            total = total + self.v2[c].astype(F32)
        per = self.s2.shape[1]
        self.s2[0] = total[:per]
        self.s2[1] = total[per:]
        self.third().start()
        for b in range(2):
            @pl.when(self.bit == b)
            def _():
                self.out[:, self.columns(b)] = self.s2[b]

    def close(self):
        self.third().wait()
        for b in range(2):
            @pl.when(self.bit == b)
            def _():
                self.out[:, self.columns(1 - b)] = self.v3[...]


def sum_plan(parts, orders):
    scratch, outs, jobs = [], [], []
    for n, (part, order) in enumerate(zip(parts, orders)):
        nc, np_, two, ch = part.shape
        outs.append(jax.ShapeDtypeStruct((two // 2, 2 * ch), F32))
        for plane_first, first, cols in order:
            n1, n2 = (np_, nc) if plane_first else (nc, np_)
            scratch += [pltpu.VMEM((n1, n2, two, cols), B16), pltpu.VMEM((n2, two, cols), B16), pltpu.VMEM((n2, two, cols), B16),
                        pltpu.VMEM((2, two // 2, cols), F32), pltpu.VMEM((two // 2, cols), F32),
                        pltpu.SemaphoreType.DMA((2, n1 + n2 + 1))]
            jobs.append((n, plane_first, first, cols))
    return scratch, outs, jobs


def make_sums(plane, jobs, parts, outs, scratch):
    return [Sum(plane, plane_first, parts[n], outs[n], (first, cols), parts[n].shape[3], *scratch[6 * i:6 * i + 6])
            for i, (n, plane_first, first, cols) in enumerate(jobs)]


def sums_kernel(*refs, count, jobs):
    plane = Plane()
    sums = make_sums(plane, jobs, refs[:count], refs[count:2 * count], refs[2 * count:])
    greet(plane, True)
    for s in sums:
        s.start(1)
    for s in sums:
        s.wait(1)
        s.middle()
    for s in sums:
        s.wait(2)
        s.last()
    for s in sums:
        s.close()


def scatter_sums(parts, orders, collective_id):
    scratch, outs, jobs = sum_plan(parts, orders)
    return pl.pallas_call(
        functools.partial(sums_kernel, count=len(parts), jobs=jobs),
        in_specs=[pl.BlockSpec(memory_space=pl.ANY)] * len(parts),
        out_specs=[pl.BlockSpec(memory_space=pltpu.VMEM)] * len(parts),
        out_shape=outs,
        scratch_shapes=scratch,
        compiler_params=pltpu.CompilerParams(vmem_limit_bytes=48 << 20, collective_id=collective_id, has_side_effects=True),
        cost_estimate=pl.CostEstimate(flops=0, bytes_accessed=sum(2 * p.size for p in parts) * 40, transcendentals=0),
        name="scatter_sums",
    )(*parts)


def bwd_all_kernel(*refs, calls, count, jobs):
    plane = Plane()
    x_in, go_in, ot_in, lse_ref, cos_ref, sin_ref = refs[:6]
    go_send = refs[6:5 + calls]
    at = 5 + calls
    parts = refs[at:at + count]
    at += count
    gx_out = refs[at]
    outs = refs[at + 1:at + 1 + count]
    at += 1 + count
    xv, gov, otv, gb, qm, dom, kf, vf, kt, delta, dqt, dka, dva, loads, gs, gr, gl, xs, xr, xl = refs[at:at + 20]
    sums = make_sums(plane, jobs, parts, outs, refs[at + 20:])
    greet(plane, True)
    load = [pltpu.make_async_copy(go_in, gov.at[0], gl.at[0])]
    for i in range(calls):
        load += [pltpu.make_async_copy(x_in.at[i], xv.at[i], loads.at[0, i]), pltpu.make_async_copy(ot_in.at[i], otv.at[i], loads.at[1, i])]
    for c in load:
        c.start()
    def go_copy(i, k, src):
        p, f, r = plane.peer(k)
        return remote(src.at[p], gov.at[i, plane.f, plane.r], gs.at[i, k], gr.at[i, k], {"frame": f, "row": r})
    for i in range(1, calls):
        pltpu.make_async_copy(go_send[i - 1].at[plane.me], gov.at[i, plane.f, plane.r], gl.at[i]).start()
        for k in range(1, plane.size):
            go_copy(i, k, go_send[i - 1]).start()
    for s in sums:
        s.start(1)

    def call(i, _):
        pltpu.make_async_copy(x_in.at[i], xv.at[i], loads.at[0, i]).wait()
        pltpu.make_async_copy(ot_in.at[i], otv.at[i], loads.at[1, i]).wait()
        if calls > 1:
            @pl.when(i > 0)
            def _():
                pltpu.make_async_copy(go_send[0].at[plane.me], gov.at[i, plane.f, plane.r], gl.at[i]).wait()
                for k in range(1, plane.size):
                    go_copy(i, k, go_send[0]).wait_recv()
        @pl.when(i == 0)
        def _():
            pltpu.make_async_copy(go_in, gov.at[0], gl.at[0]).wait()
        def block_done(b):
            send_blocks(plane, i, b, gb, gx_out, xs, xr, xl)
            @pl.when(jnp.logical_and(i == calls - 1, b == 3))
            def _():
                for s in sums:
                    s.wait(1)
                    s.middle()
        flash_backward(xv.at[i], gov.at[i], otv.at[i], lse_ref.at[i], cos_ref, sin_ref, gb.at[i],
                       qm, dom, kf, vf, kt, delta, dqt, dka, dva, block_done)
        return 0
    lax.fori_loop(0, calls, call, 0)
    for i in range(1, calls):
        for k in range(1, plane.size):
            go_copy(i, k, go_send[i - 1]).wait_send()
    for s in sums:
        s.wait(2)
        s.last()
    for s in sums:
        s.close()
    wait_blocks(plane, calls, gb, gx_out, xs, xr, xl)


def attention_backward(x, go, go_sends, ot, lse, cos, sin, parts, orders):
    calls, nf, nr, fl, pt, w3 = x.shape
    lead = (nf, nr, fl, pt)
    lw = w3 // 3
    group = nf * nr
    nh = lw // HD
    seq = nf * nr * fl * pt
    blk = 2 * nr * pt
    hbm, vmem = pl.BlockSpec(memory_space=pl.ANY), pl.BlockSpec(memory_space=pltpu.VMEM)
    s, v, dma = jax.ShapeDtypeStruct, pltpu.VMEM, pltpu.SemaphoreType.DMA
    scratch, outs, jobs = sum_plan(parts, orders)
    return pl.pallas_call(
        functools.partial(bwd_all_kernel, calls=calls, count=len(parts), jobs=jobs),
        in_specs=[hbm, hbm, hbm, vmem, vmem, vmem] + [hbm] * (len(go_sends) + len(parts)),
        out_specs=[hbm] + [vmem] * len(parts),
        out_shape=[s((calls, group, fl, pt, w3), B16)] + outs,
        scratch_shapes=[v((calls,) + lead + (w3,), B16), v((calls,) + lead + (lw,), B16), v((calls, lw, seq), F32), v((calls,) + lead + (w3,), B16),
                        v((nh, seq, lw), B16), v((nh, seq, lw), B16), v((seq, lw), B16), v((seq, lw), B16), v((lw, seq), B16),
                        v((nh, seq), F32), v((lw, seq), F32), v((blk, lw), F32), v((blk, lw), F32),
                        dma((2, calls)), dma((calls, group)), dma((calls, group)), dma((calls,)), dma((calls, group)), dma((calls, group)), dma((calls,))] + scratch,
        compiler_params=pltpu.CompilerParams(vmem_limit_bytes=61 << 20, collective_id=1, has_side_effects=True),
        cost_estimate=pl.CostEstimate(flops=calls * seq * seq * lw * 5, bytes_accessed=calls * seq * lw * 48, transcendentals=calls * seq * seq * nh // 2),
        name="attention_backward",
    )(x, go, ot, lse, cos, sin, *go_sends, *parts)


def swap(block, axis, bit):
    size = lax.axis_size(axis)
    return lax.ppermute(block, axis, [(i, i ^ bit) for i in range(size)])


def exchange(blocks, axes=("frame", "row")):
    return lax.all_to_all(blocks, axes, 0, 0, tiled=True)


def after(value, *others):
    return lax.optimization_barrier((value,) + others)[0]


def on_device(tokens, context, noise_mod, clean_mod, w_qkv, b_qkv, w_out, b_out, w_up, b_up, w_down, b_down, cotangent):
    frames, patches, clips, width = tokens.shape
    count = frames * patches
    heads = width // HD
    nf, nr = lax.axis_size("frame"), lax.axis_size("row")
    group = nf * nr
    nh = max(1, heads // group)
    lw = nh * HD
    hg = heads // nh
    cs = group // hg
    calls = clips // cs
    grid = round((patches * nr) ** 0.5)
    fi, ri = lax.axis_index("frame"), lax.axis_index("row")

    is_clean = (fi * frames + jnp.arange(frames))[None, :] < context[:, None]
    mods = jnp.where(is_clean[:, :, None, None], clean_mod[None, None], noise_mod.transpose(1, 0, 2, 3))
    full = (clips, frames, patches, width)
    inputs = tokens.transpose(2, 0, 1, 3).reshape(clips, count, width)
    cots = cotangent.transpose(2, 0, 1, 3).reshape(clips, count, width)

    tok = jnp.arange(count)
    cos, sin = rope_angles(fi * frames + tok // patches, ri * patches + tok % patches, grid)
    cos_l = jnp.tile(jnp.concatenate([cos, cos], axis=1), (1, nh))
    sin_l = jnp.tile(jnp.concatenate([-sin, sin], axis=1), (1, nh))
    every = jnp.arange(nf * frames * nr * patches)
    cos_all, sin_all = rope_angles(every // (nr * patches), every % (nr * patches), grid)
    cos_t, sin_t = cos_all.T, sin_all.T
    row_of = lambda v: v.reshape(1, -1)

    lead = (nf, nr, frames, patches)
    h1, sends = [], []
    for c in range(clips):
        o, h = qkv_forward(inputs[c], mods[c], w_qkv, row_of(b_qkv), cos_l, sin_l, hg, lw)
        sends.append(o)
        h1.append(h)
    by_call = lambda v, w: [jnp.concatenate(v[i * cs:(i + 1) * cs], axis=0).reshape(group, frames, patches, w) for i in range(calls)]
    x, attn, ot, lse = attention_forward(by_call(sends, 3 * lw), lead, lw)
    attn = attn.reshape(clips, hg, count, lw)

    outs = [mlp(c, attn, inputs[c], cots[c], mods[c], w_out, row_of(b_out), w_up, row_of(b_up), w_down, row_of(b_down))
            for c in range(clips)]
    y, gmixed, gattn, gbranch, attn_n, h2, gdown, act, gpre, sums2, db_up, db_two = zip(*outs)
    gattn = by_call(gattn, lw)
    go = exchange(gattn[0]).reshape(lead + (lw,))

    mine = jnp.reshape(ri % 2, (1,)).astype(jnp.int32)
    nc = lax.axis_size("clip")
    def summed(*pairs):
        got = [swap(outer(a, b, 1 - mine), "row", 1) for a, b in pairs]
        parts = [outer(a, b, mine, g) for (a, b), g in zip(pairs, got)]
        return [p.reshape(nc, nf * nr // 2, p.shape[0] // (nc * nf * nr // 2), p.shape[1]) for p in parts]
    parts = summed((act, gdown), (h2, gpre), (attn_n, gbranch))
    orders = [[(True, 0, parts[0].shape[3])], [(False, 0, parts[1].shape[3])], [(True, 0, parts[2].shape[3])]]
    gproj, gw_down, gw_up, gw_out = attention_backward(x, go, gattn[1:], ot, lse, cos_t, sin_t, parts, orders)
    gproj = gproj.reshape(clips, hg, count, 3 * lw)
    backs = [qkv_back(c, gproj, inputs[c], gmixed[c], mods[c], w_qkv) for c in range(clips)]
    gtokens, sums1, db_qkv = zip(*backs)
    parts = summed((h1, gproj))
    ch = parts[0].shape[3]
    gw_qkv, = scatter_sums(parts, [[(True, 0, 3 * ch // 4), (False, 3 * ch // 4, ch // 4)]], 2)
    per = gw_qkv.shape[0]
    gw_qkv = gw_qkv.reshape(per, 2, hg // 2, 3, lw).transpose(0, 3, 1, 2, 4).reshape(per, 3 * width)

    gmods = jnp.stack([jnp.concatenate([sums1[c], sums2[c]], axis=1) for c in range(clips)], axis=0)
    clean = is_clean[:, :, None, None]
    noise_part = jnp.where(clean, 0.0, gmods).transpose(1, 0, 2, 3).astype(B16)
    quarter = width // nr
    sent = noise_part.reshape(frames, clips, 6, nr, quarter).transpose(3, 0, 1, 2, 4)
    grad_noise = jnp.sum(exchange(sent, "row").astype(F32), axis=0)
    clean_part = jnp.sum(jnp.where(clean, gmods, 0.0), axis=(0, 1))
    total = lax.axis_size(ALL)
    two = sum(db_two[1:], db_two[0])
    small = jnp.concatenate(
        [v.reshape(total, -1) for v in (sum(db_qkv[1:], db_qkv[0]), two[0], sum(db_up[1:], db_up[0]), two[1])]
        + [clean_part.reshape(6, total, -1).transpose(1, 0, 2).reshape(total, -1)], axis=1)
    small = jnp.sum(exchange(small, ALL), axis=0)
    ends = []
    at = 0
    for size in (3 * width, width, w_up.shape[1], width):
        ends.append(small[at:at + size // total])
        at += size // total
    gb_qkv, gb_out, gb_up, gb_down = ends
    grad_clean = small[at:].reshape(6, -1)
    back = lambda v: jnp.stack(v, axis=0).reshape(full).transpose(1, 2, 0, 3)
    return (back(y), back(gtokens), grad_noise, grad_clean, gw_qkv, gb_qkv, gw_out, gb_out, gw_up, gb_up, gw_down, gb_down)


def solution(mesh):
    token = P("frame", "row", "clip", None)
    rows = P(ALL, None)
    return jax.shard_map(
        on_device,
        mesh=mesh,
        in_specs=(token, P("clip"), P("frame", "clip", None, None)) + (P(),) * 9 + (token,),
        out_specs=(token, token, P("frame", "clip", None, "row"), P(None, ALL), rows, P(ALL), rows, P(ALL), rows, P(ALL), rows, P(ALL)),
        check_vma=False,
    )
```

```python
import functools
import jax, jax.numpy as jnp
from jax import lax
from jax.experimental import pallas as pl
from jax.experimental.pallas import tpu as pltpu
from jax.sharding import PartitionSpec as P
HD = 64
NN = (((1,), (0,)), ((), ()))
NT = (((1,), (1,)), ((), ()))
def dot(a, b, dims):
    return lax.dot_general(a, b, dims, preferred_element_type=jnp.float32)

def head_mask(values, head, heads):
    if heads == 1:
        return values
    lane = lax.broadcasted_iota(jnp.int32, values.shape, 1)
    return jnp.where(lane // HD == head, values, jnp.zeros_like(values))


def flash_forward(x_ref, o_ref, ot_ref, lse_ref, qm, kf, vt, sb, acc, mrow, done):
    nf, nr, fl, pt, width = x_ref.shape
    lw = width // 3
    nh = lw // HD
    tok = nr * pt
    frames = nf * fl
    blk = 2 * tok
    nblk = frames // 2
    def load(f, _):
        part = x_ref[f // fl, :, f % fl].reshape(tok, width)
        rows = pl.ds(pl.multiple_of(f * tok, tok), tok)
        q = part[:, :lw] * jnp.bfloat16(HD ** -0.5)
        for h in range(nh):
            qm[h, rows, :] = head_mask(q, h, nh)
        kf[rows, :] = part[:, lw:2 * lw]
        vt[:, rows] = part[:, 2 * lw:].T
        return 0
    lax.fori_loop(0, frames, load, 0)

    def fold(v, op):
        return op(v.reshape(v.shape[0] // 8, 8, v.shape[1]), axis=0)

    def stage(cur, nxt, grow):
        zero8 = jnp.zeros((8, blk), jnp.float32)
        if nxt is not None:
            na, nhd, ns = nxt
            n0 = pl.multiple_of(na * blk, blk)
            n1 = pl.multiple_of(na * blk + tok, tok)
            ncols = pl.ds(n0, blk)
            s0 = dot(kf[pl.ds(n0, tok), :], qm[nhd, ncols, :], NT)
            s1 = dot(kf[pl.ds(n1, tok), :], qm[nhd, pl.ds(n1, tok), :], NT)
            sb[ns, pl.ds(n0, tok), :] = s0
            sb[ns, pl.ds(n1, tok), tok:] = s1
            m0 = fold(s0, jnp.max)
            mm = jnp.concatenate([m0[:, :tok], jnp.maximum(m0[:, tok:], fold(s1, jnp.max))], axis=1)
        else:
            mm = zero8
        if cur is not None:
            ca, chd, cs = cur
            hs = slice(chd * HD, (chd + 1) * HD)
            c0 = pl.multiple_of(ca * blk, blk)
            c1 = pl.multiple_of(ca * blk + tok, tok)
            m = mrow[cs]
            p0 = jnp.exp(sb[cs, pl.ds(c0, tok), :] - m)
            p1 = jnp.exp(sb[cs, pl.ds(c1, tok), tok:] - m[:, tok:])
            l0 = fold(p0, jnp.sum)
            ll = jnp.concatenate([l0[:, :tok], l0[:, tok:] + fold(p1, jnp.sum)], axis=1)
            a0 = dot(vt[hs, pl.ds(c0, tok)], p0.astype(jnp.bfloat16), NN)
            a1 = dot(vt[hs, pl.ds(c1, tok)], p1.astype(jnp.bfloat16), NN)
            acc[hs, :tok] = a0[:, :tok]
            acc[hs, tok:] = a0[:, tok:] + a1
        else:
            ll = zero8
        def score(b, mm):
            rows = pl.ds(pl.multiple_of(b * blk, blk), blk)
            s = dot(kf[rows, :], qm[nhd, ncols, :], NT)
            sb[ns, rows, :] = s
            return jnp.maximum(mm, fold(s, jnp.max))
        def body(b, carry):
            mm, ll = carry
            if nxt is not None:
                mm = score(b, mm)
            if cur is not None:
                rows = pl.ds(pl.multiple_of(b * blk, blk), blk)
                p = jnp.exp(sb[cs, rows, :] - m)
                ll = ll + fold(p, jnp.sum)
                acc[hs, :] += dot(vt[hs, rows], p.astype(jnp.bfloat16), NN)
            return mm, ll
        trip = nxt[0] if cur is None else cur[0]
        mm, ll = lax.fori_loop(0, trip, body, (mm, ll))
        if grow and nxt is not None:
            mm = score(cur[0], mm)
        if nxt is not None:
            mrow[ns] = jnp.max(mm, axis=0, keepdims=True)
        if cur is not None:
            l = jnp.sum(ll, axis=0, keepdims=True)
            ot = acc[hs, :] / l
            acc[hs, :] = ot
            cols = pl.ds(c0, blk)
            ot_ref[hs, cols] = ot
            lse_ref[chd:chd + 1, cols] = m + jnp.log(l)

    def finish(a):
        o = acc[...].T.astype(jnp.bfloat16)
        for j in range(2):
            f = 2 * a + j
            o_ref[f // fl, :, f % fl] = o[j * tok:(j + 1) * tok].reshape(nr, pt, lw)
        done(a)

    slots = sb.shape[0]
    def q_block(a, last):
        par = (a * nh) % slots if nh % slots else 0
        for h in range(nh):
            cs = (par + h) % slots
            cur = (a, h, cs)
            ns = (par + h + 1) % slots
            if h + 1 < nh:
                stage(cur, (a, h + 1, ns), False)
            else:
                stage(cur, None if last else (a + 1, 0, ns), True)
        finish(a)
    stage(None, (0, 0, 0), False)
    def step(a, _):
        q_block(a, False)
        return 0
    lax.fori_loop(0, nblk - 1, step, 0)
    q_block(nblk - 1, True)


def rotate_back(t, cos, sin, nh):
    out = []
    for h in range(nh):
        a = t[h * HD:h * HD + HD // 2]
        b = t[h * HD + HD // 2:(h + 1) * HD]
        out += [a * cos + b * sin, b * cos - a * sin]
    return jnp.concatenate(out, axis=0)

def flash_backward(x_ref, go_ref, ot_ref, lse_ref, cos_ref, sin_ref, g_ref, qm, dom, kf, vf, kt, delta, dqt, dka, dva, done):
    nf, nr, fl, pt, width = x_ref.shape
    lw = width // 3
    nh = lw // HD
    tok = nr * pt
    frames = nf * fl
    blk = 2 * tok
    def load(f, _):
        part = x_ref[f // fl, :, f % fl].reshape(tok, width)
        go = go_ref[f // fl, :, f % fl].reshape(tok, lw)
        rows = pl.ds(pl.multiple_of(f * tok, tok), tok)
        q = part[:, :lw] * jnp.bfloat16(HD ** -0.5)
        k = part[:, lw:2 * lw]
        prod = go.T.astype(jnp.float32) * ot_ref[:, rows]
        for h in range(nh):
            qm[h, rows, :] = head_mask(q, h, nh)
            dom[h, rows, :] = head_mask(go, h, nh)
            delta[h:h + 1, rows] = jnp.sum(prod[h * HD:(h + 1) * HD], axis=0, keepdims=True)
        kf[rows, :] = k
        kt[:, rows] = k.T
        vf[rows, :] = part[:, 2 * lw:]
        dqt[:, rows] = jnp.zeros((lw, tok), jnp.float32)
        return 0
    lax.fori_loop(0, frames, load, 0)

    def work(k0, kn, q0, qn):
        rows, cols = pl.ds(k0, kn), pl.ds(q0, qn)
        dv, dk = [], []
        for h in range(nh):
            hs = slice(h * HD, (h + 1) * HD)
            qh, dh = qm[h, cols, :], dom[h, cols, :]
            p = jnp.exp(dot(kf[rows, :], qh, NT) - lse_ref[h:h + 1, cols])
            ds = (p * (dot(vf[rows, :], dh, NT) - delta[h:h + 1, cols])).astype(jnp.bfloat16)
            dv.append(dot(p.astype(jnp.bfloat16), dh, NN))
            dk.append(dot(ds, qh, NN))
            dqt[hs, cols] += dot(kt[hs, rows], ds, NN)
        return sum(dk[1:], dk[0]), sum(dv[1:], dv[0])

    def k_block(b, _):
        k0 = pl.multiple_of(b * blk, blk)
        k1 = pl.multiple_of(b * blk + tok, tok)
        dk, dv = work(k0, tok, k0, blk)
        dka[:tok, :] = dk
        dva[:tok, :] = dv
        dk, dv = work(k1, tok, k1, tok)
        dka[tok:, :] = dk
        dva[tok:, :] = dv
        def q_block(a, _):
            dk, dv = work(k0, blk, pl.multiple_of(a * blk, blk), blk)
            dka[...] += dk
            dva[...] += dv
            return 0
        lax.fori_loop(b + 1, frames // 2, q_block, 0)
        cols = pl.ds(k0, blk)
        dk = rotate_back(dka[...].T, cos_ref[:, cols], sin_ref[:, cols], nh).T.astype(jnp.bfloat16)
        dv = dva[...].astype(jnp.bfloat16)
        dq = rotate_back(dqt[:, cols] * HD ** -0.5, cos_ref[:, cols], sin_ref[:, cols], nh).T.astype(jnp.bfloat16)
        for j in range(2):
            f = 2 * b + j
            for n, part in enumerate((dq, dk, dv)):
                g_ref[f // fl, :, f % fl, :, n * lw:(n + 1) * lw] = part[j * tok:(j + 1) * tok].reshape(nr, pt, lw)
        done(b)
        return 0
    lax.fori_loop(0, frames // 2, k_block, 0)


ALL = ("clip", "frame", "row")
B16, F32 = jnp.bfloat16, jnp.float32


def rope_angles(frame_pos, patch_pos, grid):
    pair_index = jnp.arange(32)
    is_time = pair_index < 8
    is_height = (pair_index >= 8) & (pair_index < 20)
    exponent = jnp.where(
        is_time,
        pair_index / 8.0,
        jnp.where(is_height, (pair_index - 8) / 12.0, (pair_index - 20) / 12.0),
    ).astype(F32)
    frequency = jnp.power(F32(10000.0), -exponent)
    position = jnp.where(
        is_time[None, :],
        frame_pos[:, None],
        jnp.where(is_height[None, :], (patch_pos // grid)[:, None], (patch_pos % grid)[:, None]),
    ).astype(F32)
    angle = position * frequency[None, :]
    return (jnp.cos(angle), jnp.sin(angle))


def rotate_lanes(t, cos, sin):
    lane = lax.broadcasted_iota(jnp.int32, t.shape, 1)
    half = HD // 2
    lanes = t.shape[1]
    low = (lane % HD) < half
    part = jnp.where(low, pltpu.roll(t, lanes - half, 1), pltpu.roll(t, half, 1))
    return t * cos + part * sin


def stats(v):
    mean = jnp.mean(v, axis=1, keepdims=True)
    centre = v - mean
    inverse = lax.rsqrt(jnp.mean(centre * centre, axis=1, keepdims=True) + 1e-06)
    return centre * inverse, inverse


def qkv_kernel(x_ref, mod_ref, w_hbm, b_ref, cos_ref, sin_ref, o_ref, h_ref, w, sem):
    count, width = x_ref.shape
    hg, _, w3 = o_ref.shape
    lw = w3 // 3
    frames = mod_ref.shape[0]
    pt = count // frames
    copies = [pltpu.make_async_copy(w_hbm.at[:, pl.ds(j * width, width)], w.at[j], sem.at[j]) for j in range(3)]
    @pl.when(pl.program_id(0) == 0)
    def _():
        for c in copies:
            c.start()
    def one(f, _):
        rows = pl.ds(pl.multiple_of(f * pt, pt), pt)
        n, _inv = stats(x_ref[rows, :].astype(F32))
        h_ref[rows, :] = (n * (1.0 + mod_ref[f, 1:2, :]) + mod_ref[f, 0:1, :]).astype(B16)
        return 0
    lax.fori_loop(0, frames, one, 0)
    step = max(256, lw)
    for j in range(3):
        @pl.when(pl.program_id(0) == 0)
        def _():
            copies[j].wait()
        for a in range(0, width, step):
            t = dot(h_ref[...], w[j, :, a:a + step], NN) + b_ref[0:1, j * width + a:j * width + a + step]
            for g in range(step // lw):
                v = t[:, g * lw:(g + 1) * lw]
                if j < 2:
                    v = rotate_lanes(v, cos_ref[...], sin_ref[...])
                o_ref[a // lw + g, :, j * lw:(j + 1) * lw] = v.astype(B16)


def qkv_forward(x, mods, w, b, cos, sin, hg, lw):
    clips, count, width = x.shape
    frames = mods.shape[1]
    one = lambda *shape: pl.BlockSpec((None,) + shape, lambda c: (c,) + (0,) * len(shape))
    same = lambda *shape: pl.BlockSpec(shape, lambda c: (0,) * len(shape))
    return pl.pallas_call(
        qkv_kernel,
        grid=(clips,),
        in_specs=[one(count, width), one(frames, 6, width), pl.BlockSpec(memory_space=pl.ANY), same(1, 3 * width), same(count, lw), same(count, lw)],
        out_specs=(one(hg, count, 3 * lw), one(count, width)),
        out_shape=(jax.ShapeDtypeStruct((clips, hg, count, 3 * lw), B16), jax.ShapeDtypeStruct((clips, count, width), B16)),
        scratch_shapes=[pltpu.VMEM((3, width, width), B16), pltpu.SemaphoreType.DMA((3,))],
        compiler_params=pltpu.CompilerParams(vmem_limit_bytes=48 << 20, dimension_semantics=("arbitrary",)),
        cost_estimate=pl.CostEstimate(flops=6 * clips * count * width * width, bytes_accessed=clips * 10 * count * width + 6 * width * width, transcendentals=0),
        name="qkv",
    )(x, mods, w, b, cos, sin)


TN = (((0,), (0,)), ((), ()))


MESH = pl.DeviceIdType.MESH


class Plane:
    def __init__(self):
        self.nf, self.nr = lax.axis_size("frame"), lax.axis_size("row")
        self.f, self.r = lax.axis_index("frame"), lax.axis_index("row")
        self.size = self.nf * self.nr
        self.me = self.f * self.nr + self.r

    def peer(self, k):
        p = lax.rem(self.me + k, self.size)
        return p, p // self.nr, lax.rem(p, self.nr)


def greet(plane, with_clips):
    barrier = pltpu.get_barrier_semaphore()
    count = plane.size - 1
    for k in range(1, plane.size):
        _, f, r = plane.peer(k)
        pl.semaphore_signal(barrier, inc=1, device_id={"frame": f, "row": r}, device_id_type=MESH)
    if with_clips:
        nc = lax.axis_size("clip")
        c = lax.axis_index("clip")
        for k in range(1, nc):
            pl.semaphore_signal(barrier, inc=1, device_id={"clip": lax.rem(c + k, nc)}, device_id_type=MESH)
        count += nc - 1
    pl.semaphore_wait(barrier, count)


def remote(src, dst, send, recv, device):
    return pltpu.make_async_remote_copy(src_ref=src, dst_ref=dst, send_sem=send, recv_sem=recv, device_id=device, device_id_type=MESH)


def send_blocks(plane, i, a, buf, out, send, recv, local):
    fl = buf.shape[3]
    fh, at = 2 * a // fl, lax.rem(2 * a, fl)
    for r in range(plane.nr):
        src = buf.at[i, fh, r, pl.ds(at, 2)]
        dst = out.at[i, plane.me, pl.ds(at, 2)]
        own = jnp.logical_and(fh == plane.f, r == plane.r)
        dest = fh * plane.nr + r
        k = lax.rem(dest - plane.me + plane.size, plane.size)
        @pl.when(own)
        def _():
            pltpu.make_async_copy(src, dst, local.at[i]).start()
        @pl.when(jnp.logical_not(own))
        def _():
            remote(src, dst, send.at[i, k], recv.at[i, k], {"frame": fh, "row": r}).start()


def wait_blocks(plane, calls, buf, out, send, recv, local):
    for i in range(calls):
        pltpu.make_async_copy(buf.at[i, plane.f, plane.r], out.at[i, plane.me], local.at[i]).wait()
        for k in range(1, plane.size):
            p, f, r = plane.peer(k)
            copy = remote(buf.at[i, f, r], out.at[i, plane.me], send.at[i, k], recv.at[i, k], {"frame": f, "row": r})
            copy.wait_send()
            copy.wait_recv()


def fwd_all_kernel(*refs, calls):
    plane = Plane()
    x_send, x_out, a_out, ot_ref, lse_ref = refs[:5]
    xv, ob, qm, kf, vt, sb, acc, mrow, xs, xr, xl, os, orr, ol, save = refs[5:]
    greet(plane, False)
    for i in range(calls):
        pltpu.make_async_copy(x_send.at[i, plane.me], xv.at[i, plane.f, plane.r], xl.at[i]).start()
        for k in range(1, plane.size):
            p, f, r = plane.peer(k)
            remote(x_send.at[i, p], xv.at[i, plane.f, plane.r], xs.at[i, k], xr.at[i, k], {"frame": f, "row": r}).start()

    def arrive(i, what):
        for k in range(1, plane.size):
            p, f, r = plane.peer(k)
            copy = remote(x_send.at[i, p], xv.at[i, plane.f, plane.r], xs.at[i, k], xr.at[i, k], {"frame": f, "row": r})
            copy.wait_recv() if what else copy.wait_send()

    def call(i, _):
        pltpu.make_async_copy(x_send.at[i, plane.me], xv.at[i, plane.f, plane.r], xl.at[i]).wait()
        arrive(i, True)
        pltpu.make_async_copy(xv.at[i], x_out.at[i], save.at[i]).start()
        flash_forward(xv.at[i], ob.at[i], ot_ref.at[i], lse_ref.at[i], qm, kf, vt, sb, acc, mrow,
                      lambda a: send_blocks(plane, i, a, ob, a_out, os, orr, ol))
        return 0
    lax.fori_loop(0, calls, call, 0)
    for i in range(calls):
        arrive(i, False)
        pltpu.make_async_copy(xv.at[i], x_out.at[i], save.at[i]).wait()
    wait_blocks(plane, calls, ob, a_out, os, orr, ol)


def attention_forward(sends, lead, lw):
    calls = sends.shape[0]
    nf, nr, fl, pt = lead
    group = nf * nr
    nh = lw // HD
    seq = nf * nr * fl * pt
    blk = 2 * nr * pt
    hbm, vmem = pl.BlockSpec(memory_space=pl.ANY), pl.BlockSpec(memory_space=pltpu.VMEM)
    s, v, dma = jax.ShapeDtypeStruct, pltpu.VMEM, pltpu.SemaphoreType.DMA
    return pl.pallas_call(
        functools.partial(fwd_all_kernel, calls=calls),
        in_specs=[hbm],
        out_specs=(hbm, hbm, vmem, vmem),
        out_shape=(s((calls,) + lead + (3 * lw,), B16), s((calls, group, fl, pt, lw), B16),
                   s((calls, lw, seq), F32), s((calls, nh, seq), F32)),
        scratch_shapes=[v((calls,) + lead + (3 * lw,), B16), v((calls,) + lead + (lw,), B16), v((nh, seq, lw), B16),
                        v((seq, lw), B16), v((lw, seq), B16), v((2, seq, blk), F32), v((lw, blk), F32), v((2, 1, blk), F32),
                        dma((calls, group)), dma((calls, group)), dma((calls,)), dma((calls, group)), dma((calls, group)),
                        dma((calls,)), dma((calls,))],
        compiler_params=pltpu.CompilerParams(vmem_limit_bytes=56 << 20, collective_id=0, has_side_effects=True),
        cost_estimate=pl.CostEstimate(flops=calls * seq * seq * lw * 2, bytes_accessed=calls * seq * lw * 24, transcendentals=calls * seq * seq * nh // 2),
        name="attention_forward",
    )(sends)


class Sum:
    def __init__(self, plane, plane_first, part, out, cols, out_cols, v1, s1, v2, s2, v3, sems):
        self.plane, self.plane_first, self.part, self.out = plane, plane_first, part, out
        self.cols, self.out_cols = cols, out_cols
        self.v1, self.s1, self.v2, self.s2, self.v3, self.sems = v1, s1, v2, s2, v3, sems
        self.bit = lax.rem(plane.r, 2)

    def place(self, stage):
        plane = self.plane
        if (stage == 1) == self.plane_first:
            half = plane.nr // 2
            return plane.nf * half, plane.f * half + plane.r // 2, lambda p: {"frame": p // half, "row": lax.rem(p, half) * 2 + self.bit}
        return lax.axis_size("clip"), lax.axis_index("clip"), lambda p: {"clip": p}

    def block(self, stage, p):
        if stage == 2:
            return self.s1.at[p]
        cols = pl.ds(*self.cols)
        return self.part.at[:, p, :, cols] if self.plane_first else self.part.at[p, :, :, cols]

    def copies(self, stage):
        count, me, device = self.place(stage)
        dst = self.v1 if stage == 1 else self.v2
        base = 0 if stage == 1 else self.v1.shape[0]
        out = []
        for k in range(1, count):
            p = lax.rem(me + k, count)
            out.append(remote(self.block(stage, p), dst.at[me], self.sems.at[0, base + k], self.sems.at[1, base + k], device(p)))
        return out, pltpu.make_async_copy(self.block(stage, me), dst.at[me], self.sems.at[0, base])

    def start(self, stage):
        copies, own = self.copies(stage)
        for c in copies:
            c.start()
        own.start()

    def wait(self, stage):
        copies, own = self.copies(stage)
        for c in copies:
            c.wait()
        own.wait()

    def middle(self):
        def one(j, _):
            total = self.v1[0, j].astype(F32)
            for c in range(1, self.v1.shape[0]):
                total = total + self.v1[c, j].astype(F32)
            self.s1[j] = total.astype(B16)
            return 0
        lax.fori_loop(0, self.s1.shape[0], one, 0)
        self.start(2)

    def third(self):
        return remote(self.s2.at[1 - self.bit], self.v3, self.sems.at[0, self.sems.shape[1] - 1], self.sems.at[1, self.sems.shape[1] - 1],
                      {"row": self.plane.r + 1 - 2 * self.bit})

    def columns(self, b):
        first, size = self.cols
        return pl.ds(b * self.out_cols + first, size)

    def last(self):
        total = self.v2[0].astype(F32)
        for c in range(1, self.v2.shape[0]):
            total = total + self.v2[c].astype(F32)
        per = self.s2.shape[1]
        self.s2[0] = total[:per]
        self.s2[1] = total[per:]
        self.third().start()
        for b in range(2):
            @pl.when(self.bit == b)
            def _():
                self.out[:, self.columns(b)] = self.s2[b]

    def close(self):
        self.third().wait()
        for b in range(2):
            @pl.when(self.bit == b)
            def _():
                self.out[:, self.columns(1 - b)] = self.v3[...]


def sum_plan(parts, orders):
    scratch, outs, jobs = [], [], []
    for n, (part, order) in enumerate(zip(parts, orders)):
        nc, np_, two, ch = part.shape
        outs.append(jax.ShapeDtypeStruct((two // 2, 2 * ch), F32))
        for plane_first, first, cols in order:
            n1, n2 = (np_, nc) if plane_first else (nc, np_)
            scratch += [pltpu.VMEM((n1, n2, two, cols), B16), pltpu.VMEM((n2, two, cols), B16), pltpu.VMEM((n2, two, cols), B16),
                        pltpu.VMEM((2, two // 2, cols), F32), pltpu.VMEM((two // 2, cols), F32),
                        pltpu.SemaphoreType.DMA((2, n1 + n2 + 1))]
            jobs.append((n, plane_first, first, cols))
    return scratch, outs, jobs


def make_sums(plane, jobs, parts, outs, scratch):
    return [Sum(plane, plane_first, parts[n], outs[n], (first, cols), parts[n].shape[3], *scratch[6 * i:6 * i + 6])
            for i, (n, plane_first, first, cols) in enumerate(jobs)]


def bwd_all_kernel(*refs, calls, count, jobs):
    plane = Plane()
    x_in, go_in, ot_in, lse_ref, cos_ref, sin_ref = refs[:6]
    go_send = refs[6:5 + calls]
    at = 5 + calls
    parts = refs[at:at + count]
    at += count
    gx_out = refs[at]
    outs = refs[at + 1:at + 1 + count]
    at += 1 + count
    xv, gov, otv, gb, qm, dom, kf, vf, kt, delta, dqt, dka, dva, loads, gs, gr, gl, xs, xr, xl = refs[at:at + 20]
    sums = make_sums(plane, jobs, parts, outs, refs[at + 20:])
    greet(plane, True)
    load = [pltpu.make_async_copy(go_in, gov.at[0], gl.at[0])]
    for i in range(calls):
        load += [pltpu.make_async_copy(x_in.at[i], xv.at[i], loads.at[0, i]), pltpu.make_async_copy(ot_in.at[i], otv.at[i], loads.at[1, i])]
    for c in load:
        c.start()
    def go_copy(i, k, src):
        p, f, r = plane.peer(k)
        return remote(src.at[p], gov.at[i, plane.f, plane.r], gs.at[i, k], gr.at[i, k], {"frame": f, "row": r})
    for i in range(1, calls):
        pltpu.make_async_copy(go_send[i - 1].at[plane.me], gov.at[i, plane.f, plane.r], gl.at[i]).start()
        for k in range(1, plane.size):
            go_copy(i, k, go_send[i - 1]).start()
    for s in sums:
        s.start(1)

    def call(i, _):
        pltpu.make_async_copy(x_in.at[i], xv.at[i], loads.at[0, i]).wait()
        pltpu.make_async_copy(ot_in.at[i], otv.at[i], loads.at[1, i]).wait()
        if calls > 1:
            @pl.when(i > 0)
            def _():
                pltpu.make_async_copy(go_send[0].at[plane.me], gov.at[i, plane.f, plane.r], gl.at[i]).wait()
                for k in range(1, plane.size):
                    go_copy(i, k, go_send[0]).wait_recv()
        @pl.when(i == 0)
        def _():
            pltpu.make_async_copy(go_in, gov.at[0], gl.at[0]).wait()
        def block_done(b):
            send_blocks(plane, i, b, gb, gx_out, xs, xr, xl)
            @pl.when(jnp.logical_and(i == calls - 1, b == 3))
            def _():
                for s in sums:
                    s.wait(1)
                    s.middle()
        flash_backward(xv.at[i], gov.at[i], otv.at[i], lse_ref.at[i], cos_ref, sin_ref, gb.at[i],
                       qm, dom, kf, vf, kt, delta, dqt, dka, dva, block_done)
        return 0
    lax.fori_loop(0, calls, call, 0)
    for i in range(1, calls):
        for k in range(1, plane.size):
            go_copy(i, k, go_send[i - 1]).wait_send()
    for s in sums:
        s.wait(2)
        s.last()
    for s in sums:
        s.close()
    wait_blocks(plane, calls, gb, gx_out, xs, xr, xl)


def attention_backward(x, go, go_sends, ot, lse, cos, sin, parts, orders):
    calls, nf, nr, fl, pt, w3 = x.shape
    lead = (nf, nr, fl, pt)
    lw = w3 // 3
    group = nf * nr
    nh = lw // HD
    seq = nf * nr * fl * pt
    blk = 2 * nr * pt
    hbm, vmem = pl.BlockSpec(memory_space=pl.ANY), pl.BlockSpec(memory_space=pltpu.VMEM)
    s, v, dma = jax.ShapeDtypeStruct, pltpu.VMEM, pltpu.SemaphoreType.DMA
    scratch, outs, jobs = sum_plan(parts, orders)
    return pl.pallas_call(
        functools.partial(bwd_all_kernel, calls=calls, count=len(parts), jobs=jobs),
        in_specs=[hbm, hbm, hbm, vmem, vmem, vmem] + [hbm] * (len(go_sends) + len(parts)),
        out_specs=[hbm] + [vmem] * len(parts),
        out_shape=[s((calls, group, fl, pt, w3), B16)] + outs,
        scratch_shapes=[v((calls,) + lead + (w3,), B16), v((calls,) + lead + (lw,), B16), v((calls, lw, seq), F32), v((calls,) + lead + (w3,), B16),
                        v((nh, seq, lw), B16), v((nh, seq, lw), B16), v((seq, lw), B16), v((seq, lw), B16), v((lw, seq), B16),
                        v((nh, seq), F32), v((lw, seq), F32), v((blk, lw), F32), v((blk, lw), F32),
                        dma((2, calls)), dma((calls, group)), dma((calls, group)), dma((calls,)), dma((calls, group)), dma((calls, group)), dma((calls,))] + scratch,
        compiler_params=pltpu.CompilerParams(vmem_limit_bytes=61 << 20, collective_id=1, has_side_effects=True),
        cost_estimate=pl.CostEstimate(flops=calls * seq * seq * lw * 5, bytes_accessed=calls * seq * lw * 48, transcendentals=calls * seq * seq * nh // 2),
        name="attention_backward",
    )(x, go, ot, lse, cos, sin, *go_sends, *parts)


def mlp_kernel(a_ref, x_hbm, g_hbm, mod_ref, wo_ref, bo_ref, wu_ref, bu_ref, wd_ref, bd_ref,
               y_out, gm_out, ga_out, go_out, pd_out, pu_out, po_out, sums_ref, du_ref, db_ref,
               g, an, branch, mixed, h, gd, down, gh, st, gav, sd, su, rd, ru, kd, ku, pd, pu, *sems, calls):
    io, od, pair, free, done, gs, gr, gl, oo = sems
    plane = Plane()
    bit = lax.rem(plane.r, 2)
    partner = {"row": plane.r + 1 - 2 * bit}
    clips, hg, count, lw = a_ref.shape
    width = an.shape[1]
    frames = mod_ref.shape[0]
    pt = clips * count // frames
    step, steps = pl.program_id(0), pl.num_programs(0)
    fc = wu_ref.shape[1]
    slots = rd.shape[0]
    hw, hf = width // 2, fc // 2

    def each(first, last, fn):
        def one(f, _):
            fn(f, pl.ds(pl.multiple_of(f * pt, pt), pt))
            return 0
        lax.fori_loop(first, last, one, 0)

    def split(value, size, send, keep):
        for b in range(2):
            @pl.when(bit == b)
            def _():
                send[...] = value[:, (1 - b) * size:(2 - b) * size].astype(B16)
                keep[...] = value[:, b * size:(b + 1) * size]

    @pl.when(step == 0)
    def _():
        loads = [pltpu.make_async_copy(x_hbm, h, io.at[0]), pltpu.make_async_copy(g_hbm, g.at[pl.ds(0, clips * count)], io.at[1])]
        for c in loads:
            c.start()
        greet(plane, False)
        for c in range(clips):
            for i in range(hg):
                an[c * count:(c + 1) * count, i * lw:(i + 1) * lw] = a_ref[c, i]
        branch[...] = dot(an[:clips * count, :], wo_ref[...], NN) + bo_ref[...]
        for c in loads:
            c.wait()
        def fn(f, rows):
            m = h[rows, :].astype(F32) + mod_ref[f, 2:3, :] * branch[rows, :]
            mean = jnp.mean(m, axis=1, keepdims=True)
            centre = m - mean
            inv = lax.rsqrt(jnp.mean(centre * centre, axis=1, keepdims=True) + 1e-06)
            mixed[rows, :] = m
            st[rows, :128] = jnp.broadcast_to(mean, (pt, 128))
            st[rows, 128:] = jnp.broadcast_to(inv, (pt, 128))
            h[rows, :] = (centre * inv * (1.0 + mod_ref[f, 4:5, :]) + mod_ref[f, 3:4, :]).astype(B16)
            gd[rows, :] = (g[rows, :].astype(F32) * mod_ref[f, 5:6, :]).astype(B16)
        each(0, frames, fn)
        down[...] = jnp.zeros_like(down)
        gh[...] = jnp.zeros_like(gh)

    c0 = (2.0 / 3.141592653589793) ** 0.5
    c1 = 0.044715
    wu, wd = wu_ref[...], wd_ref[...]
    wide, tall, bias = None, None, None
    for c in range(clips):
        rows = slice(c * count, (c + 1) * count)
        hr, gr_ = h[rows, :], gd[rows, :]
        pre = dot(hr, wu, NN) + bu_ref[...]
        gact = dot(gr_, wd, NT)
        sq = pre * pre
        u = jnp.tanh(pre * (c0 + (c0 * c1) * sq))
        half = 0.5 * (1.0 + u)
        act = (pre * half).astype(B16)
        slope = half + (0.5 * pre) * (1.0 - u * u) * (c0 + (3.0 * c0 * c1) * sq)
        gp = (gact * slope).astype(B16)
        down[rows, :] += dot(act, wd, NN)
        gh[rows, :] += dot(gp, wu, NT)
        d, t, b = dot(act, gr_, TN), dot(hr, gp, TN), jnp.sum(gp.astype(F32), axis=0, keepdims=True)
        wide = d if wide is None else wide + d
        tall = t if tall is None else tall + t
        bias = b if bias is None else bias + b
    du_ref[...] = bias
    now, slot = lax.rem(step, 2), lax.rem(step, slots)

    def swaps(j):
        n, s = lax.rem(j, 2), lax.rem(j, slots)
        return (remote(sd.at[n], rd.at[s], pair.at[0, n], pair.at[1, s], partner),
                remote(su.at[n], ru.at[s], pair.at[2, n], pair.at[3, s], partner))

    def stores(j):
        n = lax.rem(j, 2)
        return (pltpu.make_async_copy(pd.at[n], pd_out.at[pl.ds(pl.multiple_of(j * fc, fc), fc)], od.at[0, n]),
                pltpu.make_async_copy(pu.at[n], pu_out.at[:, pl.ds(pl.multiple_of(j * hf, hf), hf)], od.at[1, n]))

    def finish(j):
        n, s = lax.rem(j, 2), lax.rem(j, slots)
        @pl.when(j >= 2)
        def _():
            for c in stores(j - 2):
                c.wait()
        for c in swaps(j):
            c.wait_recv()
        pd[n] = (kd[n] + rd[s].astype(F32)).astype(B16)
        pu[n] = (ku[n] + ru[s].astype(F32)).astype(B16)
        for c in stores(j):
            c.start()
        @pl.when(j + slots < steps)
        def _():
            pl.semaphore_signal(free, inc=1, device_id=partner, device_id_type=MESH)

    @pl.when(step >= 2)
    def _():
        for c in swaps(step - 2):
            c.wait_send()
    split(wide, hw, sd.at[now], kd.at[now])
    split(tall, hf, su.at[now], ku.at[now])
    @pl.when(step >= slots)
    def _():
        pl.semaphore_wait(free, 1)
    for c in swaps(step):
        c.start()
    @pl.when(step >= 1)
    def _():
        finish(step - 1)

    @pl.when(step == steps - 1)
    def _():
        db_ref[...] = jnp.zeros_like(db_ref)
        def fn(f, rows):
            gf = g[rows, :].astype(F32)
            d = down[rows, :] + bd_ref[...]
            m = mixed[rows, :]
            ghf = gh[rows, :]
            inv = st[rows, 128:129]
            n = (m - st[rows, 0:1]) * inv
            t = ghf * (1.0 + mod_ref[f, 4:5, :])
            back = t - jnp.mean(t, axis=1, keepdims=True) - n * jnp.mean(t * n, axis=1, keepdims=True)
            gm = gf + inv * back
            gbr = (gm * mod_ref[f, 2:3, :]).astype(B16)
            s = lambda v: jnp.sum(v, axis=0, keepdims=True)
            sums_ref[f] = jnp.concatenate([s(gm * branch[rows, :]), s(ghf), s(ghf * n), s(gf * d)], axis=0)
            db_ref[...] += jnp.concatenate([s(gbr.astype(F32)), s(gd[rows, :].astype(F32))], axis=0)
            mixed[rows, :] = gm
            h[rows, :] = gbr
            gd[rows, :] = (m + mod_ref[f, 5:6, :] * d).astype(B16)
        group = plane.size
        per_call = clips // calls
        def go_copies():
            out = []
            for k in range(1, group):
                p, f, r = plane.peer(k)
                out.append(remote(gav.at[p], go_out.at[plane.f, plane.r], gs.at[k], gr.at[k], {"frame": f, "row": r}))
            return out, pltpu.make_async_copy(gav.at[plane.me], go_out.at[plane.f, plane.r], gl)
        def back_out(c):
            each(c * frames // clips, (c + 1) * frames // clips, fn)
            ga = dot(h[c * count:(c + 1) * count, :], wo_ref[...], NT).astype(B16)
            for i in range(hg):
                gav[c * hg + i] = ga[:, i * lw:(i + 1) * lw]
        for c in range(per_call):
            back_out(c)
        copies, own = go_copies()
        for c in copies:
            c.start()
        own.start()
        for c in range(per_call, clips):
            back_out(c)
        outs = [pltpu.make_async_copy(gd, y_out, oo.at[0]), pltpu.make_async_copy(mixed, gm_out, oo.at[1])]
        if calls > 1:
            outs.append(pltpu.make_async_copy(gav.at[pl.ds(group, (calls - 1) * group)], ga_out, oo.at[2]))
        for c in outs:
            c.start()
        finish(step)
        pl.semaphore_signal(done, inc=1, device_id=partner, device_id_type=MESH)
        wide_out = dot(an[:clips * count, :], h[...], TN)
        for b in range(2):
            @pl.when(bit == b)
            def _():
                an[:width, :hw] = wide_out[:, (1 - b) * hw:(2 - b) * hw].astype(B16)
                down[:width, :hw] = wide_out[:, b * hw:(b + 1) * hw]
        pl.semaphore_wait(done, 1)
        ro = g.at[pl.ds(0, width), pl.ds(0, hw)]
        last = remote(an.at[pl.ds(0, width), pl.ds(0, hw)], ro, pair.at[0, 2], pair.at[1, slots], partner)
        last.start()
        last.wait()
        an[:width, hw:] = (down[:width, :hw] + g[:width, :hw].astype(F32)).astype(B16)
        outs.append(pltpu.make_async_copy(an.at[pl.ds(0, width), pl.ds(hw, hw)], po_out, oo.at[3]))
        outs[-1].start()
        for c in copies:
            c.wait()
        own.wait()
        for c in swaps(step - 1) + swaps(step):
            c.wait_send()
        for c in stores(step - 1) + stores(step):
            c.wait()
        for c in outs:
            c.wait()


def mlp(attn, x, g, mods, w_out, b_out, w_up, b_up, w_down, b_down, calls, lead):
    clips, hg, count, lw = attn.shape
    rows, width = x.shape
    ff = w_up.shape[1]
    frames = mods.shape[0]
    fc = min(512, ff)
    hw, hf = width // 2, fc // 2
    nf, nr = lead[:2]
    group = nf * nr
    slots = 3
    tall = max(rows, width)
    whole = lambda *shape: pl.BlockSpec(shape, lambda j: (0,) * len(shape), pipeline_mode=pl.Buffered(1))
    keep = lambda *shape: pl.BlockSpec(shape, lambda j: (0,) * len(shape))
    hbm = pl.BlockSpec(memory_space=pl.ANY)
    s, v, dma = jax.ShapeDtypeStruct, pltpu.VMEM, pltpu.SemaphoreType.DMA
    return pl.pallas_call(
        functools.partial(mlp_kernel, calls=calls),
        grid=(ff // fc,),
        in_specs=[whole(clips, hg, count, lw), hbm, hbm, whole(frames, 6, width), whole(width, width), whole(1, width),
                  pl.BlockSpec((width, fc), lambda j: (0, j)), pl.BlockSpec((1, fc), lambda j: (0, j)),
                  pl.BlockSpec((fc, width), lambda j: (j, 0)), whole(1, width)],
        out_specs=[hbm] * 7 + [keep(frames, 4, width), pl.BlockSpec((1, fc), lambda j: (0, j)), keep(2, width)],
        out_shape=[s((rows, width), B16), s((rows, width), F32), s((max(1, calls - 1) * group, count, lw), B16),
                   s((nf, nr, count, lw), B16), s((ff, hw), B16), s((width, ff // 2), B16), s((width, hw), B16),
                   s((frames, 4, width), F32), s((1, ff), F32), s((2, width), F32)],
        scratch_shapes=[v((tall, width), B16), v((tall, width), B16), v((rows, width), F32), v((rows, width), F32),
                        v((rows, width), B16), v((rows, width), B16), v((tall, width), F32), v((rows, width), F32), v((rows, 256), F32),
                        v((clips * hg, count, lw), B16), v((2, fc, hw), B16), v((2, width, hf), B16), v((slots, fc, hw), B16),
                        v((slots, width, hf), B16), v((2, fc, hw), F32), v((2, width, hf), F32), v((2, fc, hw), B16), v((2, width, hf), B16),
                        dma((2,)), dma((2, 2)), dma((4, slots + 1)), pltpu.SemaphoreType.REGULAR, pltpu.SemaphoreType.REGULAR,
                        dma((group,)), dma((group,)), dma, dma((4,))],
        compiler_params=pltpu.CompilerParams(vmem_limit_bytes=63 << 20, dimension_semantics=("arbitrary",), collective_id=3, has_side_effects=True),
        cost_estimate=pl.CostEstimate(flops=2 * rows * width * (3 * width + 6 * ff), bytes_accessed=8 * width * ff + 20 * rows * width, transcendentals=rows * ff),
        name="mlp",
    )(attn, x, g, mods, w_out, b_out, w_up, b_up, w_down, b_down)


def tail_kernel(gp_hbm, h_hbm, w_hbm, x_hbm, gm_hbm, mod_ref, clean_ref, sums2_ref, vec_ref,
                o_out, gw_ref, noise_ref, vec_out,
                gp, h, w, x, gm, full, gh, send, got, part, s1s, dbq, nsend, nrecv, vsend, v1, vmid, v2, io, pair, nsem, vsem, oo, *scratch, jobs):
    plane = Plane()
    clips, hg, count, w3 = gp_hbm.shape
    lw = w3 // 3
    width = w.shape[0]
    frames = mod_ref.shape[0] // clips
    pt = count // frames
    nc, nf, nr = lax.axis_size("clip"), plane.nf, plane.nr
    group = plane.size
    bit = lax.rem(plane.r, 2)
    partner = {"row": plane.r + 1 - 2 * bit}
    packed = max(1, 128 * 3 // w3)
    blocks = hg // 2 // packed
    bw = packed * w3
    loads = [pltpu.make_async_copy(gp_hbm, gp, io.at[0]), pltpu.make_async_copy(h_hbm, h, io.at[1]),
             pltpu.make_async_copy(w_hbm, w, io.at[2]), pltpu.make_async_copy(x_hbm, x, io.at[3]), pltpu.make_async_copy(gm_hbm, gm, io.at[4])]
    for c in loads:
        c.start()
    sums = make_sums(plane, jobs, [part], [gw_ref], scratch)
    greet(plane, True)
    for c in loads[:2]:
        c.wait()

    def outer(j):
        total = None
        for c in range(clips):
            b = jnp.concatenate([gp[c, j * packed + i] for i in range(packed)], axis=1)
            t = dot(h[c], b, TN)
            total = t if total is None else total + t
        return total

    def swap(j):
        return remote(send.at[j], got.at[j], pair.at[0, j], pair.at[1, j], partner)
    other = 1 - bit
    for j in range(blocks):
        send[j] = outer(other * blocks + j).astype(B16)
        swap(j).start()
    for s, (_, plane_first, first, cols) in zip(sums, jobs):
        j = first // bw
        total = outer(bit * blocks + j)
        swap(j).wait_recv()
        total = (total + got[j].astype(F32)).astype(B16)
        part[:, :, :, first:first + cols] = total.reshape(part.shape[:3] + (cols,))
        s.start(1)

    for c in loads[2:]:
        c.wait()
    dbq[...] = jnp.zeros_like(dbq)
    for c in range(clips):
        for j in range(3):
            for g in range(hg):
                full[:, j * width + g * lw:j * width + (g + 1) * lw] = gp[c, g, :, j * lw:(j + 1) * lw]
        gh[...] = dot(full[...], w[...], NT)
        dbq[...] += jnp.sum(full[...].astype(F32), axis=0, keepdims=True)
        def one(f, _):
            rows = pl.ds(pl.multiple_of(f * pt, pt), pt)
            cf = c * frames + f
            n, inv = stats(x[c, rows, :].astype(F32))
            ghf = gh[rows, :]
            t = ghf * (1.0 + mod_ref[cf, 1:2, :])
            back = t - jnp.mean(t, axis=1, keepdims=True) - n * jnp.mean(t * n, axis=1, keepdims=True)
            gm[c, rows, :] = gm[c, rows, :] + inv * back
            s = lambda v: jnp.sum(v, axis=0, keepdims=True)
            s1s[cf, 0:2, :] = jnp.concatenate([s(ghf), s(ghf * n)], axis=0)
            s1s[cf, 2:6, :] = sums2_ref[cf]
            return 0
        lax.fori_loop(0, frames, one, 0)
        pltpu.make_async_copy(gm.at[c], o_out.at[c], oo.at[c]).start()
        for s in (sums[1:2] if c < clips - 1 else sums[2 if clips > 1 else 1:3]):
            s.wait(1)
            s.middle()

    quarter = width // nr
    vsend[...] = jnp.zeros_like(vsend)
    def gather(cf, total):
        both = s1s[cf, 0:6, :]
        keep = clean_ref[cf]
        noise = jnp.where(keep > 0.5, jnp.zeros_like(both), both)
        for q in range(nr):
            nsend[q, cf] = noise[:, q * quarter:(q + 1) * quarter].astype(B16)
        return total + (both - noise)
    clean_sum = lax.fori_loop(0, clips * frames, gather, jnp.zeros((6, width), F32))
    def ncopies():
        out = []
        for k in range(1, nr):
            q = lax.rem(plane.r + k, nr)
            out.append(remote(nsend.at[q], nrecv.at[plane.r], nsem.at[0, k], nsem.at[1, k], {"row": q}))
        return out
    for c in ncopies():
        c.start()
    vsend[:6, :] = clean_sum
    vsend[6:9, :] = jnp.concatenate([dbq[:, j * width:(j + 1) * width] for j in range(3)], axis=0)
    vsend[9:9 + vec_ref.shape[0], :] = vec_ref[...]
    def vcopies(stage):
        out = []
        if stage == 1:
            for k in range(1, group):
                p, f, r = plane.peer(k)
                out.append(remote(vsend, v1.at[plane.me], vsem.at[0, k], vsem.at[1, k], {"frame": f, "row": r}))
        else:
            c = lax.axis_index("clip")
            for k in range(1, nc):
                out.append(remote(vmid, v2.at[c], vsem.at[0, group + k], vsem.at[1, group + k], {"clip": lax.rem(c + k, nc)}))
        return out
    for c in vcopies(1):
        c.start()
    for s in sums[:1] + sums[3:]:
        s.wait(1)
        s.middle()
    for c in vcopies(1):
        c.wait()
    total = vsend[...]
    for k in range(1, group):
        p, _, _ = plane.peer(k)
        total = total + v1[p]
    vmid[...] = total
    for c in vcopies(2):
        c.start()
    for c in ncopies():
        c.wait()
    def add_noise(cf, _):
        total = nsend[plane.r, cf].astype(F32)
        for k in range(1, nr):
            total = total + nrecv[lax.rem(plane.r + k, nr), cf].astype(F32)
        noise_ref[cf] = total
        return 0
    lax.fori_loop(0, clips * frames, add_noise, 0)
    for s in sums:
        s.wait(2)
        s.last()
    for c in vcopies(2):
        c.wait()
    total = vmid[...]
    for k in range(1, nc):
        total = total + v2[lax.rem(lax.axis_index("clip") + k, nc)]
    vec_out[...] = total
    for s in sums:
        s.close()
    for j in range(blocks):
        swap(j).wait_send()
    for c in range(clips):
        pltpu.make_async_copy(gm.at[c], o_out.at[c], oo.at[c]).wait()


def tail(gproj, h1, w_qkv, x, gmixed, mods, clean, sums2, vec):
    clips, hg, count, w3 = gproj.shape
    lw = w3 // 3
    width = x.shape[2]
    nc, nf, nr = (lax.axis_size(a) for a in ALL)
    group = nf * nr
    frames = mods.shape[0]
    two = width // (nc * nf * nr // 2)
    packed = max(1, 128 * 3 // w3)
    blocks, bw = hg // 2 // packed, packed * w3
    vrows = -(-(9 + vec.shape[0]) // 8) * 8
    hbm, vmem = pl.BlockSpec(memory_space=pl.ANY), pl.BlockSpec(memory_space=pltpu.VMEM)
    s, v, dma = jax.ShapeDtypeStruct, pltpu.VMEM, pltpu.SemaphoreType.DMA
    shape = jax.ShapeDtypeStruct((nc, nf * nr // 2, two, blocks * bw), B16)
    order = [(False if j == 0 else True, j * bw, bw) for j in range(blocks)]
    scratch, outs, jobs = sum_plan([shape], [order])
    return pl.pallas_call(
        functools.partial(tail_kernel, jobs=jobs),
        in_specs=[hbm] * 5 + [vmem] * 4,
        out_specs=[hbm, vmem, vmem, vmem],
        out_shape=[s((clips, count, width), F32)] + outs + [s((frames, 6, width // nr), F32), s((vrows, width), F32)],
        scratch_shapes=[v((clips, hg, count, w3), B16), v((clips, count, width), B16), v((width, 3 * width), B16), v((clips, count, width), B16),
                        v((clips, count, width), F32), v((count, 3 * width), B16), v((count, width), F32), v((blocks, width, bw), B16),
                        v((blocks, width, bw), B16), v(shape.shape, B16), v((frames, 8, width), F32), v((1, 3 * width), F32),
                        v((nr, frames, 6, width // nr), B16), v((nr, frames, 6, width // nr), B16), v((vrows, width), F32), v((group, vrows, width), F32),
                        v((vrows, width), F32), v((nc, vrows, width), F32), dma((5,)), dma((2, blocks)), dma((2, nr)), dma((2, group + nc)), dma((clips,))] + scratch,
        compiler_params=pltpu.CompilerParams(vmem_limit_bytes=62 << 20, collective_id=2, has_side_effects=True),
        cost_estimate=pl.CostEstimate(flops=12 * clips * count * width * width, bytes_accessed=40 * clips * count * width, transcendentals=0),
        name="tail",
    )(gproj, h1, w_qkv, x, gmixed, mods, clean, sums2, vec)


def on_device(tokens, context, noise_mod, clean_mod, w_qkv, b_qkv, w_out, b_out, w_up, b_up, w_down, b_down, cotangent):
    frames, patches, clips, width = tokens.shape
    count = frames * patches
    heads = width // HD
    nf, nr = lax.axis_size("frame"), lax.axis_size("row")
    group = nf * nr
    nh = max(1, heads // group)
    lw = nh * HD
    hg = heads // nh
    cs = group // hg
    calls = clips // cs
    grid = round((patches * nr) ** 0.5)
    fi, ri = lax.axis_index("frame"), lax.axis_index("row")

    is_clean = (fi * frames + jnp.arange(frames))[None, :] < context[:, None]
    mods = jnp.where(is_clean[:, :, None, None], clean_mod[None, None], noise_mod.transpose(1, 0, 2, 3))
    full = (clips, frames, patches, width)
    inputs = tokens.transpose(2, 0, 1, 3).reshape(clips, count, width)
    cots = cotangent.transpose(2, 0, 1, 3).reshape(clips, count, width)

    tok = jnp.arange(count)
    cos, sin = rope_angles(fi * frames + tok // patches, ri * patches + tok % patches, grid)
    cos_l = jnp.tile(jnp.concatenate([cos, cos], axis=1), (1, nh))
    sin_l = jnp.tile(jnp.concatenate([-sin, sin], axis=1), (1, nh))
    every = jnp.arange(nf * frames * nr * patches)
    cos_all, sin_all = rope_angles(every // (nr * patches), every % (nr * patches), grid)
    cos_t, sin_t = cos_all.T, sin_all.T
    row_of = lambda v: v.reshape(1, -1)

    lead = (nf, nr, frames, patches)
    sends, h1 = qkv_forward(inputs, mods, w_qkv, row_of(b_qkv), cos_l, sin_l, hg, lw)
    x, attn, ot, lse = attention_forward(sends.reshape(calls, group, frames, patches, 3 * lw), lead, lw)
    attn = attn.reshape(clips, hg, count, lw)

    rows = clips * count
    by_frame = mods.reshape(clips * frames, 6, width)
    y, gmixed, ga, go, part_down, part_up, part_out, sums2, db_up, db_two = mlp(
        attn, inputs.reshape(rows, width), cots.reshape(rows, width), by_frame,
        w_out, row_of(b_out), w_up, row_of(b_up), w_down, row_of(b_down), calls, lead)
    go = go.reshape(lead + (lw,))
    go_sends = [v for v in ga.reshape((-1, group, frames, patches, lw))][:calls - 1]
    gmixed = gmixed.reshape(clips, count, width)

    nc = lax.axis_size("clip")
    as_blocks = lambda p: p.reshape(nc, nf * nr // 2, p.shape[0] // (nc * nf * nr // 2), p.shape[1])
    parts = [as_blocks(p) for p in (part_down, part_up, part_out)]
    orders = [[(True, 0, parts[0].shape[3])], [(False, 0, parts[1].shape[3])], [(False, 0, parts[2].shape[3])]]
    gproj, gw_down, gw_up, gw_out = attention_backward(x, go, go_sends, ot, lse, cos_t, sin_t, parts, orders)
    gproj = gproj.reshape(clips, hg, count, 3 * lw)
    fc = min(512, w_up.shape[1])
    gw_up = gw_up.reshape(gw_up.shape[0], 2, -1, fc // 2).transpose(0, 2, 1, 3).reshape(gw_up.shape[0], -1)
    clean = jnp.broadcast_to(is_clean.reshape(-1, 1, 1), (clips * frames, 1, width)).astype(F32)
    vec = jnp.concatenate([db_up.reshape(-1, width), db_two], axis=0)
    gtokens, gw_qkv, noise, vec = tail(gproj, h1, w_qkv, inputs, gmixed, by_frame, clean, sums2, vec)
    per = gw_qkv.shape[0]
    gw_qkv = gw_qkv.reshape(per, 2, hg // 2, 3, lw).transpose(0, 3, 1, 2, 4).reshape(per, 3 * width)
    grad_noise = noise.reshape(clips, frames, 6, -1).transpose(1, 0, 2, 3)
    total = lax.axis_size(ALL)
    place = lax.axis_index(ALL)
    def own(at, size):
        return lax.dynamic_slice_in_dim(vec[at:at + size].reshape(-1), place * (size * width // total), size * width // total)
    grad_clean = lax.dynamic_slice_in_dim(vec[:6], place * (width // total), width // total, 1)
    ff = w_up.shape[1] // width
    gb_qkv, gb_up, gb_out, gb_down = own(6, 3), own(9, ff), own(9 + ff, 1), own(10 + ff, 1)
    back = lambda v: v.reshape(full).transpose(1, 2, 0, 3)
    return (back(y), back(gtokens), grad_noise, grad_clean, gw_qkv, gb_qkv, gw_out, gb_out, gw_up, gb_up, gw_down, gb_down)


def solution(mesh):
    token = P("frame", "row", "clip", None)
    rows = P(ALL, None)
    return jax.shard_map(
        on_device,
        mesh=mesh,
        in_specs=(token, P("clip"), P("frame", "clip", None, None)) + (P(),) * 9 + (token,),
        out_specs=(token, token, P("frame", "clip", None, "row"), P(None, ALL), rows, P(ALL), rows, P(ALL), rows, P(ALL), rows, P(ALL)),
        check_vma=False,
    )
```

```python
import functools
import jax, jax.numpy as jnp
from jax import lax
from jax.experimental import pallas as pl
from jax.experimental.pallas import tpu as pltpu
from jax.sharding import PartitionSpec as P
HD = 64
NN = (((1,), (0,)), ((), ()))
NT = (((1,), (1,)), ((), ()))
def dot(a, b, dims):
    return lax.dot_general(a, b, dims, preferred_element_type=jnp.float32)

def head_mask(values, head, heads):
    if heads == 1:
        return values
    lane = lax.broadcasted_iota(jnp.int32, values.shape, 1)
    return jnp.where(lane // HD == head, values, jnp.zeros_like(values))


def flash_forward(x_ref, o_ref, ot_ref, lse_ref, qm, kf, vt, sa, sb, acc, ma, mb, done):
    nf, nr, fl, pt, width = x_ref.shape
    lw = width // 3
    nh = lw // HD
    tok = nr * pt
    frames = nf * fl
    blk = 2 * tok
    nblk = frames // 2
    def load(f, _):
        part = x_ref[f // fl, :, f % fl].reshape(tok, width)
        rows = pl.ds(pl.multiple_of(f * tok, tok), tok)
        q = part[:, :lw] * jnp.bfloat16(HD ** -0.5)
        for h in range(nh):
            qm[h, rows, :] = head_mask(q, h, nh)
        kf[rows, :] = part[:, lw:2 * lw]
        vt[:, rows] = part[:, 2 * lw:].T
        return 0
    lax.fori_loop(0, frames, load, 0)

    def fold(v, op):
        return op(v.reshape(v.shape[0] // 8, 8, v.shape[1]), axis=0)

    def stage(cur, nxt, grow):
        zero8 = jnp.zeros((8, blk), jnp.float32)
        if nxt is not None:
            na, nhd, ns = nxt
            n0 = pl.multiple_of(na * blk, blk)
            n1 = pl.multiple_of(na * blk + tok, tok)
            ncols = pl.ds(n0, blk)
            s0 = dot(kf[pl.ds(n0, tok), :], qm[nhd, ncols, :], NT)
            s1 = dot(kf[pl.ds(n1, tok), :], qm[nhd, pl.ds(n1, tok), :], NT)
            (sa, sb)[ns][pl.ds(n0, tok), :] = s0
            (sa, sb)[ns][pl.ds(n1, tok), tok:] = s1
            m0 = fold(s0, jnp.max)
            mm = jnp.concatenate([m0[:, :tok], jnp.maximum(m0[:, tok:], fold(s1, jnp.max))], axis=1)
        else:
            mm = zero8
        if cur is not None:
            ca, chd, cs = cur
            hs = slice(chd * HD, (chd + 1) * HD)
            c0 = pl.multiple_of(ca * blk, blk)
            c1 = pl.multiple_of(ca * blk + tok, tok)
            m = (ma, mb)[cs][...]
            p0 = jnp.exp((sa, sb)[cs][pl.ds(c0, tok), :] - m)
            p1 = jnp.exp((sa, sb)[cs][pl.ds(c1, tok), tok:] - m[:, tok:])
            l0 = fold(p0, jnp.sum)
            ll = jnp.concatenate([l0[:, :tok], l0[:, tok:] + fold(p1, jnp.sum)], axis=1)
            a0 = dot(vt[hs, pl.ds(c0, tok)], p0.astype(jnp.bfloat16), NN)
            a1 = dot(vt[hs, pl.ds(c1, tok)], p1.astype(jnp.bfloat16), NN)
            acc[hs, :tok] = a0[:, :tok]
            acc[hs, tok:] = a0[:, tok:] + a1
        else:
            ll = zero8
        def score(b, mm):
            rows = pl.ds(pl.multiple_of(b * blk, blk), blk)
            s = dot(kf[rows, :], qm[nhd, ncols, :], NT)
            (sa, sb)[ns][rows, :] = s
            return jnp.maximum(mm, fold(s, jnp.max))
        def body(b, carry):
            mm, ll = carry
            if nxt is not None:
                mm = score(b, mm)
            if cur is not None:
                rows = pl.ds(pl.multiple_of(b * blk, blk), blk)
                p = jnp.exp((sa, sb)[cs][rows, :] - m)
                ll = ll + fold(p, jnp.sum)
                acc[hs, :] += dot(vt[hs, rows], p.astype(jnp.bfloat16), NN)
            return mm, ll
        trip = nxt[0] if cur is None else cur[0]
        mm, ll = lax.fori_loop(0, trip, body, (mm, ll))
        if grow and nxt is not None:
            mm = score(cur[0], mm)
        if nxt is not None:
            (ma, mb)[ns][...] = jnp.max(mm, axis=0, keepdims=True)
        if cur is not None:
            l = jnp.sum(ll, axis=0, keepdims=True)
            ot = acc[hs, :] / l
            acc[hs, :] = ot
            cols = pl.ds(c0, blk)
            ot_ref[hs, cols] = ot
            lse_ref[chd:chd + 1, cols] = m + jnp.log(l)

    def finish(a):
        o = acc[...].T.astype(jnp.bfloat16)
        for j in range(2):
            f = 2 * a + j
            o_ref[f // fl, :, f % fl] = o[j * tok:(j + 1) * tok].reshape(nr, pt, lw)
        done(a)

    def q_block(a, par, last):
        for h in range(nh):
            cur, ns = (a, h, (par + h) % 2), (par + h + 1) % 2
            if h + 1 < nh:
                stage(cur, (a, h + 1, ns), False)
            else:
                stage(cur, None if last else (a + 1, 0, ns), True)
        finish(a)
    stage(None, (0, 0, 0), False)
    span = 2 if nh % 2 else 1
    def step(i, _):
        for n in range(span):
            q_block(i * span + n, n % 2, False)
        return 0
    lax.fori_loop(0, nblk // span - 1, step, 0)
    for n in range(span):
        q_block(nblk - span + n, n % 2, n == span - 1)

def rotate_back(t, cos, sin, nh):
    out = []
    for h in range(nh):
        a = t[h * HD:h * HD + HD // 2]
        b = t[h * HD + HD // 2:(h + 1) * HD]
        out += [a * cos + b * sin, b * cos - a * sin]
    return jnp.concatenate(out, axis=0)

def flash_backward(x_ref, go_ref, ot_ref, lse_ref, cos_ref, sin_ref, gq_ref, gkv_ref, qm, dom, kf, vf, kt, delta, dqt, dka, dva, done_q, done_kv):
    nf, nr, fl, pt, width = x_ref.shape
    lw = width // 3
    nh = lw // HD
    tok = nr * pt
    frames = nf * fl
    blk = 2 * tok
    def load(f, _):
        part = x_ref[f // fl, :, f % fl].reshape(tok, width)
        go = go_ref[f // fl, :, f % fl].reshape(tok, lw)
        rows = pl.ds(pl.multiple_of(f * tok, tok), tok)
        q = part[:, :lw] * jnp.bfloat16(HD ** -0.5)
        k = part[:, lw:2 * lw]
        prod = go.T.astype(jnp.float32) * ot_ref[:, rows]
        for h in range(nh):
            qm[h, rows, :] = head_mask(q, h, nh)
            dom[h, rows, :] = head_mask(go, h, nh)
            delta[h:h + 1, rows] = jnp.sum(prod[h * HD:(h + 1) * HD], axis=0, keepdims=True)
        kf[rows, :] = k
        kt[:, rows] = k.T
        vf[rows, :] = part[:, 2 * lw:]
        dqt[:, rows] = jnp.zeros((lw, tok), jnp.float32)
        return 0
    lax.fori_loop(0, frames, load, 0)

    def work(k0, kn, q0, qn):
        rows, cols = pl.ds(k0, kn), pl.ds(q0, qn)
        k, v = kf[rows, :], vf[rows, :]
        s = [dot(k, qm[h, cols, :], NT) for h in range(nh)]
        g = [dot(v, dom[h, cols, :], NT) for h in range(nh)]
        dv, dk = [], []
        for h in range(nh):
            hs = slice(h * HD, (h + 1) * HD)
            p = jnp.exp(s[h] - lse_ref[h:h + 1, cols])
            ds = (p * (g[h] - delta[h:h + 1, cols])).astype(jnp.bfloat16)
            dv.append(dot(p.astype(jnp.bfloat16), dom[h, cols, :], NN))
            dk.append(dot(ds, qm[h, cols, :], NN))
            dqt[hs, cols] += dot(kt[hs, rows], ds, NN)
        return sum(dk[1:], dk[0]), sum(dv[1:], dv[0])

    count = frames // 2
    half = count // 2

    def store_q(a):
        cols = pl.ds(pl.multiple_of(a * blk, blk), blk)
        dq = rotate_back(dqt[:, cols] * HD ** -0.5, cos_ref[:, cols], sin_ref[:, cols], nh).T.astype(jnp.bfloat16)
        for j in range(2):
            f = 2 * a + j
            gq_ref[f // fl, :, f % fl] = dq[j * tok:(j + 1) * tok].reshape(nr, pt, lw)
        done_q(a)

    def k_block(t, _):
        b = lax.rem(t + half, count)
        k0 = pl.multiple_of(b * blk, blk)
        k1 = pl.multiple_of(b * blk + tok, tok)
        dk, dv = work(k0, tok, k0, blk)
        dka[:tok, :] = dk
        dva[:tok, :] = dv
        dk, dv = work(k1, tok, k1, tok)
        dka[tok:, :] = dk
        dva[tok:, :] = dv
        @pl.when(b < half)
        def _():
            store_q(b)
        def q_block(a, _):
            dk, dv = work(k0, blk, pl.multiple_of(a * blk, blk), blk)
            dka[...] += dk
            dva[...] += dv
            @pl.when(t == count - 1)
            def _():
                store_q(a)
            return 0
        lax.fori_loop(b + 1, count, q_block, 0)
        cols = pl.ds(k0, blk)
        dk = rotate_back(dka[...].T, cos_ref[:, cols], sin_ref[:, cols], nh).T.astype(jnp.bfloat16)
        dv = dva[...].astype(jnp.bfloat16)
        for j in range(2):
            f = 2 * b + j
            for n, part in enumerate((dk, dv)):
                gkv_ref[f // fl, :, f % fl, :, n * lw:(n + 1) * lw] = part[j * tok:(j + 1) * tok].reshape(nr, pt, lw)
        done_kv(t, b)
        return 0
    lax.fori_loop(0, count, k_block, 0)

ALL = ("clip", "frame", "row")
B16, F32 = jnp.bfloat16, jnp.float32


def rope_angles(frame_pos, patch_pos, grid):
    pair_index = jnp.arange(32)
    is_time = pair_index < 8
    is_height = (pair_index >= 8) & (pair_index < 20)
    exponent = jnp.where(
        is_time,
        pair_index / 8.0,
        jnp.where(is_height, (pair_index - 8) / 12.0, (pair_index - 20) / 12.0),
    ).astype(F32)
    frequency = jnp.power(F32(10000.0), -exponent)
    position = jnp.where(
        is_time[None, :],
        frame_pos[:, None],
        jnp.where(is_height[None, :], (patch_pos // grid)[:, None], (patch_pos % grid)[:, None]),
    ).astype(F32)
    angle = position * frequency[None, :]
    return (jnp.cos(angle), jnp.sin(angle))


def rotate_lanes(t, cos, sin):
    lane = lax.broadcasted_iota(jnp.int32, t.shape, 1)
    half = HD // 2
    lanes = t.shape[1]
    low = (lane % HD) < half
    part = jnp.where(low, pltpu.roll(t, lanes - half, 1), pltpu.roll(t, half, 1))
    return t * cos + part * sin


def stats(v):
    mean = jnp.mean(v, axis=1, keepdims=True)
    centre = v - mean
    inverse = lax.rsqrt(jnp.mean(centre * centre, axis=1, keepdims=True) + 1e-06)
    return centre * inverse, inverse


def qkv_kernel(x_ref, mod_ref, w_hbm, b_ref, cos_ref, sin_ref, o_ref, h_ref, w, sem):
    count, width = x_ref.shape
    hg, _, w3 = o_ref.shape
    lw = w3 // 3
    frames = mod_ref.shape[0]
    pt = count // frames
    copies = [pltpu.make_async_copy(w_hbm.at[:, pl.ds(j * width, width)], w.at[j], sem.at[j]) for j in range(3)]
    @pl.when(pl.program_id(0) == 0)
    def _():
        for c in copies:
            c.start()
    def one(f, _):
        rows = pl.ds(pl.multiple_of(f * pt, pt), pt)
        n, _inv = stats(x_ref[rows, :].astype(F32))
        h_ref[rows, :] = (n * (1.0 + mod_ref[f, 1:2, :]) + mod_ref[f, 0:1, :]).astype(B16)
        return 0
    lax.fori_loop(0, frames, one, 0)
    step = max(256, lw)
    for j in range(3):
        @pl.when(pl.program_id(0) == 0)
        def _():
            copies[j].wait()
        for a in range(0, width, step):
            t = dot(h_ref[...], w[j, :, a:a + step], NN) + b_ref[0:1, j * width + a:j * width + a + step]
            for g in range(step // lw):
                v = t[:, g * lw:(g + 1) * lw]
                if j < 2:
                    v = rotate_lanes(v, cos_ref[...], sin_ref[...])
                o_ref[a // lw + g, :, j * lw:(j + 1) * lw] = v.astype(B16)


def qkv_forward(x, mods, w, b, cos, sin, hg, lw):
    clips, count, width = x.shape
    frames = mods.shape[1]
    one = lambda *shape: pl.BlockSpec((None,) + shape, lambda c: (c,) + (0,) * len(shape))
    same = lambda *shape: pl.BlockSpec(shape, lambda c: (0,) * len(shape))
    return pl.pallas_call(
        qkv_kernel,
        grid=(clips,),
        in_specs=[one(count, width), one(frames, 6, width), pl.BlockSpec(memory_space=pl.ANY), same(1, 3 * width), same(count, lw), same(count, lw)],
        out_specs=(one(hg, count, 3 * lw), one(count, width)),
        out_shape=(jax.ShapeDtypeStruct((clips, hg, count, 3 * lw), B16), jax.ShapeDtypeStruct((clips, count, width), B16)),
        scratch_shapes=[pltpu.VMEM((3, width, width), B16), pltpu.SemaphoreType.DMA((3,))],
        compiler_params=pltpu.CompilerParams(vmem_limit_bytes=48 << 20, dimension_semantics=("arbitrary",)),
        cost_estimate=pl.CostEstimate(flops=6 * clips * count * width * width, bytes_accessed=clips * 10 * count * width + 6 * width * width, transcendentals=0),
        name="qkv",
    )(x, mods, w, b, cos, sin)


TN = (((0,), (0,)), ((), ()))


MESH = pl.DeviceIdType.MESH


class Plane:
    def __init__(self):
        self.nf, self.nr = lax.axis_size("frame"), lax.axis_size("row")
        self.f, self.r = lax.axis_index("frame"), lax.axis_index("row")
        self.size = self.nf * self.nr
        self.me = self.f * self.nr + self.r

    def peer(self, k):
        p = lax.rem(self.me + k, self.size)
        return p, p // self.nr, lax.rem(p, self.nr)


def greet(plane, with_clips):
    barrier = pltpu.get_barrier_semaphore()
    count = plane.size - 1
    for k in range(1, plane.size):
        _, f, r = plane.peer(k)
        pl.semaphore_signal(barrier, inc=1, device_id={"frame": f, "row": r}, device_id_type=MESH)
    if with_clips:
        nc = lax.axis_size("clip")
        c = lax.axis_index("clip")
        for k in range(1, nc):
            pl.semaphore_signal(barrier, inc=1, device_id={"clip": lax.rem(c + k, nc)}, device_id_type=MESH)
        count += nc - 1
    pl.semaphore_wait(barrier, count)


def remote(src, dst, send, recv, device):
    return pltpu.make_async_remote_copy(src_ref=src, dst_ref=dst, send_sem=send, recv_sem=recv, device_id=device, device_id_type=MESH)


def send_blocks(plane, i, a, buf, out, send, recv, local):
    fl = buf.shape[3]
    fh, at = 2 * a // fl, lax.rem(2 * a, fl)
    for r in range(plane.nr):
        src = buf.at[i, fh, r, pl.ds(at, 2)]
        dst = out.at[i, plane.me, pl.ds(at, 2)]
        own = jnp.logical_and(fh == plane.f, r == plane.r)
        dest = fh * plane.nr + r
        k = lax.rem(dest - plane.me + plane.size, plane.size)
        @pl.when(own)
        def _():
            pltpu.make_async_copy(src, dst, local.at[i]).start()
        @pl.when(jnp.logical_not(own))
        def _():
            remote(src, dst, send.at[i, k], recv.at[i, k], {"frame": fh, "row": r}).start()


def wait_blocks(plane, calls, buf, out, send, recv, local):
    for i in range(calls):
        pltpu.make_async_copy(buf.at[i, plane.f, plane.r], out.at[i, plane.me], local.at[i]).wait()
        for k in range(1, plane.size):
            p, f, r = plane.peer(k)
            copy = remote(buf.at[i, f, r], out.at[i, plane.me], send.at[i, k], recv.at[i, k], {"frame": f, "row": r})
            copy.wait_send()
            copy.wait_recv()


def fwd_all_kernel(*refs, calls):
    plane = Plane()
    x_send, x_out, a_out, ot_ref, lse_ref = refs[:5]
    xv, ob, qm, kf, vt, sa, sb, acc, ma, mb, xs, xr, xl, os, orr, ol, save = refs[5:]
    greet(plane, False)
    for i in range(calls):
        pltpu.make_async_copy(x_send.at[i, plane.me], xv.at[i, plane.f, plane.r], xl.at[i]).start()
        for k in range(1, plane.size):
            p, f, r = plane.peer(k)
            remote(x_send.at[i, p], xv.at[i, plane.f, plane.r], xs.at[i, k], xr.at[i, k], {"frame": f, "row": r}).start()

    def arrive(i, what):
        for k in range(1, plane.size):
            p, f, r = plane.peer(k)
            copy = remote(x_send.at[i, p], xv.at[i, plane.f, plane.r], xs.at[i, k], xr.at[i, k], {"frame": f, "row": r})
            copy.wait_recv() if what else copy.wait_send()

    def call(i, _):
        pltpu.make_async_copy(x_send.at[i, plane.me], xv.at[i, plane.f, plane.r], xl.at[i]).wait()
        arrive(i, True)
        pltpu.make_async_copy(xv.at[i], x_out.at[i], save.at[i]).start()
        flash_forward(xv.at[i], ob.at[i], ot_ref.at[i], lse_ref.at[i], qm, kf, vt, sa, sb, acc, ma, mb,
                      lambda a: send_blocks(plane, i, a, ob, a_out, os, orr, ol))
        return 0
    lax.fori_loop(0, calls, call, 0)
    for i in range(calls):
        arrive(i, False)
        pltpu.make_async_copy(xv.at[i], x_out.at[i], save.at[i]).wait()
    wait_blocks(plane, calls, ob, a_out, os, orr, ol)


def attention_forward(sends, lead, lw):
    calls = sends.shape[0]
    nf, nr, fl, pt = lead
    group = nf * nr
    nh = lw // HD
    seq = nf * nr * fl * pt
    blk = 2 * nr * pt
    hbm, vmem = pl.BlockSpec(memory_space=pl.ANY), pl.BlockSpec(memory_space=pltpu.VMEM)
    s, v, dma = jax.ShapeDtypeStruct, pltpu.VMEM, pltpu.SemaphoreType.DMA
    return pl.pallas_call(
        functools.partial(fwd_all_kernel, calls=calls),
        in_specs=[hbm],
        out_specs=(hbm, hbm, vmem, vmem),
        out_shape=(s((calls,) + lead + (3 * lw,), B16), s((calls, group, fl, pt, lw), B16),
                   s((calls, lw, seq), F32), s((calls, nh, seq), F32)),
        scratch_shapes=[v((calls,) + lead + (3 * lw,), B16), v((calls,) + lead + (lw,), B16), v((nh, seq, lw), B16),
                        v((seq, lw), B16), v((lw, seq), B16), v((seq, blk), F32), v((seq, blk), F32), v((lw, blk), F32), v((1, blk), F32), v((1, blk), F32),
                        dma((calls, group)), dma((calls, group)), dma((calls,)), dma((calls, group)), dma((calls, group)),
                        dma((calls,)), dma((calls,))],
        compiler_params=pltpu.CompilerParams(vmem_limit_bytes=56 << 20, collective_id=0, has_side_effects=True),
        cost_estimate=pl.CostEstimate(flops=calls * seq * seq * lw * 2, bytes_accessed=calls * seq * lw * 24, transcendentals=calls * seq * seq * nh // 2),
        name="attention_forward",
    )(sends)


class Sum:
    def __init__(self, plane, plane_first, part, out, cols, out_cols, v1, s1, v2, s2, v3, sems):
        self.plane, self.plane_first, self.part, self.out = plane, plane_first, part, out
        self.cols, self.out_cols = cols, out_cols
        self.v1, self.s1, self.v2, self.s2, self.v3, self.sems = v1, s1, v2, s2, v3, sems
        self.bit = lax.rem(plane.r, 2)

    def place(self, stage):
        plane = self.plane
        if (stage == 1) == self.plane_first:
            half = plane.nr // 2
            return plane.nf * half, plane.f * half + plane.r // 2, lambda p: {"frame": p // half, "row": lax.rem(p, half) * 2 + self.bit}
        return lax.axis_size("clip"), lax.axis_index("clip"), lambda p: {"clip": p}

    def block(self, stage, p):
        if stage == 2:
            return self.s1.at[p]
        cols = pl.ds(*self.cols)
        return self.part.at[:, p, :, cols] if self.plane_first else self.part.at[p, :, :, cols]

    def copies(self, stage):
        count, me, device = self.place(stage)
        dst = self.v1 if stage == 1 else self.v2
        base = 0 if stage == 1 else self.v1.shape[0]
        out = []
        for k in range(1, count):
            p = lax.rem(me + k, count)
            out.append(remote(self.block(stage, p), dst.at[me], self.sems.at[0, base + k], self.sems.at[1, base + k], device(p)))
        return out, pltpu.make_async_copy(self.block(stage, me), dst.at[me], self.sems.at[0, base])

    def fetch(self):
        return pltpu.make_async_copy(self.part, self.v1, self.sems.at[0, 0])

    def start(self, stage):
        copies, own = self.copies(stage)
        for c in copies:
            c.start()
        own.start()

    def wait(self, stage):
        copies, own = self.copies(stage)
        for c in copies:
            c.wait()
        own.wait()

    def middle(self):
        def one(j, _):
            total = self.v1[0, j].astype(F32)
            for c in range(1, self.v1.shape[0]):
                total = total + self.v1[c, j].astype(F32)
            self.s1[j] = total.astype(B16)
            return 0
        lax.fori_loop(0, self.s1.shape[0], one, 0)
        self.start(2)

    def third(self):
        return remote(self.s2.at[1 - self.bit], self.v3, self.sems.at[0, self.sems.shape[1] - 1], self.sems.at[1, self.sems.shape[1] - 1],
                      {"row": self.plane.r + 1 - 2 * self.bit})

    def columns(self, b):
        return pl.ds(b * self.out_cols + self.at, self.cols[1])

    def last(self):
        total = self.v2[0].astype(F32)
        for c in range(1, self.v2.shape[0]):
            total = total + self.v2[c].astype(F32)
        per = self.s2.shape[1]
        self.s2[0] = total[:per]
        self.s2[1] = total[per:]
        self.third().start()
        for b in range(2):
            @pl.when(self.bit == b)
            def _():
                self.out[:, self.columns(b)] = self.s2[b]

    def close(self):
        self.third().wait()
        for b in range(2):
            @pl.when(self.bit == b)
            def _():
                self.out[:, self.columns(1 - b)] = self.v3[...]


def sum_plan(parts, orders):
    scratch, outs, jobs = [], {}, []
    for n, (part, (o, half, arrived, pieces)) in enumerate(zip(parts, orders)):
        two = part.shape[2]
        outs[o] = jax.ShapeDtypeStruct((two // 2, 2 * half), F32)
        for plane_first, first, cols, at in pieces:
            n1, n2 = part.shape[:2]
            if plane_first and not arrived:
                n1, n2 = n2, n1
            scratch += [pltpu.VMEM((n1, n2, two, cols), B16), pltpu.VMEM((n2, two, cols), B16), pltpu.VMEM((n2, two, cols), B16),
                        pltpu.VMEM((2, two // 2, cols), F32), pltpu.VMEM((two // 2, cols), F32),
                        pltpu.SemaphoreType.DMA((2, n1 + n2 + 1))]
            jobs.append((n, o, half, arrived, plane_first, first, cols, at))
    return scratch, [outs[o] for o in sorted(outs)], jobs


def make_sums(plane, jobs, parts, outs, scratch):
    sums = []
    for i, (n, o, half, arrived, plane_first, first, cols, at) in enumerate(jobs):
        s = Sum(plane, plane_first, parts[n], outs[o], (first, cols), half, *scratch[6 * i:6 * i + 6])
        s.at, s.arrived = at, arrived
        sums.append(s)
    return sums


def bwd_all_kernel(*refs, calls, count, outputs, jobs):
    plane = Plane()
    x_in, go_in, ot_in, lse_ref, cos_ref, sin_ref = refs[:6]
    go_send = refs[6:5 + calls]
    at = 5 + calls
    parts = refs[at:at + count]
    at += count
    gq_out, gkv_out = refs[at:at + 2]
    outs = refs[at + 2:at + 2 + outputs]
    at += 2 + outputs
    xv, gov, otv, gqb, gkb, qm, dom, kf, vf, kt, delta, dqt, dka, dva, loads, gs, gr, gl, qs, qr, ql, xs, xr, xl = refs[at:at + 24]
    sums = make_sums(plane, jobs, parts, outs, refs[at + 24:])
    greet(plane, True)
    load = [pltpu.make_async_copy(go_in, gov.at[0], gl.at[0])]
    for i in range(calls):
        load += [pltpu.make_async_copy(x_in.at[i], xv.at[i], loads.at[0, i]), pltpu.make_async_copy(ot_in.at[i], otv.at[i], loads.at[1, i])]
    for c in load:
        c.start()
    def go_copy(i, k, src):
        p, f, r = plane.peer(k)
        return remote(src.at[p], gov.at[i, plane.f, plane.r], gs.at[i, k], gr.at[i, k], {"frame": f, "row": r})
    for i in range(1, calls):
        pltpu.make_async_copy(go_send[i - 1].at[plane.me], gov.at[i, plane.f, plane.r], gl.at[i]).start()
        for k in range(1, plane.size):
            go_copy(i, k, go_send[i - 1]).start()
    early = [s for s in sums if s.arrived]
    late = [s for s in sums if not s.arrived]
    for s in late:
        s.start(1)
    for s in early:
        s.fetch().start()

    def call(i, _):
        pltpu.make_async_copy(x_in.at[i], xv.at[i], loads.at[0, i]).wait()
        pltpu.make_async_copy(ot_in.at[i], otv.at[i], loads.at[1, i]).wait()
        if calls > 1:
            @pl.when(i > 0)
            def _():
                pltpu.make_async_copy(go_send[0].at[plane.me], gov.at[i, plane.f, plane.r], gl.at[i]).wait()
                for k in range(1, plane.size):
                    go_copy(i, k, go_send[0]).wait_recv()
        @pl.when(i == 0)
        def _():
            pltpu.make_async_copy(go_in, gov.at[0], gl.at[0]).wait()
        def done_q(a):
            send_blocks(plane, i, a, gqb, gq_out, qs, qr, ql)
        def done_kv(t, b):
            send_blocks(plane, i, b, gkb, gkv_out, xs, xr, xl)
            @pl.when(jnp.logical_and(i == 0, t == 0))
            def _():
                for s in early:
                    s.fetch().wait()
                    s.middle()
            @pl.when(jnp.logical_and(i == calls - 1, t == 4))
            def _():
                for s in early:
                    s.wait(2)
                    s.last()
                for s in late:
                    s.wait(1)
                    s.middle()
        flash_backward(xv.at[i], gov.at[i], otv.at[i], lse_ref.at[i], cos_ref, sin_ref, gqb.at[i], gkb.at[i],
                       qm, dom, kf, vf, kt, delta, dqt, dka, dva, done_q, done_kv)
        return 0
    lax.fori_loop(0, calls, call, 0)
    for i in range(1, calls):
        for k in range(1, plane.size):
            go_copy(i, k, go_send[i - 1]).wait_send()
    for s in late:
        s.wait(2)
        s.last()
    for s in sums:
        s.close()
    wait_blocks(plane, calls, gqb, gq_out, qs, qr, ql)
    wait_blocks(plane, calls, gkb, gkv_out, xs, xr, xl)


def attention_backward(x, go, go_sends, ot, lse, cos, sin, parts, orders):
    calls, nf, nr, fl, pt, w3 = x.shape
    lead = (nf, nr, fl, pt)
    lw = w3 // 3
    group = nf * nr
    nh = lw // HD
    seq = nf * nr * fl * pt
    blk = 2 * nr * pt
    hbm, vmem = pl.BlockSpec(memory_space=pl.ANY), pl.BlockSpec(memory_space=pltpu.VMEM)
    s, v, dma = jax.ShapeDtypeStruct, pltpu.VMEM, pltpu.SemaphoreType.DMA
    scratch, outs, jobs = sum_plan(parts, orders)
    return pl.pallas_call(
        functools.partial(bwd_all_kernel, calls=calls, count=len(parts), outputs=len(outs), jobs=jobs),
        in_specs=[hbm, hbm, hbm, vmem, vmem, vmem] + [hbm] * (len(go_sends) + len(parts)),
        out_specs=[hbm, hbm] + [vmem] * len(outs),
        out_shape=[s((calls, group, fl, pt, lw), B16), s((calls, group, fl, pt, 2 * lw), B16)] + outs,
        scratch_shapes=[v((calls,) + lead + (w3,), B16), v((calls,) + lead + (lw,), B16), v((calls, lw, seq), F32), v((calls,) + lead + (lw,), B16), v((calls,) + lead + (2 * lw,), B16),
                        v((nh, seq, lw), B16), v((nh, seq, lw), B16), v((seq, lw), B16), v((seq, lw), B16), v((lw, seq), B16),
                        v((nh, seq), F32), v((lw, seq), F32), v((blk, lw), F32), v((blk, lw), F32),
                        dma((2, calls)), dma((calls, group)), dma((calls, group)), dma((calls,)), dma((calls, group)), dma((calls, group)), dma((calls,)), dma((calls, group)), dma((calls, group)), dma((calls,))] + scratch,
        compiler_params=pltpu.CompilerParams(vmem_limit_bytes=61 << 20, collective_id=1, has_side_effects=True),
        cost_estimate=pl.CostEstimate(flops=calls * seq * seq * lw * 5, bytes_accessed=calls * seq * lw * 48, transcendentals=calls * seq * seq * nh // 2),
        name="attention_backward",
    )(x, go, ot, lse, cos, sin, *go_sends, *parts)


def mlp_kernel(a_ref, x_hbm, g_hbm, mod_ref, wo_ref, bo_ref, wu_ref, bu_ref, wd_ref, bd_ref,
               y_out, gm_out, ga_out, go_out, pd_out, ugot, vgot, po_out, sums_ref, du_ref, db_ref,
               g, an, branch, mixed, h, gd, down, gh, st, gav, sd, su, rd, ru, kd, ku, pd, pu, *sems, calls):
    io, od, pair, free, done, gs, gr, gl, oo, us, ur, vr = sems
    plane = Plane()
    nc, mc = lax.axis_size("clip"), lax.axis_index("clip")
    half_row = plane.nr // 2
    places, mp = plane.nf * half_row, plane.f * half_row + plane.r // 2
    at_place = lambda p: {"frame": p // half_row, "row": lax.rem(p, half_row) * 2 + bit}
    bit = lax.rem(plane.r, 2)
    clip_first = ugot.shape[3] // (wu_ref.shape[1] // 2)
    partner = {"row": plane.r + 1 - 2 * bit}
    clips, hg, count, lw = a_ref.shape
    width = an.shape[1]
    frames = mod_ref.shape[0]
    pt = clips * count // frames
    step, steps = pl.program_id(0), pl.num_programs(0)
    fc = wu_ref.shape[1]
    slots = rd.shape[0]
    hw, hf = width // 2, fc // 2

    def each(first, last, fn):
        def one(f, _):
            fn(f, pl.ds(pl.multiple_of(f * pt, pt), pt))
            return 0
        lax.fori_loop(first, last, one, 0)

    def split(value, size, send, keep):
        for b in range(2):
            @pl.when(bit == b)
            def _():
                send[...] = value[:, (1 - b) * size:(2 - b) * size].astype(B16)
                keep[...] = value[:, b * size:(b + 1) * size]

    @pl.when(step == 0)
    def _():
        loads = [pltpu.make_async_copy(x_hbm, h, io.at[0]), pltpu.make_async_copy(g_hbm, g.at[pl.ds(0, clips * count)], io.at[1])]
        for c in loads:
            c.start()
        greet(plane, True)
        for c in range(clips):
            for i in range(hg):
                an[c * count:(c + 1) * count, i * lw:(i + 1) * lw] = a_ref[c, i]
        branch[...] = dot(an[:clips * count, :], wo_ref[...], NN) + bo_ref[...]
        for c in loads:
            c.wait()
        def fn(f, rows):
            m = h[rows, :].astype(F32) + mod_ref[f, 2:3, :] * branch[rows, :]
            mean = jnp.mean(m, axis=1, keepdims=True)
            centre = m - mean
            inv = lax.rsqrt(jnp.mean(centre * centre, axis=1, keepdims=True) + 1e-06)
            mixed[rows, :] = m
            st[rows, :128] = jnp.broadcast_to(mean, (pt, 128))
            st[rows, 128:] = jnp.broadcast_to(inv, (pt, 128))
            h[rows, :] = (centre * inv * (1.0 + mod_ref[f, 4:5, :]) + mod_ref[f, 3:4, :]).astype(B16)
            gd[rows, :] = (g[rows, :].astype(F32) * mod_ref[f, 5:6, :]).astype(B16)
        each(0, frames, fn)
        down[...] = jnp.zeros_like(down)
        gh[...] = jnp.zeros_like(gh)

    c0 = (2.0 / 3.141592653589793) ** 0.5
    c1 = 0.044715
    wu, wd = wu_ref[...], wd_ref[...]
    wide, tall, bias = None, None, None
    for c in range(clips):
        rows = slice(c * count, (c + 1) * count)
        hr, gr_ = h[rows, :], gd[rows, :]
        pre = dot(hr, wu, NN) + bu_ref[...]
        gact = dot(gr_, wd, NT)
        sq = pre * pre
        u = jnp.tanh(pre * (c0 + (c0 * c1) * sq))
        half = 0.5 * (1.0 + u)
        act = (pre * half).astype(B16)
        slope = half + (0.5 * pre) * (1.0 - u * u) * (c0 + (3.0 * c0 * c1) * sq)
        gp = (gact * slope).astype(B16)
        down[rows, :] += dot(act, wd, NN)
        gh[rows, :] += dot(gp, wu, NT)
        d, t, b = dot(act, gr_, TN), dot(hr, gp, TN), jnp.sum(gp.astype(F32), axis=0, keepdims=True)
        wide = d if wide is None else wide + d
        tall = t if tall is None else tall + t
        bias = b if bias is None else bias + b
    du_ref[...] = bias
    now, slot = lax.rem(step, 2), lax.rem(step, slots)

    def swaps(j):
        n, s = lax.rem(j, 2), lax.rem(j, slots)
        return (remote(sd.at[n], rd.at[s], pair.at[0, n], pair.at[1, s], partner),
                remote(su.at[n], ru.at[s], pair.at[2, n], pair.at[3, s], partner))

    def onward(j, what):
        n = lax.rem(j, 2)
        def do(copy, sent):
            copy.start() if what == "start" else (copy.wait_send() if sent else copy.wait())
        do(pltpu.make_async_copy(pd.at[n], pd_out.at[pl.ds(pl.multiple_of(j * fc, fc), fc)], od.at[0, n]), False)
        @pl.when(j < clip_first)
        def _():
            cols = pl.ds(pl.multiple_of(j * hf, hf), hf)
            do(pltpu.make_async_copy(pu.at[n, mc], ugot.at[mc, :, :, cols], od.at[1, n]), False)
            for k in range(1, nc):
                c = lax.rem(mc + k, nc)
                do(remote(pu.at[n, c], ugot.at[mc, :, :, cols], us.at[n, k], ur.at[mc], {"clip": c}), True)
        @pl.when(j >= clip_first)
        def _():
            cols = pl.ds(pl.multiple_of((j - clip_first) * hf, hf), hf)
            do(pltpu.make_async_copy(pu.at[n, :, mp], vgot.at[mp, :, :, cols], od.at[1, n]), False)
            for k in range(1, places):
                p = lax.rem(mp + k, places)
                do(remote(pu.at[n, :, p], vgot.at[mp, :, :, cols], us.at[n, k], vr.at[mp], at_place(p)), True)

    def finish(j):
        n, s = lax.rem(j, 2), lax.rem(j, slots)
        @pl.when(j >= 2)
        def _():
            onward(j - 2, "wait")
        for c in swaps(j):
            c.wait_recv()
        pd[n] = (kd[n] + rd[s].astype(F32)).astype(B16)
        pu[n] = (ku[n] + ru[s].astype(F32)).astype(B16).reshape(pu.shape[1:])
        onward(j, "start")
        @pl.when(j + slots < steps)
        def _():
            pl.semaphore_signal(free, inc=1, device_id=partner, device_id_type=MESH)

    @pl.when(step >= 2)
    def _():
        for c in swaps(step - 2):
            c.wait_send()
    split(wide, hw, sd.at[now], kd.at[now])
    split(tall, hf, su.at[now], ku.at[now])
    @pl.when(step >= slots)
    def _():
        pl.semaphore_wait(free, 1)
    for c in swaps(step):
        c.start()
    @pl.when(step >= 1)
    def _():
        finish(step - 1)

    @pl.when(step == steps - 1)
    def _():
        db_ref[...] = jnp.zeros_like(db_ref)
        def fn(f, rows):
            gf = g[rows, :].astype(F32)
            d = down[rows, :] + bd_ref[...]
            m = mixed[rows, :]
            ghf = gh[rows, :]
            inv = st[rows, 128:129]
            n = (m - st[rows, 0:1]) * inv
            t = ghf * (1.0 + mod_ref[f, 4:5, :])
            back = t - jnp.mean(t, axis=1, keepdims=True) - n * jnp.mean(t * n, axis=1, keepdims=True)
            gm = gf + inv * back
            gbr = (gm * mod_ref[f, 2:3, :]).astype(B16)
            s = lambda v: jnp.sum(v, axis=0, keepdims=True)
            sums_ref[f] = jnp.concatenate([s(gm * branch[rows, :]), s(ghf), s(ghf * n), s(gf * d)], axis=0)
            db_ref[...] += jnp.concatenate([s(gbr.astype(F32)), s(gd[rows, :].astype(F32))], axis=0)
            mixed[rows, :] = gm
            h[rows, :] = gbr
            gd[rows, :] = (m + mod_ref[f, 5:6, :] * d).astype(B16)
        group = plane.size
        per_call = clips // calls
        def go_copies():
            out = []
            for k in range(1, group):
                p, f, r = plane.peer(k)
                out.append(remote(gav.at[p], go_out.at[plane.f, plane.r], gs.at[k], gr.at[k], {"frame": f, "row": r}))
            return out, pltpu.make_async_copy(gav.at[plane.me], go_out.at[plane.f, plane.r], gl)
        def back_out(c):
            each(c * frames // clips, (c + 1) * frames // clips, fn)
            ga = dot(h[c * count:(c + 1) * count, :], wo_ref[...], NT).astype(B16)
            for i in range(hg):
                gav[c * hg + i] = ga[:, i * lw:(i + 1) * lw]
        for c in range(per_call):
            back_out(c)
        copies, own = go_copies()
        for c in copies:
            c.start()
        own.start()
        for c in range(per_call, clips):
            back_out(c)
        outs = [pltpu.make_async_copy(gd, y_out, oo.at[0]), pltpu.make_async_copy(mixed, gm_out, oo.at[1])]
        if calls > 1:
            outs.append(pltpu.make_async_copy(gav.at[pl.ds(group, (calls - 1) * group)], ga_out, oo.at[2]))
        for c in outs:
            c.start()
        finish(step)
        pl.semaphore_signal(done, inc=1, device_id=partner, device_id_type=MESH)
        wide_out = dot(an[:clips * count, :], h[...], TN)
        for b in range(2):
            @pl.when(bit == b)
            def _():
                an[:width, :hw] = wide_out[:, (1 - b) * hw:(2 - b) * hw].astype(B16)
                down[:width, :hw] = wide_out[:, b * hw:(b + 1) * hw]
        pl.semaphore_wait(done, 1)
        ro = g.at[pl.ds(0, width), pl.ds(0, hw)]
        last = remote(an.at[pl.ds(0, width), pl.ds(0, hw)], ro, pair.at[0, 2], pair.at[1, slots], partner)
        last.start()
        last.wait()
        an[:width, hw:] = (down[:width, :hw] + g[:width, :hw].astype(F32)).astype(B16)
        outs.append(pltpu.make_async_copy(an.at[pl.ds(0, width), pl.ds(hw, hw)], po_out, oo.at[3]))
        outs[-1].start()
        for c in copies:
            c.wait()
        own.wait()
        for c in swaps(step - 1) + swaps(step):
            c.wait_send()
        onward(step - 1, "wait")
        onward(step, "wait")
        for k in range(1, places):
            p = lax.rem(mp + k, places)
            remote(vgot.at[p], vgot.at[p], us.at[0, 0], vr.at[p], at_place(p)).wait_recv()
        for k in range(1, nc):
            c = lax.rem(mc + k, nc)
            remote(ugot.at[c], ugot.at[c], us.at[0, 0], ur.at[c], {"clip": c}).wait_recv()
        for c in outs:
            c.wait()


def mlp(attn, x, g, mods, w_out, b_out, w_up, b_up, w_down, b_down, calls, lead):
    clips, hg, count, lw = attn.shape
    rows, width = x.shape
    ff = w_up.shape[1]
    frames = mods.shape[0]
    fc = min(512, ff)
    hw, hf = width // 2, fc // 2
    nf, nr = lead[:2]
    group = nf * nr
    slots = 3
    nc = lax.axis_size("clip")
    places, steps = group // 2, ff // fc
    clip_first = max(1, steps // 4)
    two_u = width // (nc * places)
    tall = max(rows, width)
    whole = lambda *shape: pl.BlockSpec(shape, lambda j: (0,) * len(shape), pipeline_mode=pl.Buffered(1))
    keep = lambda *shape: pl.BlockSpec(shape, lambda j: (0,) * len(shape))
    hbm = pl.BlockSpec(memory_space=pl.ANY)
    s, v, dma = jax.ShapeDtypeStruct, pltpu.VMEM, pltpu.SemaphoreType.DMA
    return pl.pallas_call(
        functools.partial(mlp_kernel, calls=calls),
        grid=(ff // fc,),
        in_specs=[whole(clips, hg, count, lw), hbm, hbm, whole(frames, 6, width), whole(width, width), whole(1, width),
                  pl.BlockSpec((width, fc), lambda j: (0, j)), pl.BlockSpec((1, fc), lambda j: (0, j)),
                  pl.BlockSpec((fc, width), lambda j: (j, 0)), whole(1, width)],
        out_specs=[hbm] * 8 + [keep(frames, 4, width), pl.BlockSpec((1, fc), lambda j: (0, j)), keep(2, width)],
        out_shape=[s((rows, width), B16), s((rows, width), F32), s((max(1, calls - 1) * group, count, lw), B16),
                   s((nf, nr, count, lw), B16), s((ff, hw), B16), s((nc, places, two_u, clip_first * hf), B16), s((places, nc, two_u, (steps - clip_first) * hf), B16), s((width, hw), B16),
                   s((frames, 4, width), F32), s((1, ff), F32), s((2, width), F32)],
        scratch_shapes=[v((tall, width), B16), v((tall, width), B16), v((rows, width), F32), v((rows, width), F32),
                        v((rows, width), B16), v((rows, width), B16), v((tall, width), F32), v((rows, width), F32), v((rows, 256), F32),
                        v((clips * hg, count, lw), B16), v((2, fc, hw), B16), v((2, width, hf), B16), v((slots, fc, hw), B16),
                        v((slots, width, hf), B16), v((2, fc, hw), F32), v((2, width, hf), F32), v((2, fc, hw), B16), v((2, nc, places, two_u, hf), B16),
                        dma((2,)), dma((2, 2)), dma((4, slots + 1)), pltpu.SemaphoreType.REGULAR, pltpu.SemaphoreType.REGULAR,
                        dma((group,)), dma((group,)), dma, dma((4,)), dma((2, max(places, nc))), dma((nc,)), dma((places,))],
        compiler_params=pltpu.CompilerParams(vmem_limit_bytes=63 << 20, dimension_semantics=("arbitrary",), collective_id=3, has_side_effects=True),
        cost_estimate=pl.CostEstimate(flops=2 * rows * width * (3 * width + 6 * ff), bytes_accessed=8 * width * ff + 20 * rows * width, transcendentals=rows * ff),
        name="mlp",
    )(attn, x, g, mods, w_out, b_out, w_up, b_up, w_down, b_down)


def tail_kernel(gq_hbm, gkv_hbm, h_hbm, w_hbm, x_hbm, gm_hbm, mod_ref, clean_ref, sums2_ref, vec_ref,
                o_out, gw_ref, noise_ref, vec_out,
                gq, gkv, h, w, x, gm, full, gh, send, got, part, s1s, dbq, nsend, nrecv, vsend, v1, vmid, v2, io, pair, nsem, vsem, oo, *scratch, jobs):
    plane = Plane()
    clips, hg, count, lw = gq_hbm.shape
    w3 = 3 * lw
    width = w.shape[0]
    frames = mod_ref.shape[0] // clips
    pt = count // frames
    nc, nf, nr = lax.axis_size("clip"), plane.nf, plane.nr
    group = plane.size
    bit = lax.rem(plane.r, 2)
    partner = {"row": plane.r + 1 - 2 * bit}
    packed = max(1, 128 * 3 // w3)
    blocks = hg // 2 // packed
    bw = packed * w3
    loads = [pltpu.make_async_copy(gq_hbm, gq, io.at[0]), pltpu.make_async_copy(gkv_hbm, gkv, io.at[5]), pltpu.make_async_copy(h_hbm, h, io.at[1]),
             pltpu.make_async_copy(w_hbm, w, io.at[2]), pltpu.make_async_copy(x_hbm, x, io.at[3]), pltpu.make_async_copy(gm_hbm, gm, io.at[4])]
    for c in loads:
        c.start()
    sums = make_sums(plane, jobs, [part], [gw_ref], scratch)
    greet(plane, True)
    for c in loads[:3]:
        c.wait()

    def outer(j):
        total = None
        for c in range(clips):
            b = jnp.concatenate([v[c, j * packed + i] for i in range(packed) for v in (gq, gkv)], axis=1)
            t = dot(h[c], b, TN)
            total = t if total is None else total + t
        return total

    def swap(j):
        return remote(send.at[j], got.at[j], pair.at[0, j], pair.at[1, j], partner)
    other = 1 - bit
    for j in range(blocks):
        send[j] = outer(other * blocks + j).astype(B16)
        swap(j).start()
    for s in sums:
        first, cols = s.cols
        j = first // bw
        total = outer(bit * blocks + j)
        swap(j).wait_recv()
        total = (total + got[j].astype(F32)).astype(B16)
        part[:, :, :, first:first + cols] = total.reshape(part.shape[:3] + (cols,))
        s.start(1)

    for c in loads[3:]:
        c.wait()
    dbq[...] = jnp.zeros_like(dbq)
    for c in range(clips):
        for g in range(hg):
            full[:, g * lw:(g + 1) * lw] = gq[c, g]
            for j in range(2):
                full[:, (j + 1) * width + g * lw:(j + 1) * width + (g + 1) * lw] = gkv[c, g, :, j * lw:(j + 1) * lw]
        gh[...] = dot(full[...], w[...], NT)
        dbq[...] += jnp.sum(full[...].astype(F32), axis=0, keepdims=True)
        def one(f, _):
            rows = pl.ds(pl.multiple_of(f * pt, pt), pt)
            cf = c * frames + f
            n, inv = stats(x[c, rows, :].astype(F32))
            ghf = gh[rows, :]
            t = ghf * (1.0 + mod_ref[cf, 1:2, :])
            back = t - jnp.mean(t, axis=1, keepdims=True) - n * jnp.mean(t * n, axis=1, keepdims=True)
            gm[c, rows, :] = gm[c, rows, :] + inv * back
            s = lambda v: jnp.sum(v, axis=0, keepdims=True)
            s1s[cf, 0:2, :] = jnp.concatenate([s(ghf), s(ghf * n)], axis=0)
            s1s[cf, 2:6, :] = sums2_ref[cf]
            return 0
        lax.fori_loop(0, frames, one, 0)
        pltpu.make_async_copy(gm.at[c], o_out.at[c], oo.at[c]).start()
        for s in (sums[1:2] if c < clips - 1 else sums[2 if clips > 1 else 1:3]):
            s.wait(1)
            s.middle()

    quarter = width // nr
    vsend[...] = jnp.zeros_like(vsend)
    def gather(cf, total):
        both = s1s[cf, 0:6, :]
        keep = clean_ref[cf]
        noise = jnp.where(keep > 0.5, jnp.zeros_like(both), both)
        for q in range(nr):
            nsend[q, cf] = noise[:, q * quarter:(q + 1) * quarter].astype(B16)
        return total + (both - noise)
    clean_sum = lax.fori_loop(0, clips * frames, gather, jnp.zeros((6, width), F32))
    def ncopies():
        out = []
        for k in range(1, nr):
            q = lax.rem(plane.r + k, nr)
            out.append(remote(nsend.at[q], nrecv.at[plane.r], nsem.at[0, k], nsem.at[1, k], {"row": q}))
        return out
    for c in ncopies():
        c.start()
    vsend[:6, :] = clean_sum
    vsend[6:9, :] = jnp.concatenate([dbq[:, j * width:(j + 1) * width] for j in range(3)], axis=0)
    vsend[9:9 + vec_ref.shape[0], :] = vec_ref[...]
    def vcopies(stage):
        out = []
        if stage == 1:
            for k in range(1, group):
                p, f, r = plane.peer(k)
                out.append(remote(vsend, v1.at[plane.me], vsem.at[0, k], vsem.at[1, k], {"frame": f, "row": r}))
        else:
            c = lax.axis_index("clip")
            for k in range(1, nc):
                out.append(remote(vmid, v2.at[c], vsem.at[0, group + k], vsem.at[1, group + k], {"clip": lax.rem(c + k, nc)}))
        return out
    for c in vcopies(1):
        c.start()
    for s in sums[:1] + sums[3:]:
        s.wait(1)
        s.middle()
    for c in vcopies(1):
        c.wait()
    total = vsend[...]
    for k in range(1, group):
        p, _, _ = plane.peer(k)
        total = total + v1[p]
    vmid[...] = total
    for c in vcopies(2):
        c.start()
    for c in ncopies():
        c.wait()
    def add_noise(cf, _):
        total = nsend[plane.r, cf].astype(F32)
        for k in range(1, nr):
            total = total + nrecv[lax.rem(plane.r + k, nr), cf].astype(F32)
        noise_ref[cf] = total
        return 0
    lax.fori_loop(0, clips * frames, add_noise, 0)
    for s in sums:
        s.wait(2)
        s.last()
    for c in vcopies(2):
        c.wait()
    total = vmid[...]
    for k in range(1, nc):
        total = total + v2[lax.rem(lax.axis_index("clip") + k, nc)]
    vec_out[...] = total
    for s in sums:
        s.close()
    for j in range(blocks):
        swap(j).wait_send()
    for c in range(clips):
        pltpu.make_async_copy(gm.at[c], o_out.at[c], oo.at[c]).wait()


def tail(gq, gkv, h1, w_qkv, x, gmixed, mods, clean, sums2, vec):
    clips, hg, count, lw = gq.shape
    w3 = 3 * lw
    width = x.shape[2]
    nc, nf, nr = (lax.axis_size(a) for a in ALL)
    group = nf * nr
    frames = mods.shape[0]
    two = width // (nc * nf * nr // 2)
    packed = max(1, 128 * 3 // w3)
    blocks, bw = hg // 2 // packed, packed * w3
    vrows = -(-(9 + vec.shape[0]) // 8) * 8
    hbm, vmem = pl.BlockSpec(memory_space=pl.ANY), pl.BlockSpec(memory_space=pltpu.VMEM)
    s, v, dma = jax.ShapeDtypeStruct, pltpu.VMEM, pltpu.SemaphoreType.DMA
    shape = jax.ShapeDtypeStruct((nc, nf * nr // 2, two, blocks * bw), B16)
    order = [(False if j == 0 else True, j * bw, bw, j * bw) for j in range(blocks)]
    scratch, outs, jobs = sum_plan([shape], [(0, blocks * bw, False, order)])
    return pl.pallas_call(
        functools.partial(tail_kernel, jobs=jobs),
        in_specs=[hbm] * 6 + [vmem] * 4,
        out_specs=[hbm, vmem, vmem, vmem],
        out_shape=[s((clips, count, width), F32)] + outs + [s((frames, 6, width // nr), F32), s((vrows, width), F32)],
        scratch_shapes=[v((clips, hg, count, lw), B16), v((clips, hg, count, 2 * lw), B16), v((clips, count, width), B16), v((width, 3 * width), B16), v((clips, count, width), B16),
                        v((clips, count, width), F32), v((count, 3 * width), B16), v((count, width), F32), v((blocks, width, bw), B16),
                        v((blocks, width, bw), B16), v(shape.shape, B16), v((frames, 8, width), F32), v((1, 3 * width), F32),
                        v((nr, frames, 6, width // nr), B16), v((nr, frames, 6, width // nr), B16), v((vrows, width), F32), v((group, vrows, width), F32),
                        v((vrows, width), F32), v((nc, vrows, width), F32), dma((6,)), dma((2, blocks)), dma((2, nr)), dma((2, group + nc)), dma((clips,))] + scratch,
        compiler_params=pltpu.CompilerParams(vmem_limit_bytes=62 << 20, collective_id=2, has_side_effects=True),
        cost_estimate=pl.CostEstimate(flops=12 * clips * count * width * width, bytes_accessed=40 * clips * count * width, transcendentals=0),
        name="tail",
    )(gq, gkv, h1, w_qkv, x, gmixed, mods, clean, sums2, vec)


def on_device(tokens, context, noise_mod, clean_mod, w_qkv, b_qkv, w_out, b_out, w_up, b_up, w_down, b_down, cotangent):
    frames, patches, clips, width = tokens.shape
    count = frames * patches
    heads = width // HD
    nf, nr = lax.axis_size("frame"), lax.axis_size("row")
    group = nf * nr
    nh = max(1, heads // group)
    lw = nh * HD
    hg = heads // nh
    cs = group // hg
    calls = clips // cs
    grid = round((patches * nr) ** 0.5)
    fi, ri = lax.axis_index("frame"), lax.axis_index("row")

    is_clean = (fi * frames + jnp.arange(frames))[None, :] < context[:, None]
    mods = jnp.where(is_clean[:, :, None, None], clean_mod[None, None], noise_mod.transpose(1, 0, 2, 3))
    full = (clips, frames, patches, width)
    inputs = tokens.transpose(2, 0, 1, 3).reshape(clips, count, width)
    cots = cotangent.transpose(2, 0, 1, 3).reshape(clips, count, width)

    tok = jnp.arange(count)
    cos, sin = rope_angles(fi * frames + tok // patches, ri * patches + tok % patches, grid)
    cos_l = jnp.tile(jnp.concatenate([cos, cos], axis=1), (1, nh))
    sin_l = jnp.tile(jnp.concatenate([-sin, sin], axis=1), (1, nh))
    every = jnp.arange(nf * frames * nr * patches)
    cos_all, sin_all = rope_angles(every // (nr * patches), every % (nr * patches), grid)
    cos_t, sin_t = cos_all.T, sin_all.T
    row_of = lambda v: v.reshape(1, -1)

    lead = (nf, nr, frames, patches)
    sends, h1 = qkv_forward(inputs, mods, w_qkv, row_of(b_qkv), cos_l, sin_l, hg, lw)
    x, attn, ot, lse = attention_forward(sends.reshape(calls, group, frames, patches, 3 * lw), lead, lw)
    attn = attn.reshape(clips, hg, count, lw)

    rows = clips * count
    by_frame = mods.reshape(clips * frames, 6, width)
    y, gmixed, ga, go, part_down, got_up, got_up2, part_out, sums2, db_up, db_two = mlp(
        attn, inputs.reshape(rows, width), cots.reshape(rows, width), by_frame,
        w_out, row_of(b_out), w_up, row_of(b_up), w_down, row_of(b_down), calls, lead)
    go = go.reshape(lead + (lw,))
    go_sends = [v for v in ga.reshape((-1, group, frames, patches, lw))][:calls - 1]
    gmixed = gmixed.reshape(clips, count, width)

    nc = lax.axis_size("clip")
    places = group // 2
    first, second, hw = got_up.shape[3], got_up2.shape[3], width // 2
    as_blocks = lambda p: p.reshape(nc, places, p.shape[0] // (nc * places), p.shape[1])
    parts = [as_blocks(part_down), got_up, got_up2, as_blocks(part_out)]
    orders = [(0, hw, False, [(False, 0, hw // 2, 0), (True, hw // 2, hw // 2, hw // 2)]), (1, first + second, True, [(False, 0, first, 0)]),
              (1, first + second, True, [(True, 0, second, first)]), (2, hw, False, [(False, 0, hw, 0)])]
    gq, gkv, gw_down, gw_up, gw_out = attention_backward(x, go, go_sends, ot, lse, cos_t, sin_t, parts, orders)
    gq, gkv = gq.reshape(clips, hg, count, lw), gkv.reshape(clips, hg, count, 2 * lw)
    fc = min(512, w_up.shape[1])
    gw_up = gw_up.reshape(gw_up.shape[0], 2, -1, fc // 2).transpose(0, 2, 1, 3).reshape(gw_up.shape[0], -1)
    clean = jnp.broadcast_to(is_clean.reshape(-1, 1, 1), (clips * frames, 1, width)).astype(F32)
    vec = jnp.concatenate([db_up.reshape(-1, width), db_two], axis=0)
    gtokens, gw_qkv, noise, vec = tail(gq, gkv, h1, w_qkv, inputs, gmixed, by_frame, clean, sums2, vec)
    per = gw_qkv.shape[0]
    gw_qkv = gw_qkv.reshape(per, 2, hg // 2, 3, lw).transpose(0, 3, 1, 2, 4).reshape(per, 3 * width)
    grad_noise = noise.reshape(clips, frames, 6, -1).transpose(1, 0, 2, 3)
    total = lax.axis_size(ALL)
    place = lax.axis_index(ALL)
    def own(at, size):
        return lax.dynamic_slice_in_dim(vec[at:at + size].reshape(-1), place * (size * width // total), size * width // total)
    grad_clean = lax.dynamic_slice_in_dim(vec[:6], place * (width // total), width // total, 1)
    ff = w_up.shape[1] // width
    gb_qkv, gb_up, gb_out, gb_down = own(6, 3), own(9, ff), own(9 + ff, 1), own(10 + ff, 1)
    back = lambda v: v.reshape(full).transpose(1, 2, 0, 3)
    return (back(y), back(gtokens), grad_noise, grad_clean, gw_qkv, gb_qkv, gw_out, gb_out, gw_up, gb_up, gw_down, gb_down)


def solution(mesh):
    token = P("frame", "row", "clip", None)
    rows = P(ALL, None)
    return jax.shard_map(
        on_device,
        mesh=mesh,
        in_specs=(token, P("clip"), P("frame", "clip", None, None)) + (P(),) * 9 + (token,),
        out_specs=(token, token, P("frame", "clip", None, "row"), P(None, ALL), rows, P(ALL), rows, P(ALL), rows, P(ALL), rows, P(ALL)),
        check_vma=False,
    )
```

```python
import functools
import jax, jax.numpy as jnp
from jax import lax
from jax.experimental import pallas as pl
from jax.experimental.pallas import tpu as pltpu
from jax.sharding import PartitionSpec as P
HD = 64
NN = (((1,), (0,)), ((), ()))
NT = (((1,), (1,)), ((), ()))
def dot(a, b, dims):
    return lax.dot_general(a, b, dims, preferred_element_type=jnp.float32)

def head_mask(values, head, heads):
    if heads == 1:
        return values
    lane = lax.broadcasted_iota(jnp.int32, values.shape, 1)
    return jnp.where(lane // HD == head, values, jnp.zeros_like(values))


def flash_forward(x_ref, o_ref, ot_ref, lse_ref, qm, kf, vt, sa, sb, acc, ma, mb, done):
    nf, nr, fl, pt, width = x_ref.shape
    lw = width // 3
    nh = lw // HD
    tok = nr * pt
    frames = nf * fl
    blk = 2 * tok
    nblk = frames // 2
    def load(f, _):
        part = x_ref[f // fl, :, f % fl].reshape(tok, width)
        rows = pl.ds(pl.multiple_of(f * tok, tok), tok)
        q = part[:, :lw] * jnp.bfloat16(HD ** -0.5)
        for h in range(nh):
            qm[h, rows, :] = head_mask(q, h, nh)
        kf[rows, :] = part[:, lw:2 * lw]
        vt[:, rows] = part[:, 2 * lw:].T
        return 0
    lax.fori_loop(0, frames, load, 0)

    def fold(v, op):
        return op(v.reshape(v.shape[0] // 8, 8, v.shape[1]), axis=0)

    def stage(cur, nxt, grow):
        zero8 = jnp.zeros((8, blk), jnp.float32)
        if nxt is not None:
            na, nhd, ns = nxt
            n0 = pl.multiple_of(na * blk, blk)
            n1 = pl.multiple_of(na * blk + tok, tok)
            ncols = pl.ds(n0, blk)
            s0 = dot(kf[pl.ds(n0, tok), :], qm[nhd, ncols, :], NT)
            s1 = dot(kf[pl.ds(n1, tok), :], qm[nhd, pl.ds(n1, tok), :], NT)
            (sa, sb)[ns][pl.ds(n0, tok), :] = s0
            (sa, sb)[ns][pl.ds(n1, tok), tok:] = s1
            m0 = fold(s0, jnp.max)
            mm = jnp.concatenate([m0[:, :tok], jnp.maximum(m0[:, tok:], fold(s1, jnp.max))], axis=1)
        else:
            mm = zero8
        if cur is not None:
            ca, chd, cs = cur
            hs = slice(chd * HD, (chd + 1) * HD)
            c0 = pl.multiple_of(ca * blk, blk)
            c1 = pl.multiple_of(ca * blk + tok, tok)
            m = (ma, mb)[cs][...]
            p0 = jnp.exp((sa, sb)[cs][pl.ds(c0, tok), :] - m)
            p1 = jnp.exp((sa, sb)[cs][pl.ds(c1, tok), tok:] - m[:, tok:])
            l0 = fold(p0, jnp.sum)
            ll = jnp.concatenate([l0[:, :tok], l0[:, tok:] + fold(p1, jnp.sum)], axis=1)
            a0 = dot(vt[hs, pl.ds(c0, tok)], p0.astype(jnp.bfloat16), NN)
            a1 = dot(vt[hs, pl.ds(c1, tok)], p1.astype(jnp.bfloat16), NN)
            acc[hs, :tok] = a0[:, :tok]
            acc[hs, tok:] = a0[:, tok:] + a1
        else:
            ll = zero8
        def score(b, mm):
            rows = pl.ds(pl.multiple_of(b * blk, blk), blk)
            s = dot(kf[rows, :], qm[nhd, ncols, :], NT)
            (sa, sb)[ns][rows, :] = s
            return jnp.maximum(mm, fold(s, jnp.max))
        def body(b, carry):
            mm, ll = carry
            if nxt is not None:
                mm = score(b, mm)
            if cur is not None:
                rows = pl.ds(pl.multiple_of(b * blk, blk), blk)
                p = jnp.exp((sa, sb)[cs][rows, :] - m)
                ll = ll + fold(p, jnp.sum)
                acc[hs, :] += dot(vt[hs, rows], p.astype(jnp.bfloat16), NN)
            return mm, ll
        trip = nxt[0] if cur is None else cur[0]
        mm, ll = lax.fori_loop(0, trip, body, (mm, ll))
        if grow and nxt is not None:
            mm = score(cur[0], mm)
        if nxt is not None:
            (ma, mb)[ns][...] = jnp.max(mm, axis=0, keepdims=True)
        if cur is not None:
            l = jnp.sum(ll, axis=0, keepdims=True)
            ot = acc[hs, :] / l
            acc[hs, :] = ot
            cols = pl.ds(c0, blk)
            ot_ref[hs, cols] = ot
            lse_ref[chd:chd + 1, cols] = m + jnp.log(l)

    def finish(a):
        o = acc[...].T.astype(jnp.bfloat16)
        for j in range(2):
            f = 2 * a + j
            o_ref[f // fl, :, f % fl] = o[j * tok:(j + 1) * tok].reshape(nr, pt, lw)
        done(a)

    def q_block(a, par, last):
        for h in range(nh):
            cur, ns = (a, h, (par + h) % 2), (par + h + 1) % 2
            if h + 1 < nh:
                stage(cur, (a, h + 1, ns), False)
            else:
                stage(cur, None if last else (a + 1, 0, ns), True)
        finish(a)
    stage(None, (0, 0, 0), False)
    span = 2 if nh % 2 else 1
    def step(i, _):
        for n in range(span):
            q_block(i * span + n, n % 2, False)
        return 0
    lax.fori_loop(0, nblk // span - 1, step, 0)
    for n in range(span):
        q_block(nblk - span + n, n % 2, n == span - 1)

def rotate_back(t, cos, sin, nh):
    out = []
    for h in range(nh):
        a = t[h * HD:h * HD + HD // 2]
        b = t[h * HD + HD // 2:(h + 1) * HD]
        out += [a * cos + b * sin, b * cos - a * sin]
    return jnp.concatenate(out, axis=0)

def flash_backward(x_ref, go_ref, ot_ref, lse_ref, cos_ref, sin_ref, gq_ref, gkv_ref, qm, dom, kf, vf, kt, delta, dqt, dka, dva, done_q, done_kv):
    nf, nr, fl, pt, width = x_ref.shape
    lw = width // 3
    nh = lw // HD
    tok = nr * pt
    frames = nf * fl
    blk = 2 * tok
    def load(f, _):
        part = x_ref[f // fl, :, f % fl].reshape(tok, width)
        go = go_ref[f // fl, :, f % fl].reshape(tok, lw)
        rows = pl.ds(pl.multiple_of(f * tok, tok), tok)
        q = part[:, :lw] * jnp.bfloat16(HD ** -0.5)
        k = part[:, lw:2 * lw]
        prod = go.T.astype(jnp.float32) * ot_ref[:, rows]
        for h in range(nh):
            qm[h, rows, :] = head_mask(q, h, nh)
            dom[h, rows, :] = head_mask(go, h, nh)
            delta[h:h + 1, rows] = jnp.sum(prod[h * HD:(h + 1) * HD], axis=0, keepdims=True)
        kf[rows, :] = k
        kt[:, rows] = k.T
        vf[rows, :] = part[:, 2 * lw:]
        dqt[:, rows] = jnp.zeros((lw, tok), jnp.float32)
        return 0
    lax.fori_loop(0, frames, load, 0)

    def work(k0, kn, q0, qn):
        rows, cols = pl.ds(k0, kn), pl.ds(q0, qn)
        k, v = kf[rows, :], vf[rows, :]
        s = [dot(k, qm[h, cols, :], NT) for h in range(nh)]
        g = [dot(v, dom[h, cols, :], NT) for h in range(nh)]
        dv, dk = [], []
        for h in range(nh):
            hs = slice(h * HD, (h + 1) * HD)
            p = jnp.exp(s[h] - lse_ref[h:h + 1, cols])
            ds = (p * (g[h] - delta[h:h + 1, cols])).astype(jnp.bfloat16)
            dv.append(dot(p.astype(jnp.bfloat16), dom[h, cols, :], NN))
            dk.append(dot(ds, qm[h, cols, :], NN))
            dqt[hs, cols] += dot(kt[hs, rows], ds, NN)
        return sum(dk[1:], dk[0]), sum(dv[1:], dv[0])

    count = frames // 2
    half = count // 2

    def store_q(a):
        cols = pl.ds(pl.multiple_of(a * blk, blk), blk)
        dq = rotate_back(dqt[:, cols] * HD ** -0.5, cos_ref[:, cols], sin_ref[:, cols], nh).T.astype(jnp.bfloat16)
        for j in range(2):
            f = 2 * a + j
            gq_ref[f // fl, :, f % fl] = dq[j * tok:(j + 1) * tok].reshape(nr, pt, lw)
        done_q(a)

    def k_block(t, _):
        b = lax.rem(t + half, count)
        k0 = pl.multiple_of(b * blk, blk)
        k1 = pl.multiple_of(b * blk + tok, tok)
        dk, dv = work(k0, tok, k0, blk)
        dka[:tok, :] = dk
        dva[:tok, :] = dv
        dk, dv = work(k1, tok, k1, tok)
        dka[tok:, :] = dk
        dva[tok:, :] = dv
        @pl.when(b < half)
        def _():
            store_q(b)
        def q_block(a, _):
            dk, dv = work(k0, blk, pl.multiple_of(a * blk, blk), blk)
            dka[...] += dk
            dva[...] += dv
            @pl.when(t == count - 1)
            def _():
                store_q(a)
            return 0
        lax.fori_loop(b + 1, count, q_block, 0)
        cols = pl.ds(k0, blk)
        dk = rotate_back(dka[...].T, cos_ref[:, cols], sin_ref[:, cols], nh).T.astype(jnp.bfloat16)
        dv = dva[...].astype(jnp.bfloat16)
        for j in range(2):
            f = 2 * b + j
            for n, part in enumerate((dk, dv)):
                gkv_ref[f // fl, :, f % fl, :, n * lw:(n + 1) * lw] = part[j * tok:(j + 1) * tok].reshape(nr, pt, lw)
        done_kv(t, b)
        return 0
    lax.fori_loop(0, count, k_block, 0)

ALL = ("clip", "frame", "row")
B16, F32 = jnp.bfloat16, jnp.float32


def rope_angles(frame_pos, patch_pos, grid):
    pair_index = jnp.arange(32)
    is_time = pair_index < 8
    is_height = (pair_index >= 8) & (pair_index < 20)
    exponent = jnp.where(
        is_time,
        pair_index / 8.0,
        jnp.where(is_height, (pair_index - 8) / 12.0, (pair_index - 20) / 12.0),
    ).astype(F32)
    frequency = jnp.power(F32(10000.0), -exponent)
    position = jnp.where(
        is_time[None, :],
        frame_pos[:, None],
        jnp.where(is_height[None, :], (patch_pos // grid)[:, None], (patch_pos % grid)[:, None]),
    ).astype(F32)
    angle = position * frequency[None, :]
    return (jnp.cos(angle), jnp.sin(angle))


def rotate_lanes(t, cos, sin):
    lane = lax.broadcasted_iota(jnp.int32, t.shape, 1)
    half = HD // 2
    lanes = t.shape[1]
    low = (lane % HD) < half
    part = jnp.where(low, pltpu.roll(t, lanes - half, 1), pltpu.roll(t, half, 1))
    return t * cos + part * sin


def stats(v):
    mean = jnp.mean(v, axis=1, keepdims=True)
    centre = v - mean
    inverse = lax.rsqrt(jnp.mean(centre * centre, axis=1, keepdims=True) + 1e-06)
    return centre * inverse, inverse


def qkv_kernel(x_ref, mod_ref, w_hbm, b_ref, cos_ref, sin_ref, o_ref, h_ref, w, sem):
    count, width = x_ref.shape
    hg, _, w3 = o_ref.shape
    lw = w3 // 3
    frames = mod_ref.shape[0]
    pt = count // frames
    copies = [pltpu.make_async_copy(w_hbm.at[:, pl.ds(j * width, width)], w.at[j], sem.at[j]) for j in range(3)]
    @pl.when(pl.program_id(0) == 0)
    def _():
        for c in copies:
            c.start()
    def one(f, _):
        rows = pl.ds(pl.multiple_of(f * pt, pt), pt)
        n, _inv = stats(x_ref[rows, :].astype(F32))
        h_ref[rows, :] = (n * (1.0 + mod_ref[f, 1:2, :]) + mod_ref[f, 0:1, :]).astype(B16)
        return 0
    lax.fori_loop(0, frames, one, 0)
    step = max(256, lw)
    for j in range(3):
        @pl.when(pl.program_id(0) == 0)
        def _():
            copies[j].wait()
        for a in range(0, width, step):
            t = dot(h_ref[...], w[j, :, a:a + step], NN) + b_ref[0:1, j * width + a:j * width + a + step]
            for g in range(step // lw):
                v = t[:, g * lw:(g + 1) * lw]
                if j < 2:
                    v = rotate_lanes(v, cos_ref[...], sin_ref[...])
                o_ref[a // lw + g, :, j * lw:(j + 1) * lw] = v.astype(B16)


def qkv_forward(x, mods, w, b, cos, sin, hg, lw):
    clips, count, width = x.shape
    frames = mods.shape[1]
    one = lambda *shape: pl.BlockSpec((None,) + shape, lambda c: (c,) + (0,) * len(shape))
    same = lambda *shape: pl.BlockSpec(shape, lambda c: (0,) * len(shape))
    return pl.pallas_call(
        qkv_kernel,
        grid=(clips,),
        in_specs=[one(count, width), one(frames, 6, width), pl.BlockSpec(memory_space=pl.ANY), same(1, 3 * width), same(count, lw), same(count, lw)],
        out_specs=(one(hg, count, 3 * lw), one(count, width)),
        out_shape=(jax.ShapeDtypeStruct((clips, hg, count, 3 * lw), B16), jax.ShapeDtypeStruct((clips, count, width), B16)),
        scratch_shapes=[pltpu.VMEM((3, width, width), B16), pltpu.SemaphoreType.DMA((3,))],
        compiler_params=pltpu.CompilerParams(vmem_limit_bytes=48 << 20, dimension_semantics=("arbitrary",)),
        cost_estimate=pl.CostEstimate(flops=6 * clips * count * width * width, bytes_accessed=clips * 10 * count * width + 6 * width * width, transcendentals=0),
        name="qkv",
    )(x, mods, w, b, cos, sin)


TN = (((0,), (0,)), ((), ()))


MESH = pl.DeviceIdType.MESH


class Plane:
    def __init__(self):
        self.nf, self.nr = lax.axis_size("frame"), lax.axis_size("row")
        self.f, self.r = lax.axis_index("frame"), lax.axis_index("row")
        self.size = self.nf * self.nr
        self.me = self.f * self.nr + self.r

    def peer(self, k):
        p = lax.rem(self.me + k, self.size)
        return p, p // self.nr, lax.rem(p, self.nr)


def greet(plane, with_clips):
    barrier = pltpu.get_barrier_semaphore()
    count = plane.size - 1
    for k in range(1, plane.size):
        _, f, r = plane.peer(k)
        pl.semaphore_signal(barrier, inc=1, device_id={"frame": f, "row": r}, device_id_type=MESH)
    if with_clips:
        nc = lax.axis_size("clip")
        c = lax.axis_index("clip")
        for k in range(1, nc):
            pl.semaphore_signal(barrier, inc=1, device_id={"clip": lax.rem(c + k, nc)}, device_id_type=MESH)
        count += nc - 1
    pl.semaphore_wait(barrier, count)


def remote(src, dst, send, recv, device):
    return pltpu.make_async_remote_copy(src_ref=src, dst_ref=dst, send_sem=send, recv_sem=recv, device_id=device, device_id_type=MESH)


def send_blocks(plane, i, a, buf, out, send, recv, local):
    fl = buf.shape[3]
    fh, at = 2 * a // fl, lax.rem(2 * a, fl)
    for r in range(plane.nr):
        src = buf.at[i, fh, r, pl.ds(at, 2)]
        dst = out.at[i, plane.me, pl.ds(at, 2)]
        own = jnp.logical_and(fh == plane.f, r == plane.r)
        dest = fh * plane.nr + r
        k = lax.rem(dest - plane.me + plane.size, plane.size)
        @pl.when(own)
        def _():
            pltpu.make_async_copy(src, dst, local.at[i]).start()
        @pl.when(jnp.logical_not(own))
        def _():
            remote(src, dst, send.at[i, k], recv.at[i, k], {"frame": fh, "row": r}).start()


def wait_blocks(plane, calls, buf, out, send, recv, local):
    for i in range(calls):
        pltpu.make_async_copy(buf.at[i, plane.f, plane.r], out.at[i, plane.me], local.at[i]).wait()
        for k in range(1, plane.size):
            p, f, r = plane.peer(k)
            copy = remote(buf.at[i, f, r], out.at[i, plane.me], send.at[i, k], recv.at[i, k], {"frame": f, "row": r})
            copy.wait_send()
            copy.wait_recv()


def fwd_all_kernel(*refs, calls):
    plane = Plane()
    x_send, x_out, a_out, ot_ref, lse_ref = refs[:5]
    xv, ob, qm, kf, vt, sa, sb, acc, ma, mb, xs, xr, xl, os, orr, ol, save = refs[5:]
    greet(plane, False)
    for i in range(calls):
        pltpu.make_async_copy(x_send.at[i, plane.me], xv.at[i, plane.f, plane.r], xl.at[i]).start()
        for k in range(1, plane.size):
            p, f, r = plane.peer(k)
            remote(x_send.at[i, p], xv.at[i, plane.f, plane.r], xs.at[i, k], xr.at[i, k], {"frame": f, "row": r}).start()

    def arrive(i, what):
        for k in range(1, plane.size):
            p, f, r = plane.peer(k)
            copy = remote(x_send.at[i, p], xv.at[i, plane.f, plane.r], xs.at[i, k], xr.at[i, k], {"frame": f, "row": r})
            copy.wait_recv() if what else copy.wait_send()

    def call(i, _):
        pltpu.make_async_copy(x_send.at[i, plane.me], xv.at[i, plane.f, plane.r], xl.at[i]).wait()
        arrive(i, True)
        pltpu.make_async_copy(xv.at[i], x_out.at[i], save.at[i]).start()
        flash_forward(xv.at[i], ob.at[i], ot_ref.at[i], lse_ref.at[i], qm, kf, vt, sa, sb, acc, ma, mb,
                      lambda a: send_blocks(plane, i, a, ob, a_out, os, orr, ol))
        return 0
    lax.fori_loop(0, calls, call, 0)
    for i in range(calls):
        arrive(i, False)
        pltpu.make_async_copy(xv.at[i], x_out.at[i], save.at[i]).wait()
    wait_blocks(plane, calls, ob, a_out, os, orr, ol)


def attention_forward(sends, lead, lw):
    calls = sends.shape[0]
    nf, nr, fl, pt = lead
    group = nf * nr
    nh = lw // HD
    seq = nf * nr * fl * pt
    blk = 2 * nr * pt
    hbm, vmem = pl.BlockSpec(memory_space=pl.ANY), pl.BlockSpec(memory_space=pltpu.VMEM)
    s, v, dma = jax.ShapeDtypeStruct, pltpu.VMEM, pltpu.SemaphoreType.DMA
    return pl.pallas_call(
        functools.partial(fwd_all_kernel, calls=calls),
        in_specs=[hbm],
        out_specs=(hbm, hbm, vmem, vmem),
        out_shape=(s((calls,) + lead + (3 * lw,), B16), s((calls, group, fl, pt, lw), B16),
                   s((calls, lw, seq), F32), s((calls, nh, seq), F32)),
        scratch_shapes=[v((calls,) + lead + (3 * lw,), B16), v((calls,) + lead + (lw,), B16), v((nh, seq, lw), B16),
                        v((seq, lw), B16), v((lw, seq), B16), v((seq, blk), F32), v((seq, blk), F32), v((lw, blk), F32), v((1, blk), F32), v((1, blk), F32),
                        dma((calls, group)), dma((calls, group)), dma((calls,)), dma((calls, group)), dma((calls, group)),
                        dma((calls,)), dma((calls,))],
        compiler_params=pltpu.CompilerParams(vmem_limit_bytes=56 << 20, collective_id=0, has_side_effects=True),
        cost_estimate=pl.CostEstimate(flops=calls * seq * seq * lw * 2, bytes_accessed=calls * seq * lw * 24, transcendentals=calls * seq * seq * nh // 2),
        name="attention_forward",
    )(sends)


class Sum:
    def __init__(self, plane, plane_first, part, out, cols, out_cols, v1, s1, v2, s2, v3, sems):
        self.plane, self.plane_first, self.part, self.out = plane, plane_first, part, out
        self.cols, self.out_cols = cols, out_cols
        self.v1, self.s1, self.v2, self.s2, self.v3, self.sems = v1, s1, v2, s2, v3, sems
        self.bit = lax.rem(plane.r, 2)

    def place(self, stage):
        plane = self.plane
        if (stage == 1) == self.plane_first:
            half = plane.nr // 2
            return plane.nf * half, plane.f * half + plane.r // 2, lambda p: {"frame": p // half, "row": lax.rem(p, half) * 2 + self.bit}
        return lax.axis_size("clip"), lax.axis_index("clip"), lambda p: {"clip": p}

    def block(self, stage, p):
        if stage == 2:
            return self.s1.at[p]
        cols = pl.ds(*self.cols)
        return self.part.at[:, p, :, cols] if self.plane_first else self.part.at[p, :, :, cols]

    def copies(self, stage):
        count, me, device = self.place(stage)
        dst = self.v1 if stage == 1 else self.v2
        base = 0 if stage == 1 else self.v1.shape[0]
        out = []
        for k in range(1, count):
            p = lax.rem(me + k, count)
            out.append(remote(self.block(stage, p), dst.at[me], self.sems.at[0, base + k], self.sems.at[1, base + k], device(p)))
        return out, pltpu.make_async_copy(self.block(stage, me), dst.at[me], self.sems.at[0, base])

    def fetch(self):
        return pltpu.make_async_copy(self.part, self.v1, self.sems.at[0, 0])

    def start(self, stage):
        copies, own = self.copies(stage)
        for c in copies:
            c.start()
        own.start()

    def wait(self, stage):
        copies, own = self.copies(stage)
        for c in copies:
            c.wait()
        own.wait()

    def middle(self):
        def one(j, _):
            total = self.v1[0, j].astype(F32)
            for c in range(1, self.v1.shape[0]):
                total = total + self.v1[c, j].astype(F32)
            self.s1[j] = total.astype(B16)
            return 0
        lax.fori_loop(0, self.s1.shape[0], one, 0)
        self.start(2)

    def third(self):
        return remote(self.s2.at[1 - self.bit], self.v3, self.sems.at[0, self.sems.shape[1] - 1], self.sems.at[1, self.sems.shape[1] - 1],
                      {"row": self.plane.r + 1 - 2 * self.bit})

    def place_columns(self, b, value):
        size = self.unit
        for k in range(self.cols[1] // size):
            to = self.where(b, (self.at + k * size) // size)
            self.out[:, to:to + size] = value[:, k * size:(k + 1) * size]

    def last(self):
        total = self.v2[0].astype(F32)
        for c in range(1, self.v2.shape[0]):
            total = total + self.v2[c].astype(F32)
        per = self.s2.shape[1]
        self.s2[0] = total[:per]
        self.s2[1] = total[per:]
        self.third().start()
        for b in range(2):
            @pl.when(self.bit == b)
            def _():
                self.place_columns(b, self.s2[b])

    def close(self):
        self.third().wait()
        for b in range(2):
            @pl.when(self.bit == b)
            def _():
                self.place_columns(1 - b, self.v3[...])


def sum_plan(parts, orders):
    scratch, outs, jobs = [], {}, []
    for n, (part, (o, half, arrived, pieces, unit, where)) in enumerate(zip(parts, orders)):
        two = part.shape[2]
        outs[o] = jax.ShapeDtypeStruct((two // 2, 2 * half), F32)
        for plane_first, first, cols, at in pieces:
            n1, n2 = part.shape[:2]
            if plane_first and not arrived:
                n1, n2 = n2, n1
            scratch += [pltpu.VMEM((n1, n2, two, cols), B16), pltpu.VMEM((n2, two, cols), B16), pltpu.VMEM((n2, two, cols), B16),
                        pltpu.VMEM((2, two // 2, cols), F32), pltpu.VMEM((two // 2, cols), F32),
                        pltpu.SemaphoreType.DMA((2, n1 + n2 + 1))]
            jobs.append((n, o, half, arrived, plane_first, first, cols, at, unit, where))
    return scratch, [outs[o] for o in sorted(outs)], jobs


def make_sums(plane, jobs, parts, outs, scratch):
    sums = []
    for i, (n, o, half, arrived, plane_first, first, cols, at, unit, where) in enumerate(jobs):
        s = Sum(plane, plane_first, parts[n], outs[o], (first, cols), half, *scratch[6 * i:6 * i + 6])
        s.at, s.arrived, s.unit, s.where = at, arrived, unit, where
        sums.append(s)
    return sums


def bwd_all_kernel(*refs, calls, count, outputs, jobs):
    plane = Plane()
    x_in, go_in, ot_in, lse_ref, cos_ref, sin_ref = refs[:6]
    go_send = refs[6:5 + calls]
    at = 5 + calls
    parts = refs[at:at + count]
    at += count
    gq_out, gkv_out = refs[at:at + 2]
    outs = refs[at + 2:at + 2 + outputs]
    at += 2 + outputs
    xv, gov, otv, gqb, gkb, qm, dom, kf, vf, kt, delta, dqt, dka, dva, loads, gs, gr, gl, qs, qr, ql, xs, xr, xl = refs[at:at + 24]
    sums = make_sums(plane, jobs, parts, outs, refs[at + 24:])
    greet(plane, True)
    load = [pltpu.make_async_copy(go_in, gov.at[0], gl.at[0])]
    for i in range(calls):
        load += [pltpu.make_async_copy(x_in.at[i], xv.at[i], loads.at[0, i]), pltpu.make_async_copy(ot_in.at[i], otv.at[i], loads.at[1, i])]
    for c in load:
        c.start()
    def go_copy(i, k, src):
        p, f, r = plane.peer(k)
        return remote(src.at[p], gov.at[i, plane.f, plane.r], gs.at[i, k], gr.at[i, k], {"frame": f, "row": r})
    for i in range(1, calls):
        pltpu.make_async_copy(go_send[i - 1].at[plane.me], gov.at[i, plane.f, plane.r], gl.at[i]).start()
        for k in range(1, plane.size):
            go_copy(i, k, go_send[i - 1]).start()
    early = [s for s in sums if s.arrived]
    late = [s for s in sums if not s.arrived]
    for s in late:
        s.start(1)
    for s in early:
        s.fetch().start()

    def call(i, _):
        pltpu.make_async_copy(x_in.at[i], xv.at[i], loads.at[0, i]).wait()
        pltpu.make_async_copy(ot_in.at[i], otv.at[i], loads.at[1, i]).wait()
        if calls > 1:
            @pl.when(i > 0)
            def _():
                pltpu.make_async_copy(go_send[0].at[plane.me], gov.at[i, plane.f, plane.r], gl.at[i]).wait()
                for k in range(1, plane.size):
                    go_copy(i, k, go_send[0]).wait_recv()
        @pl.when(i == 0)
        def _():
            pltpu.make_async_copy(go_in, gov.at[0], gl.at[0]).wait()
        def done_q(a):
            send_blocks(plane, i, a, gqb, gq_out, qs, qr, ql)
        def done_kv(t, b):
            send_blocks(plane, i, b, gkb, gkv_out, xs, xr, xl)
            at = lambda call_, step_: pl.when(jnp.logical_and(i == call_, t == step_))
            last_call = calls - 1
            @at(0, 0)
            def _():
                for s in early:
                    s.fetch().wait()
                    s.middle()
            @at(0, 7 if last_call else 3)
            def _():
                for s in late:
                    if s.plane_first:
                        s.wait(1)
                        s.middle()
            @at(last_call, 4)
            def _():
                for s in early:
                    s.wait(2)
                    s.last()
                for s in late:
                    if not s.plane_first:
                        s.wait(1)
                        s.middle()
            @at(last_call, 6)
            def _():
                for s in late:
                    if s.plane_first:
                        s.wait(2)
                        s.last()
        flash_backward(xv.at[i], gov.at[i], otv.at[i], lse_ref.at[i], cos_ref, sin_ref, gqb.at[i], gkb.at[i],
                       qm, dom, kf, vf, kt, delta, dqt, dka, dva, done_q, done_kv)
        return 0
    lax.fori_loop(0, calls, call, 0)
    for i in range(1, calls):
        for k in range(1, plane.size):
            go_copy(i, k, go_send[i - 1]).wait_send()
    for s in late:
        if not s.plane_first:
            s.wait(2)
            s.last()
    for s in sums:
        s.close()
    wait_blocks(plane, calls, gqb, gq_out, qs, qr, ql)
    wait_blocks(plane, calls, gkb, gkv_out, xs, xr, xl)


def attention_backward(x, go, go_sends, ot, lse, cos, sin, parts, orders):
    calls, nf, nr, fl, pt, w3 = x.shape
    lead = (nf, nr, fl, pt)
    lw = w3 // 3
    group = nf * nr
    nh = lw // HD
    seq = nf * nr * fl * pt
    blk = 2 * nr * pt
    hbm, vmem = pl.BlockSpec(memory_space=pl.ANY), pl.BlockSpec(memory_space=pltpu.VMEM)
    s, v, dma = jax.ShapeDtypeStruct, pltpu.VMEM, pltpu.SemaphoreType.DMA
    scratch, outs, jobs = sum_plan(parts, orders)
    return pl.pallas_call(
        functools.partial(bwd_all_kernel, calls=calls, count=len(parts), outputs=len(outs), jobs=jobs),
        in_specs=[hbm, hbm, hbm, vmem, vmem, vmem] + [hbm] * (len(go_sends) + len(parts)),
        out_specs=[hbm, hbm] + [vmem] * len(outs),
        out_shape=[s((calls, group, fl, pt, lw), B16), s((calls, group, fl, pt, 2 * lw), B16)] + outs,
        scratch_shapes=[v((calls,) + lead + (w3,), B16), v((calls,) + lead + (lw,), B16), v((calls, lw, seq), F32), v((calls,) + lead + (lw,), B16), v((calls,) + lead + (2 * lw,), B16),
                        v((nh, seq, lw), B16), v((nh, seq, lw), B16), v((seq, lw), B16), v((seq, lw), B16), v((lw, seq), B16),
                        v((nh, seq), F32), v((lw, seq), F32), v((blk, lw), F32), v((blk, lw), F32),
                        dma((2, calls)), dma((calls, group)), dma((calls, group)), dma((calls,)), dma((calls, group)), dma((calls, group)), dma((calls,)), dma((calls, group)), dma((calls, group)), dma((calls,))] + scratch,
        compiler_params=pltpu.CompilerParams(vmem_limit_bytes=61 << 20, collective_id=1, has_side_effects=True),
        cost_estimate=pl.CostEstimate(flops=calls * seq * seq * lw * 5, bytes_accessed=calls * seq * lw * 48, transcendentals=calls * seq * seq * nh // 2),
        name="attention_backward",
    )(x, go, ot, lse, cos, sin, *go_sends, *parts)


def mlp_kernel(a_ref, x_hbm, g_hbm, mod_ref, wo_ref, bo_ref, wu_ref, bu_ref, wd_ref, bd_ref,
               y_out, gm_out, ga_out, go_out, pd_out, ugot, vgot, pu_out, po_out, sums_ref, du_ref, db_ref,
               g, an, branch, mixed, h, gd, down, gh, st, gav, sd, su, rd, ru, kd, ku, pd, pu, *sems, calls):
    io, od, pair, free, done, gs, gr, gl, oo, us, ur, vr = sems
    plane = Plane()
    nc, mc = lax.axis_size("clip"), lax.axis_index("clip")
    half_row = plane.nr // 2
    places, mp = plane.nf * half_row, plane.f * half_row + plane.r // 2
    at_place = lambda p: {"frame": p // half_row, "row": lax.rem(p, half_row) * 2 + bit}
    bit = lax.rem(plane.r, 2)
    clip_first = ugot.shape[3] // (wu_ref.shape[1] // 2)
    partner = {"row": plane.r + 1 - 2 * bit}
    clips, hg, count, lw = a_ref.shape
    width = an.shape[1]
    frames = mod_ref.shape[0]
    pt = clips * count // frames
    step, steps = pl.program_id(0), pl.num_programs(0)
    fc = wu_ref.shape[1]
    slots = rd.shape[0]
    hw, hf = width // 2, fc // 2

    def each(first, last, fn):
        def one(f, _):
            fn(f, pl.ds(pl.multiple_of(f * pt, pt), pt))
            return 0
        lax.fori_loop(first, last, one, 0)

    def split(value, size, send, keep):
        for b in range(2):
            @pl.when(bit == b)
            def _():
                send[...] = value[:, (1 - b) * size:(2 - b) * size].astype(B16)
                keep[...] = value[:, b * size:(b + 1) * size]

    @pl.when(step == 0)
    def _():
        loads = [pltpu.make_async_copy(x_hbm, h, io.at[0]), pltpu.make_async_copy(g_hbm, g.at[pl.ds(0, clips * count)], io.at[1])]
        for c in loads:
            c.start()
        greet(plane, True)
        for c in range(clips):
            for i in range(hg):
                an[c * count:(c + 1) * count, i * lw:(i + 1) * lw] = a_ref[c, i]
        branch[...] = dot(an[:clips * count, :], wo_ref[...], NN) + bo_ref[...]
        for c in loads:
            c.wait()
        def fn(f, rows):
            m = h[rows, :].astype(F32) + mod_ref[f, 2:3, :] * branch[rows, :]
            mean = jnp.mean(m, axis=1, keepdims=True)
            centre = m - mean
            inv = lax.rsqrt(jnp.mean(centre * centre, axis=1, keepdims=True) + 1e-06)
            mixed[rows, :] = m
            st[rows, :128] = jnp.broadcast_to(mean, (pt, 128))
            st[rows, 128:] = jnp.broadcast_to(inv, (pt, 128))
            h[rows, :] = (centre * inv * (1.0 + mod_ref[f, 4:5, :]) + mod_ref[f, 3:4, :]).astype(B16)
            gd[rows, :] = (g[rows, :].astype(F32) * mod_ref[f, 5:6, :]).astype(B16)
        each(0, frames, fn)
        down[...] = jnp.zeros_like(down)
        gh[...] = jnp.zeros_like(gh)

    c0 = (2.0 / 3.141592653589793) ** 0.5
    c1 = 0.044715
    wu, wd = wu_ref[...], wd_ref[...]
    wide, tall, bias = None, None, None
    for c in range(clips):
        rows = slice(c * count, (c + 1) * count)
        hr, gr_ = h[rows, :], gd[rows, :]
        pre = dot(hr, wu, NN) + bu_ref[...]
        gact = dot(gr_, wd, NT)
        sq = pre * pre
        u = jnp.tanh(pre * (c0 + (c0 * c1) * sq))
        half = 0.5 * (1.0 + u)
        act = (pre * half).astype(B16)
        slope = half + (0.5 * pre) * (1.0 - u * u) * (c0 + (3.0 * c0 * c1) * sq)
        gp = (gact * slope).astype(B16)
        down[rows, :] += dot(act, wd, NN)
        gh[rows, :] += dot(gp, wu, NT)
        d, t, b = dot(act, gr_, TN), dot(hr, gp, TN), jnp.sum(gp.astype(F32), axis=0, keepdims=True)
        wide = d if wide is None else wide + d
        tall = t if tall is None else tall + t
        bias = b if bias is None else bias + b
    du_ref[...] = bias
    now, slot = lax.rem(step, 2), lax.rem(step, slots)

    def swaps(j):
        n, s = lax.rem(j, 2), lax.rem(j, slots)
        return (remote(sd.at[n], rd.at[s], pair.at[0, n], pair.at[1, s], partner),
                remote(su.at[n], ru.at[s], pair.at[2, n], pair.at[3, s], partner))

    def onward(j, what):
        n = lax.rem(j, 2)
        def do(copy, sent):
            copy.start() if what == "start" else (copy.wait_send() if sent else copy.wait())
        do(pltpu.make_async_copy(pd.at[n], pd_out.at[pl.ds(pl.multiple_of(j * fc, fc), fc)], od.at[0, n]), False)
        @pl.when(j < clip_first)
        def _():
            cols = pl.ds(pl.multiple_of(j * hf, hf), hf)
            do(pltpu.make_async_copy(pu.at[n, mc], ugot.at[mc, :, :, cols], od.at[1, n]), False)
            for k in range(1, nc):
                c = lax.rem(mc + k, nc)
                do(remote(pu.at[n, c], ugot.at[mc, :, :, cols], us.at[n, k], ur.at[mc], {"clip": c}), True)
        tail_at = steps - pu_out.shape[3] // hf
        @pl.when(j >= tail_at)
        def _():
            cols = pl.ds(pl.multiple_of((j - tail_at) * hf, hf), hf)
            do(pltpu.make_async_copy(pu.at[n], pu_out.at[:, :, :, cols], od.at[1, n]), False)
        @pl.when(jnp.logical_and(j >= clip_first, j < tail_at))
        def _():
            cols = pl.ds(pl.multiple_of((j - clip_first) * hf, hf), hf)
            do(pltpu.make_async_copy(pu.at[n, :, mp], vgot.at[mp, :, :, cols], od.at[1, n]), False)
            for k in range(1, places):
                p = lax.rem(mp + k, places)
                do(remote(pu.at[n, :, p], vgot.at[mp, :, :, cols], us.at[n, k], vr.at[mp], at_place(p)), True)

    def finish(j):
        n, s = lax.rem(j, 2), lax.rem(j, slots)
        @pl.when(j >= 2)
        def _():
            onward(j - 2, "wait")
        for c in swaps(j):
            c.wait_recv()
        pd[n] = (kd[n] + rd[s].astype(F32)).astype(B16)
        pu[n] = (ku[n] + ru[s].astype(F32)).astype(B16).reshape(pu.shape[1:])
        onward(j, "start")
        @pl.when(j + slots < steps)
        def _():
            pl.semaphore_signal(free, inc=1, device_id=partner, device_id_type=MESH)

    @pl.when(step >= 2)
    def _():
        for c in swaps(step - 2):
            c.wait_send()
    split(wide, hw, sd.at[now], kd.at[now])
    split(tall, hf, su.at[now], ku.at[now])
    @pl.when(step >= slots)
    def _():
        pl.semaphore_wait(free, 1)
    for c in swaps(step):
        c.start()
    @pl.when(step >= 1)
    def _():
        finish(step - 1)

    @pl.when(step == steps - 1)
    def _():
        db_ref[...] = jnp.zeros_like(db_ref)
        def fn(f, rows):
            gf = g[rows, :].astype(F32)
            d = down[rows, :] + bd_ref[...]
            m = mixed[rows, :]
            ghf = gh[rows, :]
            inv = st[rows, 128:129]
            n = (m - st[rows, 0:1]) * inv
            t = ghf * (1.0 + mod_ref[f, 4:5, :])
            back = t - jnp.mean(t, axis=1, keepdims=True) - n * jnp.mean(t * n, axis=1, keepdims=True)
            gm = gf + inv * back
            gbr = (gm * mod_ref[f, 2:3, :]).astype(B16)
            s = lambda v: jnp.sum(v, axis=0, keepdims=True)
            sums_ref[f] = jnp.concatenate([s(gm * branch[rows, :]), s(ghf), s(ghf * n), s(gf * d)], axis=0)
            db_ref[...] += jnp.concatenate([s(gbr.astype(F32)), s(gd[rows, :].astype(F32))], axis=0)
            mixed[rows, :] = gm
            h[rows, :] = gbr
            gd[rows, :] = (m + mod_ref[f, 5:6, :] * d).astype(B16)
        group = plane.size
        per_call = clips // calls
        def go_copies():
            out = []
            for k in range(1, group):
                p, f, r = plane.peer(k)
                out.append(remote(gav.at[p], go_out.at[plane.f, plane.r], gs.at[k], gr.at[k], {"frame": f, "row": r}))
            return out, pltpu.make_async_copy(gav.at[plane.me], go_out.at[plane.f, plane.r], gl)
        def back_out(c):
            each(c * frames // clips, (c + 1) * frames // clips, fn)
            ga = dot(h[c * count:(c + 1) * count, :], wo_ref[...], NT).astype(B16)
            for i in range(hg):
                gav[c * hg + i] = ga[:, i * lw:(i + 1) * lw]
        for c in range(per_call):
            back_out(c)
        copies, own = go_copies()
        for c in copies:
            c.start()
        own.start()
        for c in range(per_call, clips):
            back_out(c)
        outs = [pltpu.make_async_copy(gd, y_out, oo.at[0]), pltpu.make_async_copy(mixed, gm_out, oo.at[1])]
        if calls > 1:
            outs.append(pltpu.make_async_copy(gav.at[pl.ds(group, (calls - 1) * group)], ga_out, oo.at[2]))
        for c in outs:
            c.start()
        finish(step)
        pl.semaphore_signal(done, inc=1, device_id=partner, device_id_type=MESH)
        wide_out = dot(an[:clips * count, :], h[...], TN)
        for b in range(2):
            @pl.when(bit == b)
            def _():
                an[:width, :hw] = wide_out[:, (1 - b) * hw:(2 - b) * hw].astype(B16)
                down[:width, :hw] = wide_out[:, b * hw:(b + 1) * hw]
        pl.semaphore_wait(done, 1)
        ro = g.at[pl.ds(0, width), pl.ds(0, hw)]
        last = remote(an.at[pl.ds(0, width), pl.ds(0, hw)], ro, pair.at[0, 2], pair.at[1, slots], partner)
        last.start()
        last.wait()
        an[:width, hw:] = (down[:width, :hw] + g[:width, :hw].astype(F32)).astype(B16)
        outs.append(pltpu.make_async_copy(an.at[pl.ds(0, width), pl.ds(hw, hw)], po_out, oo.at[3]))
        outs[-1].start()
        for c in copies:
            c.wait()
        own.wait()
        for c in swaps(step - 1) + swaps(step):
            c.wait_send()
        onward(step - 1, "wait")
        onward(step, "wait")
        for k in range(1, places):
            p = lax.rem(mp + k, places)
            remote(vgot.at[p], vgot.at[p], us.at[0, 0], vr.at[p], at_place(p)).wait_recv()
        for k in range(1, nc):
            c = lax.rem(mc + k, nc)
            remote(ugot.at[c], ugot.at[c], us.at[0, 0], ur.at[c], {"clip": c}).wait_recv()
        for c in outs:
            c.wait()


def mlp(attn, x, g, mods, w_out, b_out, w_up, b_up, w_down, b_down, calls, lead):
    clips, hg, count, lw = attn.shape
    rows, width = x.shape
    ff = w_up.shape[1]
    frames = mods.shape[0]
    fc = min(512, ff)
    hw, hf = width // 2, fc // 2
    nf, nr = lead[:2]
    group = nf * nr
    slots = 3
    nc = lax.axis_size("clip")
    places, steps = group // 2, ff // fc
    clip_first = max(1, steps // 4)
    two_u = width // (nc * places)
    tall = max(rows, width)
    whole = lambda *shape: pl.BlockSpec(shape, lambda j: (0,) * len(shape), pipeline_mode=pl.Buffered(1))
    keep = lambda *shape: pl.BlockSpec(shape, lambda j: (0,) * len(shape))
    hbm = pl.BlockSpec(memory_space=pl.ANY)
    s, v, dma = jax.ShapeDtypeStruct, pltpu.VMEM, pltpu.SemaphoreType.DMA
    return pl.pallas_call(
        functools.partial(mlp_kernel, calls=calls),
        grid=(ff // fc,),
        in_specs=[whole(clips, hg, count, lw), hbm, hbm, whole(frames, 6, width), whole(width, width), whole(1, width),
                  pl.BlockSpec((width, fc), lambda j: (0, j)), pl.BlockSpec((1, fc), lambda j: (0, j)),
                  pl.BlockSpec((fc, width), lambda j: (j, 0)), whole(1, width)],
        out_specs=[hbm] * 9 + [keep(frames, 4, width), pl.BlockSpec((1, fc), lambda j: (0, j)), keep(2, width)],
        out_shape=[s((rows, width), B16), s((rows, width), F32), s((max(1, calls - 1) * group, count, lw), B16),
                   s((nf, nr, count, lw), B16), s((ff, hw), B16), s((nc, places, two_u, clip_first * hf), B16), s((places, nc, two_u, (steps - clip_first - 2) * hf), B16), s((nc, places, two_u, 2 * hf), B16), s((width, hw), B16),
                   s((frames, 4, width), F32), s((1, ff), F32), s((2, width), F32)],
        scratch_shapes=[v((tall, width), B16), v((tall, width), B16), v((rows, width), F32), v((rows, width), F32),
                        v((rows, width), B16), v((rows, width), B16), v((tall, width), F32), v((rows, width), F32), v((rows, 256), F32),
                        v((clips * hg, count, lw), B16), v((2, fc, hw), B16), v((2, width, hf), B16), v((slots, fc, hw), B16),
                        v((slots, width, hf), B16), v((2, fc, hw), F32), v((2, width, hf), F32), v((2, fc, hw), B16), v((2, nc, places, two_u, hf), B16),
                        dma((2,)), dma((2, 2)), dma((4, slots + 1)), pltpu.SemaphoreType.REGULAR, pltpu.SemaphoreType.REGULAR,
                        dma((group,)), dma((group,)), dma, dma((4,)), dma((2, max(places, nc))), dma((nc,)), dma((places,))],
        compiler_params=pltpu.CompilerParams(vmem_limit_bytes=63 << 20, dimension_semantics=("arbitrary",), collective_id=3, has_side_effects=True),
        cost_estimate=pl.CostEstimate(flops=2 * rows * width * (3 * width + 6 * ff), bytes_accessed=8 * width * ff + 20 * rows * width, transcendentals=rows * ff),
        name="mlp",
    )(attn, x, g, mods, w_out, b_out, w_up, b_up, w_down, b_down)


def tail_kernel(gq_hbm, gkv_hbm, h_hbm, w_hbm, x_hbm, gm_hbm, y_hbm, mod_ref, clean_ref, sums2_ref, vec_ref,
                o_out, y_out, gw_ref, noise_ref, vec_out,
                gq, gkv, h, w, x, gm, yv, ob, yb, full, gh, send, got, part, s1s, dbq, nsend, nrecv, vsend, v1, vmid, v2, io, pair, nsem, vsem, oo, *scratch, jobs):
    plane = Plane()
    clips, hg, count, lw = gq_hbm.shape
    w3 = 3 * lw
    width = w.shape[0]
    frames = mod_ref.shape[0] // clips
    pt = count // frames
    nc, nf, nr = lax.axis_size("clip"), plane.nf, plane.nr
    group = plane.size
    bit = lax.rem(plane.r, 2)
    partner = {"row": plane.r + 1 - 2 * bit}
    packed = max(1, 128 * 3 // w3)
    blocks = hg // 2 // packed
    bw = packed * w3
    loads = [pltpu.make_async_copy(gq_hbm, gq, io.at[0]), pltpu.make_async_copy(gkv_hbm, gkv, io.at[5]), pltpu.make_async_copy(h_hbm, h, io.at[1]),
             pltpu.make_async_copy(w_hbm, w, io.at[2]), pltpu.make_async_copy(x_hbm, x, io.at[3]), pltpu.make_async_copy(gm_hbm, gm, io.at[4]), pltpu.make_async_copy(y_hbm, yv, io.at[6])]
    for c in loads:
        c.start()
    sums = make_sums(plane, jobs, [part], [gw_ref], scratch)
    greet(plane, True)
    for c in loads[:3]:
        c.wait()

    def outer(j):
        total = None
        for c in range(clips):
            b = jnp.concatenate([v[c, j * packed + i] for i in range(packed) for v in (gq, gkv)], axis=1)
            t = dot(h[c], b, TN)
            total = t if total is None else total + t
        return total

    def swap(j):
        return remote(send.at[j], got.at[j], pair.at[0, j], pair.at[1, j], partner)
    other = 1 - bit
    def give(j):
        send[j] = outer(other * blocks + j).astype(B16)
        swap(j).start()
    give(0)
    for n, s in enumerate(sums):
        if n + 1 < blocks:
            give(n + 1)
        first, cols = s.cols
        j = first // bw
        total = outer(bit * blocks + j)
        swap(j).wait_recv()
        total = (total + got[j].astype(F32)).astype(B16)
        part[:, :, :, first:first + cols] = total.reshape(part.shape[:3] + (cols,))
        s.start(1)

    for c in loads[3:]:
        c.wait()
    dbq[...] = jnp.zeros_like(dbq)
    for c in range(clips):
        for g in range(hg):
            full[:, g * lw:(g + 1) * lw] = gq[c, g]
            for j in range(2):
                full[:, (j + 1) * width + g * lw:(j + 1) * width + (g + 1) * lw] = gkv[c, g, :, j * lw:(j + 1) * lw]
        gh[...] = dot(full[...], w[...], NT)
        dbq[...] += jnp.sum(full[...].astype(F32), axis=0, keepdims=True)
        def one(f, _):
            rows = pl.ds(pl.multiple_of(f * pt, pt), pt)
            cf = c * frames + f
            n, inv = stats(x[c, rows, :].astype(F32))
            ghf = gh[rows, :]
            t = ghf * (1.0 + mod_ref[cf, 1:2, :])
            back = t - jnp.mean(t, axis=1, keepdims=True) - n * jnp.mean(t * n, axis=1, keepdims=True)
            ob[f, :, c, :] = gm[c, rows, :] + inv * back
            yb[f, :, c, :] = yv[c, rows, :]
            s = lambda v: jnp.sum(v, axis=0, keepdims=True)
            s1s[cf, 0:2, :] = jnp.concatenate([s(ghf), s(ghf * n)], axis=0)
            s1s[cf, 2:6, :] = sums2_ref[cf]
            return 0
        lax.fori_loop(0, frames, one, 0)
        for s in (sums[1:2] if c < clips - 1 else sums[2 if clips > 1 else 1:3]):
            s.wait(1)
            s.middle()

    results = [pltpu.make_async_copy(ob, o_out, oo.at[0]), pltpu.make_async_copy(yb, y_out, oo.at[1])]
    for c in results:
        c.start()

    quarter = width // nr
    vsend[...] = jnp.zeros_like(vsend)
    def gather(cf, total):
        both = s1s[cf, 0:6, :]
        keep = clean_ref[cf]
        noise = jnp.where(keep > 0.5, jnp.zeros_like(both), both)
        for q in range(nr):
            nsend[q, cf] = noise[:, q * quarter:(q + 1) * quarter].astype(B16)
        return total + (both - noise)
    clean_sum = lax.fori_loop(0, clips * frames, gather, jnp.zeros((6, width), F32))
    def ncopies():
        out = []
        for k in range(1, nr):
            q = lax.rem(plane.r + k, nr)
            out.append(remote(nsend.at[q], nrecv.at[plane.r], nsem.at[0, k], nsem.at[1, k], {"row": q}))
        return out
    for c in ncopies():
        c.start()
    vsend[:6, :] = clean_sum
    vsend[6:9, :] = jnp.concatenate([dbq[:, j * width:(j + 1) * width] for j in range(3)], axis=0)
    vsend[9:9 + vec_ref.shape[0], :] = vec_ref[...]
    def vcopies(stage):
        out = []
        if stage == 1:
            for k in range(1, group):
                p, f, r = plane.peer(k)
                out.append(remote(vsend, v1.at[plane.me], vsem.at[0, k], vsem.at[1, k], {"frame": f, "row": r}))
        else:
            c = lax.axis_index("clip")
            for k in range(1, nc):
                out.append(remote(vmid, v2.at[c], vsem.at[0, group + k], vsem.at[1, group + k], {"clip": lax.rem(c + k, nc)}))
        return out
    for c in vcopies(1):
        c.start()
    for s in sums[:1] + sums[3:]:
        s.wait(1)
        s.middle()
    for c in vcopies(1):
        c.wait()
    total = vsend[...]
    for k in range(1, group):
        p, _, _ = plane.peer(k)
        total = total + v1[p]
    vmid[...] = total
    for c in vcopies(2):
        c.start()
    for c in ncopies():
        c.wait()
    def add_noise(cf, _):
        total = nsend[plane.r, cf].astype(F32)
        for k in range(1, nr):
            total = total + nrecv[lax.rem(plane.r + k, nr), cf].astype(F32)
        noise_ref[cf] = total
        return 0
    lax.fori_loop(0, clips * frames, add_noise, 0)
    for s in sums:
        s.wait(2)
        s.last()
    for c in vcopies(2):
        c.wait()
    total = vmid[...]
    for k in range(1, nc):
        total = total + v2[lax.rem(lax.axis_index("clip") + k, nc)]
    vec_out[...] = total
    for s in sums:
        s.close()
    for j in range(blocks):
        swap(j).wait_send()
    for c in results:
        c.wait()


def tail(gq, gkv, h1, w_qkv, x, gmixed, y, mods, clean, sums2, vec):
    clips, hg, count, lw = gq.shape
    w3 = 3 * lw
    width = x.shape[2]
    nc, nf, nr = (lax.axis_size(a) for a in ALL)
    group = nf * nr
    frames = mods.shape[0]
    fl, pt = frames // clips, count // (frames // clips)
    two = width // (nc * nf * nr // 2)
    packed = max(1, 128 * 3 // w3)
    blocks, bw = hg // 2 // packed, packed * w3
    vrows = -(-(9 + vec.shape[0]) // 8) * 8
    hbm, vmem = pl.BlockSpec(memory_space=pl.ANY), pl.BlockSpec(memory_space=pltpu.VMEM)
    s, v, dma = jax.ShapeDtypeStruct, pltpu.VMEM, pltpu.SemaphoreType.DMA
    shape = jax.ShapeDtypeStruct((nc, nf * nr // 2, two, blocks * bw), B16)
    order = [(False if j == 0 else True, j * bw, bw, j * bw) for j in range(blocks)]
    where = lambda b, u: u % 3 * width + (b * (hg // 2) + u // 3) * lw
    scratch, outs, jobs = sum_plan([shape], [(0, blocks * bw, False, order, lw, where)])
    return pl.pallas_call(
        functools.partial(tail_kernel, jobs=jobs),
        in_specs=[hbm] * 7 + [vmem] * 4,
        out_specs=[hbm, hbm, vmem, vmem, vmem],
        out_shape=[s((fl, pt, clips, width), F32), s((fl, pt, clips, width), B16)] + outs + [s((frames, 6, width // nr), F32), s((vrows, width), F32)],
        scratch_shapes=[v((clips, hg, count, lw), B16), v((clips, hg, count, 2 * lw), B16), v((clips, count, width), B16), v((width, 3 * width), B16), v((clips, count, width), B16),
                        v((clips, count, width), F32), v((clips, count, width), B16), v((fl, pt, clips, width), F32), v((fl, pt, clips, width), B16), v((count, 3 * width), B16), v((count, width), F32), v((blocks, width, bw), B16),
                        v((blocks, width, bw), B16), v(shape.shape, B16), v((frames, 8, width), F32), v((1, 3 * width), F32),
                        v((nr, frames, 6, width // nr), B16), v((nr, frames, 6, width // nr), B16), v((vrows, width), F32), v((group, vrows, width), F32),
                        v((vrows, width), F32), v((nc, vrows, width), F32), dma((7,)), dma((2, blocks)), dma((2, nr)), dma((2, group + nc)), dma((2,))] + scratch,
        compiler_params=pltpu.CompilerParams(vmem_limit_bytes=62 << 20, collective_id=2, has_side_effects=True),
        cost_estimate=pl.CostEstimate(flops=12 * clips * count * width * width, bytes_accessed=40 * clips * count * width, transcendentals=0),
        name="tail",
    )(gq, gkv, h1, w_qkv, x, gmixed, y, mods, clean, sums2, vec)


def on_device(tokens, context, noise_mod, clean_mod, w_qkv, b_qkv, w_out, b_out, w_up, b_up, w_down, b_down, cotangent):
    frames, patches, clips, width = tokens.shape
    count = frames * patches
    heads = width // HD
    nf, nr = lax.axis_size("frame"), lax.axis_size("row")
    group = nf * nr
    nh = max(1, heads // group)
    lw = nh * HD
    hg = heads // nh
    cs = group // hg
    calls = clips // cs
    grid = round((patches * nr) ** 0.5)
    fi, ri = lax.axis_index("frame"), lax.axis_index("row")

    is_clean = (fi * frames + jnp.arange(frames))[None, :] < context[:, None]
    mods = jnp.where(is_clean[:, :, None, None], clean_mod[None, None], noise_mod.transpose(1, 0, 2, 3))
    inputs = tokens.transpose(2, 0, 1, 3).reshape(clips, count, width)
    cots = cotangent.transpose(2, 0, 1, 3).reshape(clips, count, width)

    tok = jnp.arange(count)
    cos, sin = rope_angles(fi * frames + tok // patches, ri * patches + tok % patches, grid)
    cos_l = jnp.tile(jnp.concatenate([cos, cos], axis=1), (1, nh))
    sin_l = jnp.tile(jnp.concatenate([-sin, sin], axis=1), (1, nh))
    every = jnp.arange(nf * frames * nr * patches)
    cos_all, sin_all = rope_angles(every // (nr * patches), every % (nr * patches), grid)
    cos_t, sin_t = cos_all.T, sin_all.T
    row_of = lambda v: v.reshape(1, -1)

    lead = (nf, nr, frames, patches)
    sends, h1 = qkv_forward(inputs, mods, w_qkv, row_of(b_qkv), cos_l, sin_l, hg, lw)
    x, attn, ot, lse = attention_forward(sends.reshape(calls, group, frames, patches, 3 * lw), lead, lw)
    attn = attn.reshape(clips, hg, count, lw)

    rows = clips * count
    by_frame = mods.reshape(clips * frames, 6, width)
    y, gmixed, ga, go, part_down, got_up, got_up2, part_up, part_out, sums2, db_up, db_two = mlp(
        attn, inputs.reshape(rows, width), cots.reshape(rows, width), by_frame,
        w_out, row_of(b_out), w_up, row_of(b_up), w_down, row_of(b_down), calls, lead)
    go = go.reshape(lead + (lw,))
    go_sends = [v for v in ga.reshape((-1, group, frames, patches, lw))][:calls - 1]
    gmixed = gmixed.reshape(clips, count, width)

    nc = lax.axis_size("clip")
    places = group // 2
    first, second, hw = got_up.shape[3], got_up2.shape[3], width // 2
    as_blocks = lambda p: p.reshape(nc, places, p.shape[0] // (nc * places), p.shape[1])
    parts = [as_blocks(part_down), got_up, got_up2, part_up, as_blocks(part_out)]
    third, unit = part_up.shape[3], part_up.shape[3] // 2
    half_up = first + second + third
    by_half = lambda b, u: b * hw + u * (hw // 2)
    by_chunk = lambda b, u: (2 * u + b) * unit
    orders = [(0, hw, False, [(False, 0, hw // 2, 0), (True, hw // 2, hw // 2, hw // 2)], hw // 2, by_half),
              (1, half_up, True, [(False, 0, first, 0)], unit, by_chunk),
              (1, half_up, True, [(True, 0, second, first)], unit, by_chunk),
              (1, half_up, False, [(True, 0, third, first + second)], unit, by_chunk),
              (2, hw, False, [(False, 0, hw, 0)], hw // 2, by_half)]
    gq, gkv, gw_down, gw_up, gw_out = attention_backward(x, go, go_sends, ot, lse, cos_t, sin_t, parts, orders)
    gq, gkv = gq.reshape(clips, hg, count, lw), gkv.reshape(clips, hg, count, 2 * lw)
    clean = jnp.broadcast_to(is_clean.reshape(-1, 1, 1), (clips * frames, 1, width)).astype(F32)
    vec = jnp.concatenate([db_up.reshape(-1, width), db_two], axis=0)
    gtokens, output, gw_qkv, noise, vec = tail(gq, gkv, h1, w_qkv, inputs, gmixed, y.reshape(clips, count, width), by_frame, clean, sums2, vec)
    grad_noise = noise.reshape(clips, frames, 6, -1).transpose(1, 0, 2, 3)
    total = lax.axis_size(ALL)
    place = lax.axis_index(ALL)
    def own(at, size):
        return lax.dynamic_slice_in_dim(vec[at:at + size].reshape(-1), place * (size * width // total), size * width // total)
    grad_clean = lax.dynamic_slice_in_dim(vec[:6], place * (width // total), width // total, 1)
    ff = w_up.shape[1] // width
    gb_qkv, gb_up, gb_out, gb_down = own(6, 3), own(9, ff), own(9 + ff, 1), own(10 + ff, 1)
    return (output, gtokens, grad_noise, grad_clean, gw_qkv, gb_qkv, gw_out, gb_out, gw_up, gb_up, gw_down, gb_down)


def solution(mesh):
    token = P("frame", "row", "clip", None)
    rows = P(ALL, None)
    return jax.shard_map(
        on_device,
        mesh=mesh,
        in_specs=(token, P("clip"), P("frame", "clip", None, None)) + (P(),) * 9 + (token,),
        out_specs=(token, token, P("frame", "clip", None, "row"), P(None, ALL), rows, P(ALL), rows, P(ALL), rows, P(ALL), rows, P(ALL)),
        check_vma=False,
    )
```

```python
import functools
import jax, jax.numpy as jnp
from jax import lax
from jax.experimental import pallas as pl
from jax.experimental.pallas import tpu as pltpu
from jax.sharding import PartitionSpec as P
HD = 64
NN = (((1,), (0,)), ((), ()))
NT = (((1,), (1,)), ((), ()))
def dot(a, b, dims):
    return lax.dot_general(a, b, dims, preferred_element_type=jnp.float32)

def head_mask(values, head, heads):
    if heads == 1:
        return values
    lane = lax.broadcasted_iota(jnp.int32, values.shape, 1)
    return jnp.where(lane // HD == head, values, jnp.zeros_like(values))


def flash_forward(x_ref, o_ref, ot_ref, lse_ref, qm, kf, vt, sa, sb, acc, ma, mb, done):
    nf, nr, fl, pt, width = x_ref.shape
    lw = width // 3
    nh = lw // HD
    tok = nr * pt
    frames = nf * fl
    blk = 2 * tok
    nblk = frames // 2
    def load(f, _):
        part = x_ref[f // fl, :, f % fl].reshape(tok, width)
        rows = pl.ds(pl.multiple_of(f * tok, tok), tok)
        q = part[:, :lw] * jnp.bfloat16(HD ** -0.5)
        for h in range(nh):
            qm[h, rows, :] = head_mask(q, h, nh)
        kf[rows, :] = part[:, lw:2 * lw]
        vt[:, rows] = part[:, 2 * lw:].T
        return 0
    lax.fori_loop(0, frames, load, 0)

    def fold(v, op):
        return op(v.reshape(v.shape[0] // 8, 8, v.shape[1]), axis=0)

    def stage(cur, nxt, grow):
        zero8 = jnp.zeros((8, blk), jnp.float32)
        if nxt is not None:
            na, nhd, ns = nxt
            n0 = pl.multiple_of(na * blk, blk)
            n1 = pl.multiple_of(na * blk + tok, tok)
            ncols = pl.ds(n0, blk)
            s0 = dot(kf[pl.ds(n0, tok), :], qm[nhd, ncols, :], NT)
            s1 = dot(kf[pl.ds(n1, tok), :], qm[nhd, pl.ds(n1, tok), :], NT)
            (sa, sb)[ns][pl.ds(n0, tok), :] = s0
            (sa, sb)[ns][pl.ds(n1, tok), tok:] = s1
            m0 = fold(s0, jnp.max)
            mm = jnp.concatenate([m0[:, :tok], jnp.maximum(m0[:, tok:], fold(s1, jnp.max))], axis=1)
        else:
            mm = zero8
        if cur is not None:
            ca, chd, cs = cur
            hs = slice(chd * HD, (chd + 1) * HD)
            c0 = pl.multiple_of(ca * blk, blk)
            c1 = pl.multiple_of(ca * blk + tok, tok)
            m = (ma, mb)[cs][...]
            p0 = jnp.exp((sa, sb)[cs][pl.ds(c0, tok), :] - m)
            p1 = jnp.exp((sa, sb)[cs][pl.ds(c1, tok), tok:] - m[:, tok:])
            l0 = fold(p0, jnp.sum)
            ll = jnp.concatenate([l0[:, :tok], l0[:, tok:] + fold(p1, jnp.sum)], axis=1)
            a0 = dot(vt[hs, pl.ds(c0, tok)], p0.astype(jnp.bfloat16), NN)
            a1 = dot(vt[hs, pl.ds(c1, tok)], p1.astype(jnp.bfloat16), NN)
            acc[hs, :tok] = a0[:, :tok]
            acc[hs, tok:] = a0[:, tok:] + a1
        else:
            ll = zero8
        def score(b, mm, size=1):
            rows = pl.ds(pl.multiple_of(b * blk, blk), size * blk)
            s = dot(kf[rows, :], qm[nhd, ncols, :], NT)
            (sa, sb)[ns][rows, :] = s
            return jnp.maximum(mm, fold(s, jnp.max))
        def body(b, carry, size=1):
            mm, ll = carry
            if nxt is not None:
                mm = score(b, mm, size)
            if cur is not None:
                rows = pl.ds(pl.multiple_of(b * blk, blk), size * blk)
                p = jnp.exp((sa, sb)[cs][rows, :] - m)
                ll = ll + fold(p, jnp.sum)
                acc[hs, :] += dot(vt[hs, rows], p.astype(jnp.bfloat16), NN)
            return mm, ll
        trip = nxt[0] if cur is None else cur[0]
        pairs = trip // 2
        mm, ll = lax.fori_loop(0, pairs, lambda n, carry: body(2 * n, carry, 2), (mm, ll))
        mm, ll = lax.fori_loop(2 * pairs, trip, body, (mm, ll))
        if grow and nxt is not None:
            mm = score(cur[0], mm)
        if nxt is not None:
            (ma, mb)[ns][...] = jnp.max(mm, axis=0, keepdims=True)
        if cur is not None:
            l = jnp.sum(ll, axis=0, keepdims=True)
            ot = acc[hs, :] / l
            acc[hs, :] = ot
            cols = pl.ds(c0, blk)
            ot_ref[hs, cols] = ot
            lse_ref[chd:chd + 1, cols] = m + jnp.log(l)

    def finish(a):
        o = acc[...].T.astype(jnp.bfloat16)
        for j in range(2):
            f = 2 * a + j
            o_ref[f // fl, :, f % fl] = o[j * tok:(j + 1) * tok].reshape(nr, pt, lw)
        done(a)

    def q_block(a, par, last):
        for h in range(nh):
            cur, ns = (a, h, (par + h) % 2), (par + h + 1) % 2
            if h + 1 < nh:
                stage(cur, (a, h + 1, ns), False)
            else:
                stage(cur, None if last else (a + 1, 0, ns), True)
        finish(a)
    stage(None, (0, 0, 0), False)
    span = 2 if nh % 2 else 1
    def step(i, _):
        for n in range(span):
            q_block(i * span + n, n % 2, False)
        return 0
    lax.fori_loop(0, nblk // span - 1, step, 0)
    for n in range(span):
        q_block(nblk - span + n, n % 2, n == span - 1)

def rotate_back(t, cos, sin, nh):
    out = []
    for h in range(nh):
        a = t[h * HD:h * HD + HD // 2]
        b = t[h * HD + HD // 2:(h + 1) * HD]
        out += [a * cos + b * sin, b * cos - a * sin]
    return jnp.concatenate(out, axis=0)

def flash_backward(x_ref, go_ref, ot_ref, lse_ref, cos_ref, sin_ref, gq_ref, gkv_ref, qm, dom, kf, vf, kt, delta, dqt, dka, dva, done_q, done_kv):
    nf, nr, fl, pt, width = x_ref.shape
    lw = width // 3
    nh = lw // HD
    tok = nr * pt
    frames = nf * fl
    blk = 2 * tok
    def load(f, _):
        part = x_ref[f // fl, :, f % fl].reshape(tok, width)
        go = go_ref[f // fl, :, f % fl].reshape(tok, lw)
        rows = pl.ds(pl.multiple_of(f * tok, tok), tok)
        q = part[:, :lw] * jnp.bfloat16(HD ** -0.5)
        k = part[:, lw:2 * lw]
        prod = go.T.astype(jnp.float32) * ot_ref[:, rows]
        for h in range(nh):
            qm[h, rows, :] = head_mask(q, h, nh)
            dom[h, rows, :] = head_mask(go, h, nh)
            delta[h:h + 1, rows] = jnp.sum(prod[h * HD:(h + 1) * HD], axis=0, keepdims=True)
        kf[rows, :] = k
        kt[:, rows] = k.T
        vf[rows, :] = part[:, 2 * lw:]
        dqt[:, rows] = jnp.zeros((lw, tok), jnp.float32)
        return 0
    lax.fori_loop(0, frames, load, 0)

    def work(k0, kn, q0, qn):
        rows, cols = pl.ds(k0, kn), pl.ds(q0, qn)
        k, v = kf[rows, :], vf[rows, :]
        s = [dot(k, qm[h, cols, :], NT) for h in range(nh)]
        g = [dot(v, dom[h, cols, :], NT) for h in range(nh)]
        dv, dk = [], []
        for h in range(nh):
            hs = slice(h * HD, (h + 1) * HD)
            p = jnp.exp(s[h] - lse_ref[h:h + 1, cols])
            ds = (p * (g[h] - delta[h:h + 1, cols])).astype(jnp.bfloat16)
            dv.append(dot(p.astype(jnp.bfloat16), dom[h, cols, :], NN))
            dk.append(dot(ds, qm[h, cols, :], NN))
            dqt[hs, cols] += dot(kt[hs, rows], ds, NN)
        return sum(dk[1:], dk[0]), sum(dv[1:], dv[0])

    count = frames // 2
    half = count // 2

    def store_q(a):
        cols = pl.ds(pl.multiple_of(a * blk, blk), blk)
        dq = rotate_back(dqt[:, cols] * HD ** -0.5, cos_ref[:, cols], sin_ref[:, cols], nh).T.astype(jnp.bfloat16)
        for j in range(2):
            f = 2 * a + j
            gq_ref[f // fl, :, f % fl] = dq[j * tok:(j + 1) * tok].reshape(nr, pt, lw)
        done_q(a)

    def k_block(t, _):
        b = lax.rem(t + half, count)
        k0 = pl.multiple_of(b * blk, blk)
        k1 = pl.multiple_of(b * blk + tok, tok)
        dk, dv = work(k0, tok, k0, blk)
        dka[:tok, :] = dk
        dva[:tok, :] = dv
        dk, dv = work(k1, tok, k1, tok)
        dka[tok:, :] = dk
        dva[tok:, :] = dv
        @pl.when(b < half)
        def _():
            store_q(b)
        def q_block(a, _):
            dk, dv = work(k0, blk, pl.multiple_of(a * blk, blk), blk)
            dka[...] += dk
            dva[...] += dv
            @pl.when(t == count - 1)
            def _():
                store_q(a)
            return 0
        def q_two(n, _):
            a = b + 1 + 2 * n
            dk, dv = work(k0, blk, pl.multiple_of(a * blk, blk), 2 * blk)
            dka[...] += dk
            dva[...] += dv
            @pl.when(t == count - 1)
            def _():
                store_q(a)
                store_q(a + 1)
            return 0
        todo = (count - 1 - b) // 2
        lax.fori_loop(0, todo, q_two, 0)
        lax.fori_loop(b + 1 + 2 * todo, count, q_block, 0)
        cols = pl.ds(k0, blk)
        dk = rotate_back(dka[...].T, cos_ref[:, cols], sin_ref[:, cols], nh).T.astype(jnp.bfloat16)
        dv = dva[...].astype(jnp.bfloat16)
        for j in range(2):
            f = 2 * b + j
            for n, part in enumerate((dk, dv)):
                gkv_ref[f // fl, :, f % fl, :, n * lw:(n + 1) * lw] = part[j * tok:(j + 1) * tok].reshape(nr, pt, lw)
        done_kv(t, b)
        return 0
    lax.fori_loop(0, count, k_block, 0)

ALL = ("clip", "frame", "row")
B16, F32 = jnp.bfloat16, jnp.float32


def rope_angles(frame_pos, patch_pos, grid):
    pair_index = jnp.arange(32)
    is_time = pair_index < 8
    is_height = (pair_index >= 8) & (pair_index < 20)
    exponent = jnp.where(
        is_time,
        pair_index / 8.0,
        jnp.where(is_height, (pair_index - 8) / 12.0, (pair_index - 20) / 12.0),
    ).astype(F32)
    frequency = jnp.power(F32(10000.0), -exponent)
    position = jnp.where(
        is_time[None, :],
        frame_pos[:, None],
        jnp.where(is_height[None, :], (patch_pos // grid)[:, None], (patch_pos % grid)[:, None]),
    ).astype(F32)
    angle = position * frequency[None, :]
    return (jnp.cos(angle), jnp.sin(angle))


def rotate_lanes(t, cos, sin):
    lane = lax.broadcasted_iota(jnp.int32, t.shape, 1)
    half = HD // 2
    lanes = t.shape[1]
    low = (lane % HD) < half
    part = jnp.where(low, pltpu.roll(t, lanes - half, 1), pltpu.roll(t, half, 1))
    return t * cos + part * sin


def stats(v):
    mean = jnp.mean(v, axis=1, keepdims=True)
    centre = v - mean
    inverse = lax.rsqrt(jnp.mean(centre * centre, axis=1, keepdims=True) + 1e-06)
    return centre * inverse, inverse


def qkv_kernel(x_ref, mod_ref, w_hbm, b_ref, cos_ref, sin_ref, o_ref, h_ref, w, sem):
    count, width = x_ref.shape
    hg, _, w3 = o_ref.shape
    lw = w3 // 3
    frames = mod_ref.shape[0]
    pt = count // frames
    copies = [pltpu.make_async_copy(w_hbm.at[:, pl.ds(j * width, width)], w.at[j], sem.at[j]) for j in range(3)]
    @pl.when(pl.program_id(0) == 0)
    def _():
        for c in copies:
            c.start()
    def one(f, _):
        rows = pl.ds(pl.multiple_of(f * pt, pt), pt)
        n, _inv = stats(x_ref[rows, :].astype(F32))
        h_ref[rows, :] = (n * (1.0 + mod_ref[f, 1:2, :]) + mod_ref[f, 0:1, :]).astype(B16)
        return 0
    lax.fori_loop(0, frames, one, 0)
    step = max(256, lw)
    for j in range(3):
        @pl.when(pl.program_id(0) == 0)
        def _():
            copies[j].wait()
        for a in range(0, width, step):
            t = dot(h_ref[...], w[j, :, a:a + step], NN) + b_ref[0:1, j * width + a:j * width + a + step]
            for g in range(step // lw):
                v = t[:, g * lw:(g + 1) * lw]
                if j < 2:
                    v = rotate_lanes(v, cos_ref[...], sin_ref[...])
                o_ref[a // lw + g, :, j * lw:(j + 1) * lw] = v.astype(B16)


def qkv_forward(x, mods, w, b, cos, sin, hg, lw):
    clips, count, width = x.shape
    frames = mods.shape[1]
    one = lambda *shape: pl.BlockSpec((None,) + shape, lambda c: (c,) + (0,) * len(shape))
    same = lambda *shape: pl.BlockSpec(shape, lambda c: (0,) * len(shape))
    return pl.pallas_call(
        qkv_kernel,
        grid=(clips,),
        in_specs=[one(count, width), one(frames, 6, width), pl.BlockSpec(memory_space=pl.ANY), same(1, 3 * width), same(count, lw), same(count, lw)],
        out_specs=(one(hg, count, 3 * lw), one(count, width)),
        out_shape=(jax.ShapeDtypeStruct((clips, hg, count, 3 * lw), B16), jax.ShapeDtypeStruct((clips, count, width), B16)),
        scratch_shapes=[pltpu.VMEM((3, width, width), B16), pltpu.SemaphoreType.DMA((3,))],
        compiler_params=pltpu.CompilerParams(vmem_limit_bytes=48 << 20, dimension_semantics=("arbitrary",)),
        cost_estimate=pl.CostEstimate(flops=6 * clips * count * width * width, bytes_accessed=clips * 10 * count * width + 6 * width * width, transcendentals=0),
        name="qkv",
    )(x, mods, w, b, cos, sin)


TN = (((0,), (0,)), ((), ()))


MESH = pl.DeviceIdType.MESH


class Plane:
    def __init__(self):
        self.nf, self.nr = lax.axis_size("frame"), lax.axis_size("row")
        self.f, self.r = lax.axis_index("frame"), lax.axis_index("row")
        self.size = self.nf * self.nr
        self.me = self.f * self.nr + self.r

    def peer(self, k):
        p = lax.rem(self.me + k, self.size)
        return p, p // self.nr, lax.rem(p, self.nr)


def greet(plane, with_clips):
    barrier = pltpu.get_barrier_semaphore()
    count = plane.size - 1
    for k in range(1, plane.size):
        _, f, r = plane.peer(k)
        pl.semaphore_signal(barrier, inc=1, device_id={"frame": f, "row": r}, device_id_type=MESH)
    if with_clips:
        nc = lax.axis_size("clip")
        c = lax.axis_index("clip")
        for k in range(1, nc):
            pl.semaphore_signal(barrier, inc=1, device_id={"clip": lax.rem(c + k, nc)}, device_id_type=MESH)
        count += nc - 1
    pl.semaphore_wait(barrier, count)


def remote(src, dst, send, recv, device):
    return pltpu.make_async_remote_copy(src_ref=src, dst_ref=dst, send_sem=send, recv_sem=recv, device_id=device, device_id_type=MESH)


def send_blocks(plane, i, a, buf, out, send, recv, local):
    fl = buf.shape[3]
    fh, at = 2 * a // fl, lax.rem(2 * a, fl)
    for r in range(plane.nr):
        src = buf.at[i, fh, r, pl.ds(at, 2)]
        dst = out.at[i, plane.me, pl.ds(at, 2)]
        own = jnp.logical_and(fh == plane.f, r == plane.r)
        dest = fh * plane.nr + r
        k = lax.rem(dest - plane.me + plane.size, plane.size)
        @pl.when(own)
        def _():
            pltpu.make_async_copy(src, dst, local.at[i]).start()
        @pl.when(jnp.logical_not(own))
        def _():
            remote(src, dst, send.at[i, k], recv.at[i, k], {"frame": fh, "row": r}).start()


def wait_blocks(plane, calls, buf, out, send, recv, local):
    for i in range(calls):
        pltpu.make_async_copy(buf.at[i, plane.f, plane.r], out.at[i, plane.me], local.at[i]).wait()
        for k in range(1, plane.size):
            p, f, r = plane.peer(k)
            copy = remote(buf.at[i, f, r], out.at[i, plane.me], send.at[i, k], recv.at[i, k], {"frame": f, "row": r})
            copy.wait_send()
            copy.wait_recv()


def fwd_all_kernel(*refs, calls):
    plane = Plane()
    x_send, x_out, a_out, ot_ref, lse_ref = refs[:5]
    xv, ob, qm, kf, vt, sa, sb, acc, ma, mb, xs, xr, xl, os, orr, ol, save = refs[5:]
    greet(plane, False)
    for i in range(calls):
        pltpu.make_async_copy(x_send.at[i, plane.me], xv.at[i, plane.f, plane.r], xl.at[i]).start()
        for k in range(1, plane.size):
            p, f, r = plane.peer(k)
            remote(x_send.at[i, p], xv.at[i, plane.f, plane.r], xs.at[i, k], xr.at[i, k], {"frame": f, "row": r}).start()

    def arrive(i, what):
        for k in range(1, plane.size):
            p, f, r = plane.peer(k)
            copy = remote(x_send.at[i, p], xv.at[i, plane.f, plane.r], xs.at[i, k], xr.at[i, k], {"frame": f, "row": r})
            copy.wait_recv() if what else copy.wait_send()

    def call(i, _):
        pltpu.make_async_copy(x_send.at[i, plane.me], xv.at[i, plane.f, plane.r], xl.at[i]).wait()
        arrive(i, True)
        pltpu.make_async_copy(xv.at[i], x_out.at[i], save.at[i]).start()
        flash_forward(xv.at[i], ob.at[i], ot_ref.at[i], lse_ref.at[i], qm, kf, vt, sa, sb, acc, ma, mb,
                      lambda a: send_blocks(plane, i, a, ob, a_out, os, orr, ol))
        return 0
    lax.fori_loop(0, calls, call, 0)
    for i in range(calls):
        arrive(i, False)
        pltpu.make_async_copy(xv.at[i], x_out.at[i], save.at[i]).wait()
    wait_blocks(plane, calls, ob, a_out, os, orr, ol)


def attention_forward(sends, lead, lw):
    calls = sends.shape[0]
    nf, nr, fl, pt = lead
    group = nf * nr
    nh = lw // HD
    seq = nf * nr * fl * pt
    blk = 2 * nr * pt
    hbm, vmem = pl.BlockSpec(memory_space=pl.ANY), pl.BlockSpec(memory_space=pltpu.VMEM)
    s, v, dma = jax.ShapeDtypeStruct, pltpu.VMEM, pltpu.SemaphoreType.DMA
    return pl.pallas_call(
        functools.partial(fwd_all_kernel, calls=calls),
        in_specs=[hbm],
        out_specs=(hbm, hbm, vmem, vmem),
        out_shape=(s((calls,) + lead + (3 * lw,), B16), s((calls, group, fl, pt, lw), B16),
                   s((calls, lw, seq), F32), s((calls, nh, seq), F32)),
        scratch_shapes=[v((calls,) + lead + (3 * lw,), B16), v((calls,) + lead + (lw,), B16), v((nh, seq, lw), B16),
                        v((seq, lw), B16), v((lw, seq), B16), v((seq, blk), F32), v((seq, blk), F32), v((lw, blk), F32), v((1, blk), F32), v((1, blk), F32),
                        dma((calls, group)), dma((calls, group)), dma((calls,)), dma((calls, group)), dma((calls, group)),
                        dma((calls,)), dma((calls,))],
        compiler_params=pltpu.CompilerParams(vmem_limit_bytes=56 << 20, collective_id=0, has_side_effects=True),
        cost_estimate=pl.CostEstimate(flops=calls * seq * seq * lw * 2, bytes_accessed=calls * seq * lw * 24, transcendentals=calls * seq * seq * nh // 2),
        name="attention_forward",
    )(sends)


class Sum:
    def __init__(self, plane, plane_first, part, out, cols, out_cols, v1, s1, v2, s2, v3, sems):
        self.plane, self.plane_first, self.part, self.out = plane, plane_first, part, out
        self.cols, self.out_cols = cols, out_cols
        self.v1, self.s1, self.v2, self.s2, self.v3, self.sems = v1, s1, v2, s2, v3, sems
        self.bit = lax.rem(plane.r, 2)

    def place(self, stage):
        plane = self.plane
        if (stage == 1) == self.plane_first:
            half = plane.nr // 2
            return plane.nf * half, plane.f * half + plane.r // 2, lambda p: {"frame": p // half, "row": lax.rem(p, half) * 2 + self.bit}
        return lax.axis_size("clip"), lax.axis_index("clip"), lambda p: {"clip": p}

    def block(self, stage, p):
        if stage == 2:
            return self.s1.at[p]
        cols = pl.ds(*self.cols)
        return self.part.at[:, p, :, cols] if self.plane_first else self.part.at[p, :, :, cols]

    def copies(self, stage):
        count, me, device = self.place(stage)
        dst = self.v1 if stage == 1 else self.v2
        base = 0 if stage == 1 else self.v1.shape[0]
        out = []
        for k in range(1, count):
            p = lax.rem(me + k, count)
            out.append(remote(self.block(stage, p), dst.at[me], self.sems.at[0, base + k], self.sems.at[1, base + k], device(p)))
        return out, pltpu.make_async_copy(self.block(stage, me), dst.at[me], self.sems.at[0, base])

    def fetch(self):
        return pltpu.make_async_copy(self.part, self.v1, self.sems.at[0, 0])

    def start(self, stage):
        copies, own = self.copies(stage)
        for c in copies:
            c.start()
        own.start()

    def wait(self, stage):
        copies, own = self.copies(stage)
        for c in copies:
            c.wait()
        own.wait()

    def middle(self):
        def one(j, _):
            total = self.v1[0, j].astype(F32)
            for c in range(1, self.v1.shape[0]):
                total = total + self.v1[c, j].astype(F32)
            self.s1[j] = total.astype(B16)
            return 0
        lax.fori_loop(0, self.s1.shape[0], one, 0)
        self.start(2)

    def third(self):
        return remote(self.s2.at[1 - self.bit], self.v3, self.sems.at[0, self.sems.shape[1] - 1], self.sems.at[1, self.sems.shape[1] - 1],
                      {"row": self.plane.r + 1 - 2 * self.bit})

    def place_columns(self, b, value):
        size = self.unit
        for k in range(self.cols[1] // size):
            to = self.where(b, (self.at + k * size) // size)
            self.out[:, to:to + size] = value[:, k * size:(k + 1) * size]

    def last(self):
        total = self.v2[0].astype(F32)
        for c in range(1, self.v2.shape[0]):
            total = total + self.v2[c].astype(F32)
        per = self.s2.shape[1]
        self.s2[0] = total[:per]
        self.s2[1] = total[per:]
        self.third().start()
        for b in range(2):
            @pl.when(self.bit == b)
            def _():
                self.place_columns(b, self.s2[b])

    def close(self):
        self.third().wait()
        for b in range(2):
            @pl.when(self.bit == b)
            def _():
                self.place_columns(1 - b, self.v3[...])


def sum_plan(parts, orders):
    scratch, outs, jobs = [], {}, []
    for n, (part, (o, half, arrived, pieces, unit, where)) in enumerate(zip(parts, orders)):
        two = part.shape[2]
        outs[o] = jax.ShapeDtypeStruct((two // 2, 2 * half), F32)
        for plane_first, first, cols, at in pieces:
            n1, n2 = part.shape[:2]
            if plane_first and not arrived:
                n1, n2 = n2, n1
            scratch += [pltpu.VMEM((n1, n2, two, cols), B16), pltpu.VMEM((n2, two, cols), B16), pltpu.VMEM((n2, two, cols), B16),
                        pltpu.VMEM((2, two // 2, cols), F32), pltpu.VMEM((two // 2, cols), F32),
                        pltpu.SemaphoreType.DMA((2, n1 + n2 + 1))]
            jobs.append((n, o, half, arrived, plane_first, first, cols, at, unit, where))
    return scratch, [outs[o] for o in sorted(outs)], jobs


def make_sums(plane, jobs, parts, outs, scratch):
    sums = []
    for i, (n, o, half, arrived, plane_first, first, cols, at, unit, where) in enumerate(jobs):
        s = Sum(plane, plane_first, parts[n], outs[o], (first, cols), half, *scratch[6 * i:6 * i + 6])
        s.at, s.arrived, s.unit, s.where = at, arrived, unit, where
        sums.append(s)
    return sums


def bwd_all_kernel(*refs, calls, count, outputs, jobs):
    plane = Plane()
    x_in, go_in, ot_in, lse_ref, cos_ref, sin_ref = refs[:6]
    go_send = refs[6:5 + calls]
    at = 5 + calls
    parts = refs[at:at + count]
    at += count
    gq_out, gkv_out = refs[at:at + 2]
    outs = refs[at + 2:at + 2 + outputs]
    at += 2 + outputs
    xv, gov, otv, gqb, gkb, qm, dom, kf, vf, kt, delta, dqt, dka, dva, loads, gs, gr, gl, qs, qr, ql, xs, xr, xl = refs[at:at + 24]
    sums = make_sums(plane, jobs, parts, outs, refs[at + 24:])
    greet(plane, True)
    load = [pltpu.make_async_copy(go_in, gov.at[0], gl.at[0])]
    for i in range(calls):
        load += [pltpu.make_async_copy(x_in.at[i], xv.at[i], loads.at[0, i]), pltpu.make_async_copy(ot_in.at[i], otv.at[i], loads.at[1, i])]
    for c in load:
        c.start()
    def go_copy(i, k, src):
        p, f, r = plane.peer(k)
        return remote(src.at[p], gov.at[i, plane.f, plane.r], gs.at[i, k], gr.at[i, k], {"frame": f, "row": r})
    for i in range(1, calls):
        pltpu.make_async_copy(go_send[i - 1].at[plane.me], gov.at[i, plane.f, plane.r], gl.at[i]).start()
        for k in range(1, plane.size):
            go_copy(i, k, go_send[i - 1]).start()
    early = [s for s in sums if s.arrived]
    late = [s for s in sums if not s.arrived]
    for s in late:
        s.start(1)
    for s in early:
        s.fetch().start()

    def call(i, _):
        pltpu.make_async_copy(x_in.at[i], xv.at[i], loads.at[0, i]).wait()
        pltpu.make_async_copy(ot_in.at[i], otv.at[i], loads.at[1, i]).wait()
        if calls > 1:
            @pl.when(i > 0)
            def _():
                pltpu.make_async_copy(go_send[0].at[plane.me], gov.at[i, plane.f, plane.r], gl.at[i]).wait()
                for k in range(1, plane.size):
                    go_copy(i, k, go_send[0]).wait_recv()
        @pl.when(i == 0)
        def _():
            pltpu.make_async_copy(go_in, gov.at[0], gl.at[0]).wait()
        def done_q(a):
            send_blocks(plane, i, a, gqb, gq_out, qs, qr, ql)
        def done_kv(t, b):
            send_blocks(plane, i, b, gkb, gkv_out, xs, xr, xl)
            at = lambda call_, step_: pl.when(jnp.logical_and(i == call_, t == step_))
            last_call = calls - 1
            @at(0, 0)
            def _():
                for s in early:
                    s.fetch().wait()
                    s.middle()
            @at(0, 7 if last_call else 3)
            def _():
                for s in late:
                    if s.plane_first:
                        s.wait(1)
                        s.middle()
            @at(last_call, 4)
            def _():
                for s in early:
                    s.wait(2)
                    s.last()
                for s in late:
                    if not s.plane_first:
                        s.wait(1)
                        s.middle()
            @at(last_call, 6)
            def _():
                for s in late:
                    if s.plane_first:
                        s.wait(2)
                        s.last()
        flash_backward(xv.at[i], gov.at[i], otv.at[i], lse_ref.at[i], cos_ref, sin_ref, gqb.at[i], gkb.at[i],
                       qm, dom, kf, vf, kt, delta, dqt, dka, dva, done_q, done_kv)
        return 0
    lax.fori_loop(0, calls, call, 0)
    for i in range(1, calls):
        for k in range(1, plane.size):
            go_copy(i, k, go_send[i - 1]).wait_send()
    for s in late:
        if not s.plane_first:
            s.wait(2)
            s.last()
    for s in sums:
        s.close()
    wait_blocks(plane, calls, gqb, gq_out, qs, qr, ql)
    wait_blocks(plane, calls, gkb, gkv_out, xs, xr, xl)


def attention_backward(x, go, go_sends, ot, lse, cos, sin, parts, orders):
    calls, nf, nr, fl, pt, w3 = x.shape
    lead = (nf, nr, fl, pt)
    lw = w3 // 3
    group = nf * nr
    nh = lw // HD
    seq = nf * nr * fl * pt
    blk = 2 * nr * pt
    hbm, vmem = pl.BlockSpec(memory_space=pl.ANY), pl.BlockSpec(memory_space=pltpu.VMEM)
    s, v, dma = jax.ShapeDtypeStruct, pltpu.VMEM, pltpu.SemaphoreType.DMA
    scratch, outs, jobs = sum_plan(parts, orders)
    return pl.pallas_call(
        functools.partial(bwd_all_kernel, calls=calls, count=len(parts), outputs=len(outs), jobs=jobs),
        in_specs=[hbm, hbm, hbm, vmem, vmem, vmem] + [hbm] * (len(go_sends) + len(parts)),
        out_specs=[hbm, hbm] + [vmem] * len(outs),
        out_shape=[s((calls, group, fl, pt, lw), B16), s((calls, group, fl, pt, 2 * lw), B16)] + outs,
        scratch_shapes=[v((calls,) + lead + (w3,), B16), v((calls,) + lead + (lw,), B16), v((calls, lw, seq), F32), v((calls,) + lead + (lw,), B16), v((calls,) + lead + (2 * lw,), B16),
                        v((nh, seq, lw), B16), v((nh, seq, lw), B16), v((seq, lw), B16), v((seq, lw), B16), v((lw, seq), B16),
                        v((nh, seq), F32), v((lw, seq), F32), v((blk, lw), F32), v((blk, lw), F32),
                        dma((2, calls)), dma((calls, group)), dma((calls, group)), dma((calls,)), dma((calls, group)), dma((calls, group)), dma((calls,)), dma((calls, group)), dma((calls, group)), dma((calls,))] + scratch,
        compiler_params=pltpu.CompilerParams(vmem_limit_bytes=61 << 20, collective_id=1, has_side_effects=True),
        cost_estimate=pl.CostEstimate(flops=calls * seq * seq * lw * 5, bytes_accessed=calls * seq * lw * 48, transcendentals=calls * seq * seq * nh // 2),
        name="attention_backward",
    )(x, go, ot, lse, cos, sin, *go_sends, *parts)


def mlp_kernel(a_ref, x_hbm, g_hbm, mod_ref, wo_ref, bo_ref, wu_ref, bu_ref, wd_ref, bd_ref,
               y_out, gm_out, ga_out, go_out, pd_out, ugot, vgot, pu_out, po_out, sums_ref, du_ref, db_ref,
               g, an, branch, mixed, h, gd, down, gh, st, gav, sd, su, rd, ru, kd, ku, pd, pu, *sems, calls):
    io, od, pair, free, done, gs, gr, gl, oo, us, ur, vr = sems
    plane = Plane()
    nc, mc = lax.axis_size("clip"), lax.axis_index("clip")
    half_row = plane.nr // 2
    places, mp = plane.nf * half_row, plane.f * half_row + plane.r // 2
    at_place = lambda p: {"frame": p // half_row, "row": lax.rem(p, half_row) * 2 + bit}
    bit = lax.rem(plane.r, 2)
    clip_first = ugot.shape[3] // (wu_ref.shape[1] // 2)
    partner = {"row": plane.r + 1 - 2 * bit}
    clips, hg, count, lw = a_ref.shape
    width = an.shape[1]
    frames = mod_ref.shape[0]
    pt = clips * count // frames
    step, steps = pl.program_id(0), pl.num_programs(0)
    fc = wu_ref.shape[1]
    slots = rd.shape[0]
    hw, hf = width // 2, fc // 2

    def each(first, last, fn):
        def one(f, _):
            fn(f, pl.ds(pl.multiple_of(f * pt, pt), pt))
            return 0
        lax.fori_loop(first, last, one, 0)

    def split(value, size, send, keep):
        for b in range(2):
            @pl.when(bit == b)
            def _():
                send[...] = value[:, (1 - b) * size:(2 - b) * size].astype(B16)
                keep[...] = value[:, b * size:(b + 1) * size]

    @pl.when(step == 0)
    def _():
        loads = [pltpu.make_async_copy(x_hbm, h, io.at[0]), pltpu.make_async_copy(g_hbm, g.at[pl.ds(0, clips * count)], io.at[1])]
        for c in loads:
            c.start()
        greet(plane, True)
        for c in range(clips):
            for i in range(hg):
                an[c * count:(c + 1) * count, i * lw:(i + 1) * lw] = a_ref[c, i]
        branch[...] = dot(an[:clips * count, :], wo_ref[...], NN) + bo_ref[...]
        for c in loads:
            c.wait()
        def fn(f, rows):
            m = h[rows, :].astype(F32) + mod_ref[f, 2:3, :] * branch[rows, :]
            mean = jnp.mean(m, axis=1, keepdims=True)
            centre = m - mean
            inv = lax.rsqrt(jnp.mean(centre * centre, axis=1, keepdims=True) + 1e-06)
            mixed[rows, :] = m
            st[rows, :128] = jnp.broadcast_to(mean, (pt, 128))
            st[rows, 128:] = jnp.broadcast_to(inv, (pt, 128))
            h[rows, :] = (centre * inv * (1.0 + mod_ref[f, 4:5, :]) + mod_ref[f, 3:4, :]).astype(B16)
            gd[rows, :] = (g[rows, :].astype(F32) * mod_ref[f, 5:6, :]).astype(B16)
        each(0, frames, fn)
        down[...] = jnp.zeros_like(down)
        gh[...] = jnp.zeros_like(gh)

    c0 = (2.0 / 3.141592653589793) ** 0.5
    c1 = 0.044715
    wu, wd = wu_ref[...], wd_ref[...]
    wide, tall, bias = None, None, None
    for c in range(clips):
        rows = slice(c * count, (c + 1) * count)
        hr, gr_ = h[rows, :], gd[rows, :]
        pre = dot(hr, wu, NN) + bu_ref[...]
        gact = dot(gr_, wd, NT)
        sq = pre * pre
        u = jnp.tanh(pre * (c0 + (c0 * c1) * sq))
        half = 0.5 * (1.0 + u)
        act = (pre * half).astype(B16)
        slope = half + (0.5 * pre) * (1.0 - u * u) * (c0 + (3.0 * c0 * c1) * sq)
        gp = (gact * slope).astype(B16)
        down[rows, :] += dot(act, wd, NN)
        gh[rows, :] += dot(gp, wu, NT)
        d, t, b = dot(act, gr_, TN), dot(hr, gp, TN), jnp.sum(gp.astype(F32), axis=0, keepdims=True)
        wide = d if wide is None else wide + d
        tall = t if tall is None else tall + t
        bias = b if bias is None else bias + b
    du_ref[...] = bias
    now, slot = lax.rem(step, 2), lax.rem(step, slots)

    def swaps(j):
        n, s = lax.rem(j, 2), lax.rem(j, slots)
        return (remote(sd.at[n], rd.at[s], pair.at[0, n], pair.at[1, s], partner),
                remote(su.at[n], ru.at[s], pair.at[2, n], pair.at[3, s], partner))

    def onward(j, what):
        n = lax.rem(j, 2)
        def do(copy, sent):
            copy.start() if what == "start" else (copy.wait_send() if sent else copy.wait())
        do(pltpu.make_async_copy(pd.at[n], pd_out.at[pl.ds(pl.multiple_of(j * fc, fc), fc)], od.at[0, n]), False)
        @pl.when(j < clip_first)
        def _():
            cols = pl.ds(pl.multiple_of(j * hf, hf), hf)
            do(pltpu.make_async_copy(pu.at[n, mc], ugot.at[mc, :, :, cols], od.at[1, n]), False)
            for k in range(1, nc):
                c = lax.rem(mc + k, nc)
                do(remote(pu.at[n, c], ugot.at[mc, :, :, cols], us.at[n, k], ur.at[mc], {"clip": c}), True)
        tail_at = steps - pu_out.shape[3] // hf
        @pl.when(j >= tail_at)
        def _():
            cols = pl.ds(pl.multiple_of((j - tail_at) * hf, hf), hf)
            do(pltpu.make_async_copy(pu.at[n], pu_out.at[:, :, :, cols], od.at[1, n]), False)
        @pl.when(jnp.logical_and(j >= clip_first, j < tail_at))
        def _():
            cols = pl.ds(pl.multiple_of((j - clip_first) * hf, hf), hf)
            do(pltpu.make_async_copy(pu.at[n, :, mp], vgot.at[mp, :, :, cols], od.at[1, n]), False)
            for k in range(1, places):
                p = lax.rem(mp + k, places)
                do(remote(pu.at[n, :, p], vgot.at[mp, :, :, cols], us.at[n, k], vr.at[mp], at_place(p)), True)

    def finish(j):
        n, s = lax.rem(j, 2), lax.rem(j, slots)
        @pl.when(j >= 2)
        def _():
            onward(j - 2, "wait")
        for c in swaps(j):
            c.wait_recv()
        pd[n] = (kd[n] + rd[s].astype(F32)).astype(B16)
        pu[n] = (ku[n] + ru[s].astype(F32)).astype(B16).reshape(pu.shape[1:])
        onward(j, "start")
        @pl.when(j + slots < steps)
        def _():
            pl.semaphore_signal(free, inc=1, device_id=partner, device_id_type=MESH)

    @pl.when(step >= 2)
    def _():
        for c in swaps(step - 2):
            c.wait_send()
    split(wide, hw, sd.at[now], kd.at[now])
    split(tall, hf, su.at[now], ku.at[now])
    @pl.when(step >= slots)
    def _():
        pl.semaphore_wait(free, 1)
    for c in swaps(step):
        c.start()
    @pl.when(step >= 1)
    def _():
        finish(step - 1)

    @pl.when(step == steps - 1)
    def _():
        db_ref[...] = jnp.zeros_like(db_ref)
        def fn(f, rows):
            gf = g[rows, :].astype(F32)
            d = down[rows, :] + bd_ref[...]
            m = mixed[rows, :]
            ghf = gh[rows, :]
            inv = st[rows, 128:129]
            n = (m - st[rows, 0:1]) * inv
            t = ghf * (1.0 + mod_ref[f, 4:5, :])
            back = t - jnp.mean(t, axis=1, keepdims=True) - n * jnp.mean(t * n, axis=1, keepdims=True)
            gm = gf + inv * back
            gbr = (gm * mod_ref[f, 2:3, :]).astype(B16)
            s = lambda v: jnp.sum(v, axis=0, keepdims=True)
            sums_ref[f] = jnp.concatenate([s(gm * branch[rows, :]), s(ghf), s(ghf * n), s(gf * d)], axis=0)
            db_ref[...] += jnp.concatenate([s(gbr.astype(F32)), s(gd[rows, :].astype(F32))], axis=0)
            mixed[rows, :] = gm
            h[rows, :] = gbr
            gd[rows, :] = (m + mod_ref[f, 5:6, :] * d).astype(B16)
        group = plane.size
        per_call = clips // calls
        def go_copies():
            out = []
            for k in range(1, group):
                p, f, r = plane.peer(k)
                out.append(remote(gav.at[p], go_out.at[plane.f, plane.r], gs.at[k], gr.at[k], {"frame": f, "row": r}))
            return out, pltpu.make_async_copy(gav.at[plane.me], go_out.at[plane.f, plane.r], gl)
        def back_out(c):
            each(c * frames // clips, (c + 1) * frames // clips, fn)
            ga = dot(h[c * count:(c + 1) * count, :], wo_ref[...], NT).astype(B16)
            for i in range(hg):
                gav[c * hg + i] = ga[:, i * lw:(i + 1) * lw]
        for c in range(per_call):
            back_out(c)
        copies, own = go_copies()
        for c in copies:
            c.start()
        own.start()
        for c in range(per_call, clips):
            back_out(c)
        outs = [pltpu.make_async_copy(gd, y_out, oo.at[0]), pltpu.make_async_copy(mixed, gm_out, oo.at[1])]
        if calls > 1:
            outs.append(pltpu.make_async_copy(gav.at[pl.ds(group, (calls - 1) * group)], ga_out, oo.at[2]))
        for c in outs:
            c.start()
        finish(step)
        pl.semaphore_signal(done, inc=1, device_id=partner, device_id_type=MESH)
        wide_out = dot(an[:clips * count, :], h[...], TN)
        for b in range(2):
            @pl.when(bit == b)
            def _():
                an[:width, :hw] = wide_out[:, (1 - b) * hw:(2 - b) * hw].astype(B16)
                down[:width, :hw] = wide_out[:, b * hw:(b + 1) * hw]
        pl.semaphore_wait(done, 1)
        ro = g.at[pl.ds(0, width), pl.ds(0, hw)]
        last = remote(an.at[pl.ds(0, width), pl.ds(0, hw)], ro, pair.at[0, 2], pair.at[1, slots], partner)
        last.start()
        last.wait()
        an[:width, hw:] = (down[:width, :hw] + g[:width, :hw].astype(F32)).astype(B16)
        outs.append(pltpu.make_async_copy(an.at[pl.ds(0, width), pl.ds(hw, hw)], po_out, oo.at[3]))
        outs[-1].start()
        for c in copies:
            c.wait()
        own.wait()
        for c in swaps(step - 1) + swaps(step):
            c.wait_send()
        onward(step - 1, "wait")
        onward(step, "wait")
        for k in range(1, places):
            p = lax.rem(mp + k, places)
            remote(vgot.at[p], vgot.at[p], us.at[0, 0], vr.at[p], at_place(p)).wait_recv()
        for k in range(1, nc):
            c = lax.rem(mc + k, nc)
            remote(ugot.at[c], ugot.at[c], us.at[0, 0], ur.at[c], {"clip": c}).wait_recv()
        for c in outs:
            c.wait()


def mlp(attn, x, g, mods, w_out, b_out, w_up, b_up, w_down, b_down, calls, lead):
    clips, hg, count, lw = attn.shape
    rows, width = x.shape
    ff = w_up.shape[1]
    frames = mods.shape[0]
    fc = min(512, ff)
    hw, hf = width // 2, fc // 2
    nf, nr = lead[:2]
    group = nf * nr
    slots = 3
    nc = lax.axis_size("clip")
    places, steps = group // 2, ff // fc
    clip_first = max(1, steps // 4)
    two_u = width // (nc * places)
    tall = max(rows, width)
    whole = lambda *shape: pl.BlockSpec(shape, lambda j: (0,) * len(shape), pipeline_mode=pl.Buffered(1))
    keep = lambda *shape: pl.BlockSpec(shape, lambda j: (0,) * len(shape))
    hbm = pl.BlockSpec(memory_space=pl.ANY)
    s, v, dma = jax.ShapeDtypeStruct, pltpu.VMEM, pltpu.SemaphoreType.DMA
    return pl.pallas_call(
        functools.partial(mlp_kernel, calls=calls),
        grid=(ff // fc,),
        in_specs=[whole(clips, hg, count, lw), hbm, hbm, whole(frames, 6, width), whole(width, width), whole(1, width),
                  pl.BlockSpec((width, fc), lambda j: (0, j)), pl.BlockSpec((1, fc), lambda j: (0, j)),
                  pl.BlockSpec((fc, width), lambda j: (j, 0)), whole(1, width)],
        out_specs=[hbm] * 9 + [keep(frames, 4, width), pl.BlockSpec((1, fc), lambda j: (0, j)), keep(2, width)],
        out_shape=[s((rows, width), B16), s((rows, width), F32), s((max(1, calls - 1) * group, count, lw), B16),
                   s((nf, nr, count, lw), B16), s((ff, hw), B16), s((nc, places, two_u, clip_first * hf), B16), s((places, nc, two_u, (steps - clip_first - 2) * hf), B16), s((nc, places, two_u, 2 * hf), B16), s((width, hw), B16),
                   s((frames, 4, width), F32), s((1, ff), F32), s((2, width), F32)],
        scratch_shapes=[v((tall, width), B16), v((tall, width), B16), v((rows, width), F32), v((rows, width), F32),
                        v((rows, width), B16), v((rows, width), B16), v((tall, width), F32), v((rows, width), F32), v((rows, 256), F32),
                        v((clips * hg, count, lw), B16), v((2, fc, hw), B16), v((2, width, hf), B16), v((slots, fc, hw), B16),
                        v((slots, width, hf), B16), v((2, fc, hw), F32), v((2, width, hf), F32), v((2, fc, hw), B16), v((2, nc, places, two_u, hf), B16),
                        dma((2,)), dma((2, 2)), dma((4, slots + 1)), pltpu.SemaphoreType.REGULAR, pltpu.SemaphoreType.REGULAR,
                        dma((group,)), dma((group,)), dma, dma((4,)), dma((2, max(places, nc))), dma((nc,)), dma((places,))],
        compiler_params=pltpu.CompilerParams(vmem_limit_bytes=63 << 20, dimension_semantics=("arbitrary",), collective_id=3, has_side_effects=True),
        cost_estimate=pl.CostEstimate(flops=2 * rows * width * (3 * width + 6 * ff), bytes_accessed=8 * width * ff + 20 * rows * width, transcendentals=rows * ff),
        name="mlp",
    )(attn, x, g, mods, w_out, b_out, w_up, b_up, w_down, b_down)


def tail_kernel(gq_hbm, gkv_hbm, h_hbm, w_hbm, x_hbm, gm_hbm, y_hbm, mod_ref, clean_ref, sums2_ref, vec_ref,
                o_out, y_out, gw_ref, noise_ref, vec_out,
                gq, gkv, h, w, x, gm, yv, ob, yb, full, gh, send, got, part, s1s, dbq, nsend, nrecv, vsend, v1, vmid, v2, io, pair, nsem, vsem, oo, *scratch, jobs):
    plane = Plane()
    clips, hg, count, lw = gq_hbm.shape
    w3 = 3 * lw
    width = w.shape[0]
    frames = mod_ref.shape[0] // clips
    pt = count // frames
    nc, nf, nr = lax.axis_size("clip"), plane.nf, plane.nr
    group = plane.size
    bit = lax.rem(plane.r, 2)
    partner = {"row": plane.r + 1 - 2 * bit}
    packed = max(1, 128 * 3 // w3)
    blocks = hg // 2 // packed
    bw = packed * w3
    loads = [pltpu.make_async_copy(gq_hbm, gq, io.at[0]), pltpu.make_async_copy(gkv_hbm, gkv, io.at[5]), pltpu.make_async_copy(h_hbm, h, io.at[1]),
             pltpu.make_async_copy(w_hbm, w, io.at[2]), pltpu.make_async_copy(x_hbm, x, io.at[3]), pltpu.make_async_copy(gm_hbm, gm, io.at[4]), pltpu.make_async_copy(y_hbm, yv, io.at[6])]
    for c in loads:
        c.start()
    sums = make_sums(plane, jobs, [part], [gw_ref], scratch)
    greet(plane, True)
    for c in loads[:3]:
        c.wait()

    def outer(j):
        total = None
        for c in range(clips):
            b = jnp.concatenate([v[c, j * packed + i] for i in range(packed) for v in (gq, gkv)], axis=1)
            t = dot(h[c], b, TN)
            total = t if total is None else total + t
        return total

    def swap(j):
        return remote(send.at[j], got.at[j], pair.at[0, j], pair.at[1, j], partner)
    other = 1 - bit
    def block(n, _):
        @pl.when(n < blocks)
        def _():
            send[n] = outer(other * blocks + n).astype(B16)
            swap(n).start()
        @pl.when(n > 0)
        def _():
            j = n - 1
            total = outer(bit * blocks + j)
            swap(j).wait_recv()
            total = (total + got[j].astype(F32)).astype(B16)
            part[:, :, :, pl.ds(pl.multiple_of(j * bw, 128), bw)] = total.reshape(part.shape[:3] + (bw,))
            for k, s in enumerate(sums):
                @pl.when(j == k)
                def _():
                    s.start(1)
        return 0
    lax.fori_loop(0, blocks + 1, block, 0)

    for c in loads[3:]:
        c.wait()
    dbq[...] = jnp.zeros_like(dbq)
    def clip_back(c, _):
        for g in range(hg):
            full[:, g * lw:(g + 1) * lw] = gq[c, g]
            for j in range(2):
                full[:, (j + 1) * width + g * lw:(j + 1) * width + (g + 1) * lw] = gkv[c, g, :, j * lw:(j + 1) * lw]
        gh[...] = dot(full[...], w[...], NT)
        dbq[...] += jnp.sum(full[...].astype(F32), axis=0, keepdims=True)
        def one(f, _):
            rows = pl.ds(pl.multiple_of(f * pt, pt), pt)
            cf = c * frames + f
            n, inv = stats(x[c, rows, :].astype(F32))
            ghf = gh[rows, :]
            t = ghf * (1.0 + mod_ref[cf, 1:2, :])
            back = t - jnp.mean(t, axis=1, keepdims=True) - n * jnp.mean(t * n, axis=1, keepdims=True)
            new, out = gm[c, rows, :] + inv * back, yv[c, rows, :]
            for m in range(clips):
                @pl.when(c == m)
                def _():
                    ob[f, :, m, :] = new
                    yb[f, :, m, :] = out
            s = lambda v: jnp.sum(v, axis=0, keepdims=True)
            s1s[cf, 0:2, :] = jnp.concatenate([s(ghf), s(ghf * n)], axis=0)
            s1s[cf, 2:6, :] = sums2_ref[cf]
            return 0
        lax.fori_loop(0, frames, one, 0)
        for n in range(clips):
            @pl.when(c == n)
            def _():
                for s in (sums[1:2] if n < clips - 1 else sums[2 if clips > 1 else 1:3]):
                    s.wait(1)
                    s.middle()
        return 0
    lax.fori_loop(0, clips, clip_back, 0)

    results = [pltpu.make_async_copy(ob, o_out, oo.at[0]), pltpu.make_async_copy(yb, y_out, oo.at[1])]
    for c in results:
        c.start()

    quarter = width // nr
    vsend[...] = jnp.zeros_like(vsend)
    def gather(cf, total):
        both = s1s[cf, 0:6, :]
        keep = clean_ref[cf]
        noise = jnp.where(keep > 0.5, jnp.zeros_like(both), both)
        for q in range(nr):
            nsend[q, cf] = noise[:, q * quarter:(q + 1) * quarter].astype(B16)
        return total + (both - noise)
    clean_sum = lax.fori_loop(0, clips * frames, gather, jnp.zeros((6, width), F32))
    def ncopies():
        out = []
        for k in range(1, nr):
            q = lax.rem(plane.r + k, nr)
            out.append(remote(nsend.at[q], nrecv.at[plane.r], nsem.at[0, k], nsem.at[1, k], {"row": q}))
        return out
    for c in ncopies():
        c.start()
    vsend[:6, :] = clean_sum
    vsend[6:9, :] = jnp.concatenate([dbq[:, j * width:(j + 1) * width] for j in range(3)], axis=0)
    vsend[9:9 + vec_ref.shape[0], :] = vec_ref[...]
    def vcopies(stage):
        out = []
        if stage == 1:
            for k in range(1, group):
                p, f, r = plane.peer(k)
                out.append(remote(vsend, v1.at[plane.me], vsem.at[0, k], vsem.at[1, k], {"frame": f, "row": r}))
        else:
            c = lax.axis_index("clip")
            for k in range(1, nc):
                out.append(remote(vmid, v2.at[c], vsem.at[0, group + k], vsem.at[1, group + k], {"clip": lax.rem(c + k, nc)}))
        return out
    for c in vcopies(1):
        c.start()
    for s in sums[:1] + sums[3:]:
        s.wait(1)
        s.middle()
    for c in vcopies(1):
        c.wait()
    total = vsend[...]
    for k in range(1, group):
        p, _, _ = plane.peer(k)
        total = total + v1[p]
    vmid[...] = total
    for c in vcopies(2):
        c.start()
    for c in ncopies():
        c.wait()
    def add_noise(cf, _):
        total = nsend[plane.r, cf].astype(F32)
        for k in range(1, nr):
            total = total + nrecv[lax.rem(plane.r + k, nr), cf].astype(F32)
        noise_ref[cf] = total
        return 0
    lax.fori_loop(0, clips * frames, add_noise, 0)
    for s in sums:
        s.wait(2)
        s.last()
    for c in vcopies(2):
        c.wait()
    total = vmid[...]
    for k in range(1, nc):
        total = total + v2[lax.rem(lax.axis_index("clip") + k, nc)]
    vec_out[...] = total
    for s in sums:
        s.close()
    for j in range(blocks):
        swap(j).wait_send()
    for c in results:
        c.wait()


def tail(gq, gkv, h1, w_qkv, x, gmixed, y, mods, clean, sums2, vec):
    clips, hg, count, lw = gq.shape
    w3 = 3 * lw
    width = x.shape[2]
    nc, nf, nr = (lax.axis_size(a) for a in ALL)
    group = nf * nr
    frames = mods.shape[0]
    fl, pt = frames // clips, count // (frames // clips)
    two = width // (nc * nf * nr // 2)
    packed = max(1, 128 * 3 // w3)
    blocks, bw = hg // 2 // packed, packed * w3
    vrows = -(-(9 + vec.shape[0]) // 8) * 8
    hbm, vmem = pl.BlockSpec(memory_space=pl.ANY), pl.BlockSpec(memory_space=pltpu.VMEM)
    s, v, dma = jax.ShapeDtypeStruct, pltpu.VMEM, pltpu.SemaphoreType.DMA
    shape = jax.ShapeDtypeStruct((nc, nf * nr // 2, two, blocks * bw), B16)
    order = [(False if j == 0 else True, j * bw, bw, j * bw) for j in range(blocks)]
    where = lambda b, u: u % 3 * width + (b * (hg // 2) + u // 3) * lw
    scratch, outs, jobs = sum_plan([shape], [(0, blocks * bw, False, order, lw, where)])
    return pl.pallas_call(
        functools.partial(tail_kernel, jobs=jobs),
        in_specs=[hbm] * 7 + [vmem] * 4,
        out_specs=[hbm, hbm, vmem, vmem, vmem],
        out_shape=[s((fl, pt, clips, width), F32), s((fl, pt, clips, width), B16)] + outs + [s((frames, 6, width // nr), F32), s((vrows, width), F32)],
        scratch_shapes=[v((clips, hg, count, lw), B16), v((clips, hg, count, 2 * lw), B16), v((clips, count, width), B16), v((width, 3 * width), B16), v((clips, count, width), B16),
                        v((clips, count, width), F32), v((clips, count, width), B16), v((fl, pt, clips, width), F32), v((fl, pt, clips, width), B16), v((count, 3 * width), B16), v((count, width), F32), v((blocks, width, bw), B16),
                        v((blocks, width, bw), B16), v(shape.shape, B16), v((frames, 8, width), F32), v((1, 3 * width), F32),
                        v((nr, frames, 6, width // nr), B16), v((nr, frames, 6, width // nr), B16), v((vrows, width), F32), v((group, vrows, width), F32),
                        v((vrows, width), F32), v((nc, vrows, width), F32), dma((7,)), dma((2, blocks)), dma((2, nr)), dma((2, group + nc)), dma((2,))] + scratch,
        compiler_params=pltpu.CompilerParams(vmem_limit_bytes=62 << 20, collective_id=2, has_side_effects=True),
        cost_estimate=pl.CostEstimate(flops=12 * clips * count * width * width, bytes_accessed=40 * clips * count * width, transcendentals=0),
        name="tail",
    )(gq, gkv, h1, w_qkv, x, gmixed, y, mods, clean, sums2, vec)


def on_device(tokens, context, noise_mod, clean_mod, w_qkv, b_qkv, w_out, b_out, w_up, b_up, w_down, b_down, cotangent):
    frames, patches, clips, width = tokens.shape
    count = frames * patches
    heads = width // HD
    nf, nr = lax.axis_size("frame"), lax.axis_size("row")
    group = nf * nr
    nh = max(1, heads // group)
    lw = nh * HD
    hg = heads // nh
    cs = group // hg
    calls = clips // cs
    grid = round((patches * nr) ** 0.5)
    fi, ri = lax.axis_index("frame"), lax.axis_index("row")

    is_clean = (fi * frames + jnp.arange(frames))[None, :] < context[:, None]
    mods = jnp.where(is_clean[:, :, None, None], clean_mod[None, None], noise_mod.transpose(1, 0, 2, 3))
    inputs = tokens.transpose(2, 0, 1, 3).reshape(clips, count, width)
    cots = cotangent.transpose(2, 0, 1, 3).reshape(clips, count, width)

    tok = jnp.arange(count)
    cos, sin = rope_angles(fi * frames + tok // patches, ri * patches + tok % patches, grid)
    cos_l = jnp.tile(jnp.concatenate([cos, cos], axis=1), (1, nh))
    sin_l = jnp.tile(jnp.concatenate([-sin, sin], axis=1), (1, nh))
    every = jnp.arange(nf * frames * nr * patches)
    cos_all, sin_all = rope_angles(every // (nr * patches), every % (nr * patches), grid)
    cos_t, sin_t = cos_all.T, sin_all.T
    row_of = lambda v: v.reshape(1, -1)

    lead = (nf, nr, frames, patches)
    sends, h1 = qkv_forward(inputs, mods, w_qkv, row_of(b_qkv), cos_l, sin_l, hg, lw)
    x, attn, ot, lse = attention_forward(sends.reshape(calls, group, frames, patches, 3 * lw), lead, lw)
    attn = attn.reshape(clips, hg, count, lw)

    rows = clips * count
    by_frame = mods.reshape(clips * frames, 6, width)
    y, gmixed, ga, go, part_down, got_up, got_up2, part_up, part_out, sums2, db_up, db_two = mlp(
        attn, inputs.reshape(rows, width), cots.reshape(rows, width), by_frame,
        w_out, row_of(b_out), w_up, row_of(b_up), w_down, row_of(b_down), calls, lead)
    go = go.reshape(lead + (lw,))
    go_sends = [v for v in ga.reshape((-1, group, frames, patches, lw))][:calls - 1]
    gmixed = gmixed.reshape(clips, count, width)

    nc = lax.axis_size("clip")
    places = group // 2
    first, second, hw = got_up.shape[3], got_up2.shape[3], width // 2
    as_blocks = lambda p: p.reshape(nc, places, p.shape[0] // (nc * places), p.shape[1])
    parts = [as_blocks(part_down), got_up, got_up2, part_up, as_blocks(part_out)]
    third, unit = part_up.shape[3], part_up.shape[3] // 2
    half_up = first + second + third
    by_half = lambda b, u: b * hw + u * (hw // 2)
    by_chunk = lambda b, u: (2 * u + b) * unit
    orders = [(0, hw, False, [(False, 0, hw // 2, 0), (True, hw // 2, hw // 2, hw // 2)], hw // 2, by_half),
              (1, half_up, True, [(False, 0, first, 0)], unit, by_chunk),
              (1, half_up, True, [(True, 0, second, first)], unit, by_chunk),
              (1, half_up, False, [(True, 0, third, first + second)], unit, by_chunk),
              (2, hw, False, [(False, 0, hw, 0)], hw // 2, by_half)]
    gq, gkv, gw_down, gw_up, gw_out = attention_backward(x, go, go_sends, ot, lse, cos_t, sin_t, parts, orders)
    gq, gkv = gq.reshape(clips, hg, count, lw), gkv.reshape(clips, hg, count, 2 * lw)
    clean = jnp.broadcast_to(is_clean.reshape(-1, 1, 1), (clips * frames, 1, width)).astype(F32)
    vec = jnp.concatenate([db_up.reshape(-1, width), db_two], axis=0)
    gtokens, output, gw_qkv, noise, vec = tail(gq, gkv, h1, w_qkv, inputs, gmixed, y.reshape(clips, count, width), by_frame, clean, sums2, vec)
    grad_noise = noise.reshape(clips, frames, 6, -1).transpose(1, 0, 2, 3)
    total = lax.axis_size(ALL)
    place = lax.axis_index(ALL)
    def own(at, size):
        return lax.dynamic_slice_in_dim(vec[at:at + size].reshape(-1), place * (size * width // total), size * width // total)
    grad_clean = lax.dynamic_slice_in_dim(vec[:6], place * (width // total), width // total, 1)
    ff = w_up.shape[1] // width
    gb_qkv, gb_up, gb_out, gb_down = own(6, 3), own(9, ff), own(9 + ff, 1), own(10 + ff, 1)
    return (output, gtokens, grad_noise, grad_clean, gw_qkv, gb_qkv, gw_out, gb_out, gw_up, gb_up, gw_down, gb_down)


def solution(mesh):
    token = P("frame", "row", "clip", None)
    rows = P(ALL, None)
    return jax.shard_map(
        on_device,
        mesh=mesh,
        in_specs=(token, P("clip"), P("frame", "clip", None, None)) + (P(),) * 9 + (token,),
        out_specs=(token, token, P("frame", "clip", None, "row"), P(None, ALL), rows, P(ALL), rows, P(ALL), rows, P(ALL), rows, P(ALL)),
        check_vma=False,
    )
```

```python
import functools
import jax, jax.numpy as jnp
from jax import lax
from jax.experimental import pallas as pl
from jax.experimental.pallas import tpu as pltpu
from jax.sharding import PartitionSpec as P
HD = 64
NN = (((1,), (0,)), ((), ()))
NT = (((1,), (1,)), ((), ()))
def dot(a, b, dims):
    return lax.dot_general(a, b, dims, preferred_element_type=jnp.float32)

def head_mask(values, head, heads):
    if heads == 1:
        return values
    lane = lax.broadcasted_iota(jnp.int32, values.shape, 1)
    return jnp.where(lane // HD == head, values, jnp.zeros_like(values))


def flash_forward(x_ref, o_ref, ot_ref, lse_ref, qm, kf, vt, sa, sb, acc, ma, mb, done):
    nf, nr, fl, pt, width = x_ref.shape
    lw = width // 3
    nh = lw // HD
    tok = nr * pt
    frames = nf * fl
    blk = 2 * tok
    nblk = frames // 2
    def load(f, _):
        part = x_ref[f // fl, :, f % fl].reshape(tok, width)
        rows = pl.ds(pl.multiple_of(f * tok, tok), tok)
        q = part[:, :lw] * jnp.bfloat16(HD ** -0.5)
        for h in range(nh):
            qm[h, rows, :] = head_mask(q, h, nh)
        kf[rows, :] = part[:, lw:2 * lw]
        vt[:, rows] = part[:, 2 * lw:].T
        return 0
    lax.fori_loop(0, frames, load, 0)

    def fold(v, op):
        return op(v.reshape(v.shape[0] // 8, 8, v.shape[1]), axis=0)

    def stage(cur, nxt, grow):
        zero8 = jnp.zeros((8, blk), jnp.float32)
        if nxt is not None:
            na, nhd, ns = nxt
            n0 = pl.multiple_of(na * blk, blk)
            n1 = pl.multiple_of(na * blk + tok, tok)
            ncols = pl.ds(n0, blk)
            s0 = dot(kf[pl.ds(n0, tok), :], qm[nhd, ncols, :], NT)
            s1 = dot(kf[pl.ds(n1, tok), :], qm[nhd, pl.ds(n1, tok), :], NT)
            (sa, sb)[ns][pl.ds(n0, tok), :] = s0
            (sa, sb)[ns][pl.ds(n1, tok), tok:] = s1
            m0 = fold(s0, jnp.max)
            mm = jnp.concatenate([m0[:, :tok], jnp.maximum(m0[:, tok:], fold(s1, jnp.max))], axis=1)
        else:
            mm = zero8
        if cur is not None:
            ca, chd, cs = cur
            hs = slice(chd * HD, (chd + 1) * HD)
            c0 = pl.multiple_of(ca * blk, blk)
            c1 = pl.multiple_of(ca * blk + tok, tok)
            m = (ma, mb)[cs][...]
            p0 = jnp.exp((sa, sb)[cs][pl.ds(c0, tok), :] - m)
            p1 = jnp.exp((sa, sb)[cs][pl.ds(c1, tok), tok:] - m[:, tok:])
            l0 = fold(p0, jnp.sum)
            ll = jnp.concatenate([l0[:, :tok], l0[:, tok:] + fold(p1, jnp.sum)], axis=1)
            a0 = dot(vt[hs, pl.ds(c0, tok)], p0.astype(jnp.bfloat16), NN)
            a1 = dot(vt[hs, pl.ds(c1, tok)], p1.astype(jnp.bfloat16), NN)
            acc[hs, :tok] = a0[:, :tok]
            acc[hs, tok:] = a0[:, tok:] + a1
        else:
            ll = zero8
        def score(b, mm, size=1):
            rows = pl.ds(pl.multiple_of(b * blk, blk), size * blk)
            s = dot(kf[rows, :], qm[nhd, ncols, :], NT)
            (sa, sb)[ns][rows, :] = s
            return jnp.maximum(mm, fold(s, jnp.max))
        def body(b, carry, size=1):
            mm, ll = carry
            if nxt is not None:
                mm = score(b, mm, size)
            if cur is not None:
                rows = pl.ds(pl.multiple_of(b * blk, blk), size * blk)
                p = jnp.exp((sa, sb)[cs][rows, :] - m)
                ll = ll + fold(p, jnp.sum)
                acc[hs, :] += dot(vt[hs, rows], p.astype(jnp.bfloat16), NN)
            return mm, ll
        trip = nxt[0] if cur is None else cur[0]
        pairs = trip // 2
        mm, ll = lax.fori_loop(0, pairs, lambda n, carry: body(2 * n, carry, 2), (mm, ll))
        mm, ll = lax.fori_loop(2 * pairs, trip, body, (mm, ll))
        if grow and nxt is not None:
            mm = score(cur[0], mm)
        if nxt is not None:
            (ma, mb)[ns][...] = jnp.max(mm, axis=0, keepdims=True)
        if cur is not None:
            l = jnp.sum(ll, axis=0, keepdims=True)
            ot = acc[hs, :] / l
            acc[hs, :] = ot
            cols = pl.ds(c0, blk)
            ot_ref[hs, cols] = ot
            lse_ref[chd:chd + 1, cols] = m + jnp.log(l)

    def finish(a):
        o = acc[...].T.astype(jnp.bfloat16)
        for j in range(2):
            f = 2 * a + j
            o_ref[f // fl, :, f % fl] = o[j * tok:(j + 1) * tok].reshape(nr, pt, lw)
        done(a)

    def q_block(a, par, last):
        for h in range(nh):
            cur, ns = (a, h, (par + h) % 2), (par + h + 1) % 2
            if h + 1 < nh:
                stage(cur, (a, h + 1, ns), False)
            else:
                stage(cur, None if last else (a + 1, 0, ns), True)
        finish(a)
    stage(None, (0, 0, 0), False)
    span = 2 if nh % 2 else 1
    def step(i, _):
        for n in range(span):
            q_block(i * span + n, n % 2, False)
        return 0
    lax.fori_loop(0, nblk // span - 1, step, 0)
    for n in range(span):
        q_block(nblk - span + n, n % 2, n == span - 1)

def rotate_back(t, cos, sin, nh):
    out = []
    for h in range(nh):
        a = t[h * HD:h * HD + HD // 2]
        b = t[h * HD + HD // 2:(h + 1) * HD]
        out += [a * cos + b * sin, b * cos - a * sin]
    return jnp.concatenate(out, axis=0)

def flash_backward(x_ref, go_ref, ot_ref, lse_ref, cos_ref, sin_ref, gq_ref, gkv_ref, qm, dom, kf, vf, kt, delta, dqt, dka, dva, done_q, done_kv):
    nf, nr, fl, pt, width = x_ref.shape
    lw = width // 3
    nh = lw // HD
    tok = nr * pt
    frames = nf * fl
    blk = 2 * tok
    def load(f, _):
        part = x_ref[f // fl, :, f % fl].reshape(tok, width)
        go = go_ref[f // fl, :, f % fl].reshape(tok, lw)
        rows = pl.ds(pl.multiple_of(f * tok, tok), tok)
        q = part[:, :lw] * jnp.bfloat16(HD ** -0.5)
        k = part[:, lw:2 * lw]
        prod = go.T.astype(jnp.float32) * ot_ref[:, rows]
        for h in range(nh):
            qm[h, rows, :] = head_mask(q, h, nh)
            dom[h, rows, :] = head_mask(go, h, nh)
            delta[h:h + 1, rows] = jnp.sum(prod[h * HD:(h + 1) * HD], axis=0, keepdims=True)
        kf[rows, :] = k
        kt[:, rows] = k.T
        vf[rows, :] = part[:, 2 * lw:]
        dqt[:, rows] = jnp.zeros((lw, tok), jnp.float32)
        return 0
    lax.fori_loop(0, frames, load, 0)

    def work(k0, kn, q0, qn):
        rows, cols = pl.ds(k0, kn), pl.ds(q0, qn)
        k, v = kf[rows, :], vf[rows, :]
        s = [dot(k, qm[h, cols, :], NT) for h in range(nh)]
        g = [dot(v, dom[h, cols, :], NT) for h in range(nh)]
        dv, dk = [], []
        for h in range(nh):
            hs = slice(h * HD, (h + 1) * HD)
            p = jnp.exp(s[h] - lse_ref[h:h + 1, cols])
            ds = (p * (g[h] - delta[h:h + 1, cols])).astype(jnp.bfloat16)
            dv.append(dot(p.astype(jnp.bfloat16), dom[h, cols, :], NN))
            dk.append(dot(ds, qm[h, cols, :], NN))
            dqt[hs, cols] += dot(kt[hs, rows], ds, NN)
        return sum(dk[1:], dk[0]), sum(dv[1:], dv[0])

    count = frames // 2
    half = count // 2

    def store_q(a):
        cols = pl.ds(pl.multiple_of(a * blk, blk), blk)
        dq = rotate_back(dqt[:, cols] * HD ** -0.5, cos_ref[:, cols], sin_ref[:, cols], nh).T.astype(jnp.bfloat16)
        for j in range(2):
            f = 2 * a + j
            gq_ref[f // fl, :, f % fl] = dq[j * tok:(j + 1) * tok].reshape(nr, pt, lw)
        done_q(a)

    def k_block(t, _):
        b = lax.rem(t + half, count)
        k0 = pl.multiple_of(b * blk, blk)
        k1 = pl.multiple_of(b * blk + tok, tok)
        dk, dv = work(k0, tok, k0, blk)
        dka[:tok, :] = dk
        dva[:tok, :] = dv
        dk, dv = work(k1, tok, k1, tok)
        dka[tok:, :] = dk
        dva[tok:, :] = dv
        @pl.when(b < half)
        def _():
            store_q(b)
        def q_block(a, _):
            dk, dv = work(k0, blk, pl.multiple_of(a * blk, blk), blk)
            dka[...] += dk
            dva[...] += dv
            @pl.when(t == count - 1)
            def _():
                store_q(a)
            return 0
        def q_two(n, _):
            a = b + 1 + 2 * n
            dk, dv = work(k0, blk, pl.multiple_of(a * blk, blk), 2 * blk)
            dka[...] += dk
            dva[...] += dv
            @pl.when(t == count - 1)
            def _():
                store_q(a)
                store_q(a + 1)
            return 0
        todo = (count - 1 - b) // 2
        lax.fori_loop(0, todo, q_two, 0)
        lax.fori_loop(b + 1 + 2 * todo, count, q_block, 0)
        cols = pl.ds(k0, blk)
        dk = rotate_back(dka[...].T, cos_ref[:, cols], sin_ref[:, cols], nh).T.astype(jnp.bfloat16)
        dv = dva[...].astype(jnp.bfloat16)
        for j in range(2):
            f = 2 * b + j
            for n, part in enumerate((dk, dv)):
                gkv_ref[f // fl, :, f % fl, :, n * lw:(n + 1) * lw] = part[j * tok:(j + 1) * tok].reshape(nr, pt, lw)
        done_kv(t, b)
        return 0
    lax.fori_loop(0, count, k_block, 0)

ALL = ("clip", "frame", "row")
B16, F32 = jnp.bfloat16, jnp.float32


def rope_angles(frame_pos, patch_pos, grid):
    pair_index = jnp.arange(32)
    is_time = pair_index < 8
    is_height = (pair_index >= 8) & (pair_index < 20)
    exponent = jnp.where(
        is_time,
        pair_index / 8.0,
        jnp.where(is_height, (pair_index - 8) / 12.0, (pair_index - 20) / 12.0),
    ).astype(F32)
    frequency = jnp.power(F32(10000.0), -exponent)
    position = jnp.where(
        is_time[None, :],
        frame_pos[:, None],
        jnp.where(is_height[None, :], (patch_pos // grid)[:, None], (patch_pos % grid)[:, None]),
    ).astype(F32)
    angle = position * frequency[None, :]
    return (jnp.cos(angle), jnp.sin(angle))


def rotate_lanes(t, cos, sin):
    lane = lax.broadcasted_iota(jnp.int32, t.shape, 1)
    half = HD // 2
    lanes = t.shape[1]
    low = (lane % HD) < half
    part = jnp.where(low, pltpu.roll(t, lanes - half, 1), pltpu.roll(t, half, 1))
    return t * cos + part * sin


def stats(v):
    mean = jnp.mean(v, axis=1, keepdims=True)
    centre = v - mean
    inverse = lax.rsqrt(jnp.mean(centre * centre, axis=1, keepdims=True) + 1e-06)
    return centre * inverse, inverse


def qkv_kernel(x_ref, mod_ref, w_hbm, b_ref, cos_ref, sin_ref, o_ref, h_ref, w, sem):
    count, width = x_ref.shape
    hg, _, w3 = o_ref.shape
    lw = w3 // 3
    frames = mod_ref.shape[0]
    pt = count // frames
    copies = [pltpu.make_async_copy(w_hbm.at[:, pl.ds(j * width, width)], w.at[j], sem.at[j]) for j in range(3)]
    @pl.when(pl.program_id(0) == 0)
    def _():
        for c in copies:
            c.start()
    def one(f, _):
        rows = pl.ds(pl.multiple_of(f * pt, pt), pt)
        n, _inv = stats(x_ref[rows, :].astype(F32))
        h_ref[rows, :] = (n * (1.0 + mod_ref[f, 1:2, :]) + mod_ref[f, 0:1, :]).astype(B16)
        return 0
    lax.fori_loop(0, frames, one, 0)
    step = max(256, lw)
    for j in range(3):
        @pl.when(pl.program_id(0) == 0)
        def _():
            copies[j].wait()
        for a in range(0, width, step):
            t = dot(h_ref[...], w[j, :, a:a + step], NN) + b_ref[0:1, j * width + a:j * width + a + step]
            for g in range(step // lw):
                v = t[:, g * lw:(g + 1) * lw]
                if j < 2:
                    v = rotate_lanes(v, cos_ref[...], sin_ref[...])
                o_ref[a // lw + g, :, j * lw:(j + 1) * lw] = v.astype(B16)


def qkv_forward(x, mods, w, b, cos, sin, hg, lw):
    clips, count, width = x.shape
    frames = mods.shape[1]
    one = lambda *shape: pl.BlockSpec((None,) + shape, lambda c: (c,) + (0,) * len(shape))
    same = lambda *shape: pl.BlockSpec(shape, lambda c: (0,) * len(shape))
    return pl.pallas_call(
        qkv_kernel,
        grid=(clips,),
        in_specs=[one(count, width), one(frames, 6, width), pl.BlockSpec(memory_space=pl.ANY), same(1, 3 * width), same(count, lw), same(count, lw)],
        out_specs=(one(hg, count, 3 * lw), one(count, width)),
        out_shape=(jax.ShapeDtypeStruct((clips, hg, count, 3 * lw), B16), jax.ShapeDtypeStruct((clips, count, width), B16)),
        scratch_shapes=[pltpu.VMEM((3, width, width), B16), pltpu.SemaphoreType.DMA((3,))],
        compiler_params=pltpu.CompilerParams(vmem_limit_bytes=48 << 20, dimension_semantics=("arbitrary",)),
        cost_estimate=pl.CostEstimate(flops=6 * clips * count * width * width, bytes_accessed=clips * 10 * count * width + 6 * width * width, transcendentals=0),
        name="qkv",
    )(x, mods, w, b, cos, sin)


TN = (((0,), (0,)), ((), ()))


MESH = pl.DeviceIdType.MESH


class Plane:
    def __init__(self):
        self.nf, self.nr = lax.axis_size("frame"), lax.axis_size("row")
        self.f, self.r = lax.axis_index("frame"), lax.axis_index("row")
        self.size = self.nf * self.nr
        self.me = self.f * self.nr + self.r

    def peer(self, k):
        p = lax.rem(self.me + k, self.size)
        return p, p // self.nr, lax.rem(p, self.nr)


def greet(plane, with_clips):
    barrier = pltpu.get_barrier_semaphore()
    count = plane.size - 1
    for k in range(1, plane.size):
        _, f, r = plane.peer(k)
        pl.semaphore_signal(barrier, inc=1, device_id={"frame": f, "row": r}, device_id_type=MESH)
    if with_clips:
        nc = lax.axis_size("clip")
        c = lax.axis_index("clip")
        for k in range(1, nc):
            pl.semaphore_signal(barrier, inc=1, device_id={"clip": lax.rem(c + k, nc)}, device_id_type=MESH)
        count += nc - 1
    pl.semaphore_wait(barrier, count)


def remote(src, dst, send, recv, device):
    return pltpu.make_async_remote_copy(src_ref=src, dst_ref=dst, send_sem=send, recv_sem=recv, device_id=device, device_id_type=MESH)


def send_blocks(plane, i, a, buf, out, send, recv, local):
    fl = buf.shape[3]
    fh, at = 2 * a // fl, lax.rem(2 * a, fl)
    for r in range(plane.nr):
        src = buf.at[i, fh, r, pl.ds(at, 2)]
        dst = out.at[i, plane.me, pl.ds(at, 2)]
        own = jnp.logical_and(fh == plane.f, r == plane.r)
        dest = fh * plane.nr + r
        k = lax.rem(dest - plane.me + plane.size, plane.size)
        @pl.when(own)
        def _():
            pltpu.make_async_copy(src, dst, local.at[i]).start()
        @pl.when(jnp.logical_not(own))
        def _():
            remote(src, dst, send.at[i, k], recv.at[i, k], {"frame": fh, "row": r}).start()


def wait_blocks(plane, calls, buf, out, send, recv, local):
    for i in range(calls):
        pltpu.make_async_copy(buf.at[i, plane.f, plane.r], out.at[i, plane.me], local.at[i]).wait()
        for k in range(1, plane.size):
            p, f, r = plane.peer(k)
            copy = remote(buf.at[i, f, r], out.at[i, plane.me], send.at[i, k], recv.at[i, k], {"frame": f, "row": r})
            copy.wait_send()
            copy.wait_recv()


def fwd_all_kernel(*refs, calls):
    plane = Plane()
    x_send, x_out, a_out, ot_ref, lse_ref = refs[:5]
    xv, ob, qm, kf, vt, sa, sb, acc, ma, mb, xs, xr, xl, os, orr, ol, save = refs[5:]
    greet(plane, False)
    for i in range(calls):
        pltpu.make_async_copy(x_send.at[i, plane.me], xv.at[i, plane.f, plane.r], xl.at[i]).start()
        for k in range(1, plane.size):
            p, f, r = plane.peer(k)
            remote(x_send.at[i, p], xv.at[i, plane.f, plane.r], xs.at[i, k], xr.at[i, k], {"frame": f, "row": r}).start()

    def arrive(i, what):
        for k in range(1, plane.size):
            p, f, r = plane.peer(k)
            copy = remote(x_send.at[i, p], xv.at[i, plane.f, plane.r], xs.at[i, k], xr.at[i, k], {"frame": f, "row": r})
            copy.wait_recv() if what else copy.wait_send()

    def call(i, _):
        pltpu.make_async_copy(x_send.at[i, plane.me], xv.at[i, plane.f, plane.r], xl.at[i]).wait()
        arrive(i, True)
        pltpu.make_async_copy(xv.at[i], x_out.at[i], save.at[i]).start()
        flash_forward(xv.at[i], ob.at[i], ot_ref.at[i], lse_ref.at[i], qm, kf, vt, sa, sb, acc, ma, mb,
                      lambda a: send_blocks(plane, i, a, ob, a_out, os, orr, ol))
        return 0
    lax.fori_loop(0, calls, call, 0)
    for i in range(calls):
        arrive(i, False)
        pltpu.make_async_copy(xv.at[i], x_out.at[i], save.at[i]).wait()
    wait_blocks(plane, calls, ob, a_out, os, orr, ol)


def attention_forward(sends, lead, lw):
    calls = sends.shape[0]
    nf, nr, fl, pt = lead
    group = nf * nr
    nh = lw // HD
    seq = nf * nr * fl * pt
    blk = 2 * nr * pt
    hbm, vmem = pl.BlockSpec(memory_space=pl.ANY), pl.BlockSpec(memory_space=pltpu.VMEM)
    s, v, dma = jax.ShapeDtypeStruct, pltpu.VMEM, pltpu.SemaphoreType.DMA
    return pl.pallas_call(
        functools.partial(fwd_all_kernel, calls=calls),
        in_specs=[hbm],
        out_specs=(hbm, hbm, vmem, vmem),
        out_shape=(s((calls,) + lead + (3 * lw,), B16), s((calls, group, fl, pt, lw), B16),
                   s((calls, lw, seq), F32), s((calls, nh, seq), F32)),
        scratch_shapes=[v((calls,) + lead + (3 * lw,), B16), v((calls,) + lead + (lw,), B16), v((nh, seq, lw), B16),
                        v((seq, lw), B16), v((lw, seq), B16), v((seq, blk), F32), v((seq, blk), F32), v((lw, blk), F32), v((1, blk), F32), v((1, blk), F32),
                        dma((calls, group)), dma((calls, group)), dma((calls,)), dma((calls, group)), dma((calls, group)),
                        dma((calls,)), dma((calls,))],
        compiler_params=pltpu.CompilerParams(vmem_limit_bytes=56 << 20, collective_id=0, has_side_effects=True),
        cost_estimate=pl.CostEstimate(flops=calls * seq * seq * lw * 2, bytes_accessed=calls * seq * lw * 24, transcendentals=calls * seq * seq * nh // 2),
        name="attention_forward",
    )(sends)


class Sum:
    def __init__(self, plane, plane_first, part, out, cols, out_cols, v1, s1, v2, s2, v3, sems):
        self.plane, self.plane_first, self.part, self.out = plane, plane_first, part, out
        self.cols, self.out_cols = cols, out_cols
        self.v1, self.s1, self.v2, self.s2, self.v3, self.sems = v1, s1, v2, s2, v3, sems
        self.bit = lax.rem(plane.r, 2)

    def place(self, stage):
        plane = self.plane
        if (stage == 1) == self.plane_first:
            half = plane.nr // 2
            return plane.nf * half, plane.f * half + plane.r // 2, lambda p: {"frame": p // half, "row": lax.rem(p, half) * 2 + self.bit}
        return lax.axis_size("clip"), lax.axis_index("clip"), lambda p: {"clip": p}

    def block(self, stage, p):
        if stage == 2:
            return self.s1.at[p]
        cols = pl.ds(*self.cols)
        return self.part.at[:, p, :, cols] if self.plane_first else self.part.at[p, :, :, cols]

    def copies(self, stage):
        count, me, device = self.place(stage)
        dst = self.v1 if stage == 1 else self.v2
        base = 0 if stage == 1 else self.v1.shape[0]
        out = []
        for k in range(1, count):
            p = lax.rem(me + k, count)
            out.append(remote(self.block(stage, p), dst.at[me], self.sems.at[0, base + k], self.sems.at[1, base + k], device(p)))
        return out, pltpu.make_async_copy(self.block(stage, me), dst.at[me], self.sems.at[0, base])

    def fetch(self):
        return pltpu.make_async_copy(self.part, self.v1, self.sems.at[0, 0])

    def start(self, stage):
        copies, own = self.copies(stage)
        for c in copies:
            c.start()
        own.start()

    def wait(self, stage):
        copies, own = self.copies(stage)
        for c in copies:
            c.wait()
        own.wait()

    def middle(self):
        def one(j, _):
            total = self.v1[0, j].astype(F32)
            for c in range(1, self.v1.shape[0]):
                total = total + self.v1[c, j].astype(F32)
            self.s1[j] = total.astype(B16)
            return 0
        lax.fori_loop(0, self.s1.shape[0], one, 0)
        self.start(2)

    def third(self):
        return remote(self.s2.at[1 - self.bit], self.v3, self.sems.at[0, self.sems.shape[1] - 1], self.sems.at[1, self.sems.shape[1] - 1],
                      {"row": self.plane.r + 1 - 2 * self.bit})

    def place_columns(self, b, value):
        size = self.unit
        for k in range(self.cols[1] // size):
            to = self.where(b, (self.at + k * size) // size)
            self.out[:, to:to + size] = value[:, k * size:(k + 1) * size]

    def last(self):
        total = self.v2[0].astype(F32)
        for c in range(1, self.v2.shape[0]):
            total = total + self.v2[c].astype(F32)
        per = self.s2.shape[1]
        self.s2[0] = total[:per]
        self.s2[1] = total[per:]
        self.third().start()
        for b in range(2):
            @pl.when(self.bit == b)
            def _():
                self.place_columns(b, self.s2[b])

    def close(self):
        self.third().wait()
        for b in range(2):
            @pl.when(self.bit == b)
            def _():
                self.place_columns(1 - b, self.v3[...])


def sum_plan(parts, orders):
    scratch, outs, jobs = [], {}, []
    for n, (part, (o, half, arrived, pieces, unit, where)) in enumerate(zip(parts, orders)):
        two = part.shape[2]
        outs[o] = jax.ShapeDtypeStruct((two // 2, 2 * half), F32)
        for plane_first, first, cols, at in pieces:
            n1, n2 = part.shape[:2]
            if plane_first and not arrived:
                n1, n2 = n2, n1
            scratch += [pltpu.VMEM((n1, n2, two, cols), B16), pltpu.VMEM((n2, two, cols), B16), pltpu.VMEM((n2, two, cols), B16),
                        pltpu.VMEM((2, two // 2, cols), F32), pltpu.VMEM((two // 2, cols), F32),
                        pltpu.SemaphoreType.DMA((2, n1 + n2 + 1))]
            jobs.append((n, o, half, arrived, plane_first, first, cols, at, unit, where))
    return scratch, [outs[o] for o in sorted(outs)], jobs


def make_sums(plane, jobs, parts, outs, scratch):
    sums = []
    for i, (n, o, half, arrived, plane_first, first, cols, at, unit, where) in enumerate(jobs):
        s = Sum(plane, plane_first, parts[n], outs[o], (first, cols), half, *scratch[6 * i:6 * i + 6])
        s.at, s.arrived, s.unit, s.where = at, arrived, unit, where
        sums.append(s)
    return sums


def bwd_all_kernel(*refs, calls, count, outputs, jobs):
    plane = Plane()
    x_in, go_in, ot_in, lse_ref, cos_ref, sin_ref = refs[:6]
    go_send = refs[6:5 + calls]
    at = 5 + calls
    parts = refs[at:at + count]
    at += count
    gq_out, gkv_out = refs[at:at + 2]
    outs = refs[at + 2:at + 2 + outputs]
    at += 2 + outputs
    xv, gov, otv, gqb, gkb, qm, dom, kf, vf, kt, delta, dqt, dka, dva, loads, gs, gr, gl, qs, qr, ql, xs, xr, xl = refs[at:at + 24]
    sums = make_sums(plane, jobs, parts, outs, refs[at + 24:])
    greet(plane, True)
    load = [pltpu.make_async_copy(go_in, gov.at[0], gl.at[0])]
    for i in range(calls):
        load += [pltpu.make_async_copy(x_in.at[i], xv.at[i], loads.at[0, i]), pltpu.make_async_copy(ot_in.at[i], otv.at[i], loads.at[1, i])]
    for c in load:
        c.start()
    def go_copy(i, k, src):
        p, f, r = plane.peer(k)
        return remote(src.at[p], gov.at[i, plane.f, plane.r], gs.at[i, k], gr.at[i, k], {"frame": f, "row": r})
    for i in range(1, calls):
        pltpu.make_async_copy(go_send[i - 1].at[plane.me], gov.at[i, plane.f, plane.r], gl.at[i]).start()
        for k in range(1, plane.size):
            go_copy(i, k, go_send[i - 1]).start()
    early = [s for s in sums if s.arrived]
    late = [s for s in sums if not s.arrived]
    for s in late:
        s.start(1)
    for s in early:
        s.fetch().start()

    def call(i, _):
        pltpu.make_async_copy(x_in.at[i], xv.at[i], loads.at[0, i]).wait()
        pltpu.make_async_copy(ot_in.at[i], otv.at[i], loads.at[1, i]).wait()
        if calls > 1:
            @pl.when(i > 0)
            def _():
                pltpu.make_async_copy(go_send[0].at[plane.me], gov.at[i, plane.f, plane.r], gl.at[i]).wait()
                for k in range(1, plane.size):
                    go_copy(i, k, go_send[0]).wait_recv()
        @pl.when(i == 0)
        def _():
            pltpu.make_async_copy(go_in, gov.at[0], gl.at[0]).wait()
        def done_q(a):
            send_blocks(plane, i, a, gqb, gq_out, qs, qr, ql)
        def done_kv(t, b):
            send_blocks(plane, i, b, gkb, gkv_out, xs, xr, xl)
            at = lambda call_, step_: pl.when(jnp.logical_and(i == call_, t == step_))
            last_call = calls - 1
            @at(0, 0)
            def _():
                for s in early:
                    s.fetch().wait()
                    s.middle()
            @at(0, 7 if last_call else 3)
            def _():
                for s in late:
                    if s.plane_first:
                        s.wait(1)
                        s.middle()
            @at(last_call, 4)
            def _():
                for s in early:
                    s.wait(2)
                    s.last()
                for s in late:
                    if not s.plane_first:
                        s.wait(1)
                        s.middle()
            @at(last_call, 6)
            def _():
                for s in late:
                    if s.plane_first:
                        s.wait(2)
                        s.last()
        flash_backward(xv.at[i], gov.at[i], otv.at[i], lse_ref.at[i], cos_ref, sin_ref, gqb.at[i], gkb.at[i],
                       qm, dom, kf, vf, kt, delta, dqt, dka, dva, done_q, done_kv)
        return 0
    lax.fori_loop(0, calls, call, 0)
    for i in range(1, calls):
        for k in range(1, plane.size):
            go_copy(i, k, go_send[i - 1]).wait_send()
    for s in late:
        if not s.plane_first:
            s.wait(2)
            s.last()
    for s in sums:
        s.close()
    wait_blocks(plane, calls, gqb, gq_out, qs, qr, ql)
    wait_blocks(plane, calls, gkb, gkv_out, xs, xr, xl)


def attention_backward(x, go, go_sends, ot, lse, cos, sin, parts, orders):
    calls, nf, nr, fl, pt, w3 = x.shape
    lead = (nf, nr, fl, pt)
    lw = w3 // 3
    group = nf * nr
    nh = lw // HD
    seq = nf * nr * fl * pt
    blk = 2 * nr * pt
    hbm, vmem = pl.BlockSpec(memory_space=pl.ANY), pl.BlockSpec(memory_space=pltpu.VMEM)
    s, v, dma = jax.ShapeDtypeStruct, pltpu.VMEM, pltpu.SemaphoreType.DMA
    scratch, outs, jobs = sum_plan(parts, orders)
    return pl.pallas_call(
        functools.partial(bwd_all_kernel, calls=calls, count=len(parts), outputs=len(outs), jobs=jobs),
        in_specs=[hbm, hbm, hbm, vmem, vmem, vmem] + [hbm] * (len(go_sends) + len(parts)),
        out_specs=[hbm, hbm] + [vmem] * len(outs),
        out_shape=[s((calls, group, fl, pt, lw), B16), s((calls, group, fl, pt, 2 * lw), B16)] + outs,
        scratch_shapes=[v((calls,) + lead + (w3,), B16), v((calls,) + lead + (lw,), B16), v((calls, lw, seq), F32), v((calls,) + lead + (lw,), B16), v((calls,) + lead + (2 * lw,), B16),
                        v((nh, seq, lw), B16), v((nh, seq, lw), B16), v((seq, lw), B16), v((seq, lw), B16), v((lw, seq), B16),
                        v((nh, seq), F32), v((lw, seq), F32), v((blk, lw), F32), v((blk, lw), F32),
                        dma((2, calls)), dma((calls, group)), dma((calls, group)), dma((calls,)), dma((calls, group)), dma((calls, group)), dma((calls,)), dma((calls, group)), dma((calls, group)), dma((calls,))] + scratch,
        compiler_params=pltpu.CompilerParams(vmem_limit_bytes=61 << 20, collective_id=1, has_side_effects=True),
        cost_estimate=pl.CostEstimate(flops=calls * seq * seq * lw * 5, bytes_accessed=calls * seq * lw * 48, transcendentals=calls * seq * seq * nh // 2),
        name="attention_backward",
    )(x, go, ot, lse, cos, sin, *go_sends, *parts)


def mlp_kernel(a_ref, x_hbm, g_hbm, mod_ref, wo_ref, bo_ref, wu_ref, bu_ref, wd_ref, bd_ref,
               y_out, gm_out, ga_out, go_out, pd_out, ugot, vgot, pu_out, po_out, sums_ref, du_ref, db_ref,
               g, an, branch, mixed, h, gd, down, gh, st, gav, sd, su, rd, ru, kd, ku, pd, pu, *sems, calls):
    io, od, pair, free, done, gs, gr, gl, oo, us, ur, vr = sems
    plane = Plane()
    nc, mc = lax.axis_size("clip"), lax.axis_index("clip")
    half_row = plane.nr // 2
    places, mp = plane.nf * half_row, plane.f * half_row + plane.r // 2
    at_place = lambda p: {"frame": p // half_row, "row": lax.rem(p, half_row) * 2 + bit}
    bit = lax.rem(plane.r, 2)
    clip_first = ugot.shape[3] // (wu_ref.shape[1] // 2)
    partner = {"row": plane.r + 1 - 2 * bit}
    clips, hg, count, lw = a_ref.shape
    width = an.shape[1]
    frames = mod_ref.shape[0]
    pt = clips * count // frames
    step, steps = pl.program_id(0), pl.num_programs(0)
    fc = wu_ref.shape[1]
    slots = rd.shape[0]
    hw, hf = width // 2, fc // 2

    def each(first, last, fn):
        def one(f, _):
            fn(f, pl.ds(pl.multiple_of(f * pt, pt), pt))
            return 0
        lax.fori_loop(first, last, one, 0)

    def split(value, size, send, keep):
        for b in range(2):
            @pl.when(bit == b)
            def _():
                send[...] = value[:, (1 - b) * size:(2 - b) * size].astype(B16)
                keep[...] = value[:, b * size:(b + 1) * size]

    @pl.when(step == 0)
    def _():
        loads = [pltpu.make_async_copy(x_hbm, h, io.at[0]), pltpu.make_async_copy(g_hbm, g.at[pl.ds(0, clips * count)], io.at[1])]
        for c in loads:
            c.start()
        greet(plane, True)
        for c in range(clips):
            for i in range(hg):
                an[c * count:(c + 1) * count, i * lw:(i + 1) * lw] = a_ref[c, i]
        branch[...] = dot(an[:clips * count, :], wo_ref[...], NN) + bo_ref[...]
        for c in loads:
            c.wait()
        def fn(f, rows):
            m = h[rows, :].astype(F32) + mod_ref[f, 2:3, :] * branch[rows, :]
            mean = jnp.mean(m, axis=1, keepdims=True)
            centre = m - mean
            inv = lax.rsqrt(jnp.mean(centre * centre, axis=1, keepdims=True) + 1e-06)
            mixed[rows, :] = m
            st[rows, :128] = jnp.broadcast_to(mean, (pt, 128))
            st[rows, 128:] = jnp.broadcast_to(inv, (pt, 128))
            h[rows, :] = (centre * inv * (1.0 + mod_ref[f, 4:5, :]) + mod_ref[f, 3:4, :]).astype(B16)
            gd[rows, :] = (g[rows, :].astype(F32) * mod_ref[f, 5:6, :]).astype(B16)
        each(0, frames, fn)
        down[...] = jnp.zeros_like(down)
        gh[...] = jnp.zeros_like(gh)

    c0 = (2.0 / 3.141592653589793) ** 0.5
    c1 = 0.044715
    wu, wd = wu_ref[...], wd_ref[...]
    wide, tall, bias = None, None, None
    for c in range(clips):
        rows = slice(c * count, (c + 1) * count)
        hr, gr_ = h[rows, :], gd[rows, :]
        pre = dot(hr, wu, NN) + bu_ref[...]
        gact = dot(gr_, wd, NT)
        sq = pre * pre
        u = jnp.tanh(pre * (c0 + (c0 * c1) * sq))
        half = 0.5 * (1.0 + u)
        act = (pre * half).astype(B16)
        slope = half + (0.5 * pre) * (1.0 - u * u) * (c0 + (3.0 * c0 * c1) * sq)
        gp = (gact * slope).astype(B16)
        down[rows, :] += dot(act, wd, NN)
        gh[rows, :] += dot(gp, wu, NT)
        d, t, b = dot(act, gr_, TN), dot(hr, gp, TN), jnp.sum(gp.astype(F32), axis=0, keepdims=True)
        wide = d if wide is None else wide + d
        tall = t if tall is None else tall + t
        bias = b if bias is None else bias + b
    du_ref[...] = bias
    now, slot = lax.rem(step, 2), lax.rem(step, slots)

    def swaps(j):
        n, s = lax.rem(j, 2), lax.rem(j, slots)
        return (remote(sd.at[n], rd.at[s], pair.at[0, n], pair.at[1, s], partner),
                remote(su.at[n], ru.at[s], pair.at[2, n], pair.at[3, s], partner))

    def onward(j, what):
        n = lax.rem(j, 2)
        def do(copy, sent):
            copy.start() if what == "start" else (copy.wait_send() if sent else copy.wait())
        do(pltpu.make_async_copy(pd.at[n], pd_out.at[pl.ds(pl.multiple_of(j * fc, fc), fc)], od.at[0, n]), False)
        @pl.when(j < clip_first)
        def _():
            cols = pl.ds(pl.multiple_of(j * hf, hf), hf)
            do(pltpu.make_async_copy(pu.at[n, mc], ugot.at[mc, :, :, cols], od.at[1, n]), False)
            for k in range(1, nc):
                c = lax.rem(mc + k, nc)
                do(remote(pu.at[n, c], ugot.at[mc, :, :, cols], us.at[n, k], ur.at[mc], {"clip": c}), True)
        tail_at = steps - pu_out.shape[3] // hf
        @pl.when(j >= tail_at)
        def _():
            cols = pl.ds(pl.multiple_of((j - tail_at) * hf, hf), hf)
            do(pltpu.make_async_copy(pu.at[n], pu_out.at[:, :, :, cols], od.at[1, n]), False)
        @pl.when(jnp.logical_and(j >= clip_first, j < tail_at))
        def _():
            cols = pl.ds(pl.multiple_of((j - clip_first) * hf, hf), hf)
            do(pltpu.make_async_copy(pu.at[n, :, mp], vgot.at[mp, :, :, cols], od.at[1, n]), False)
            for k in range(1, places):
                p = lax.rem(mp + k, places)
                do(remote(pu.at[n, :, p], vgot.at[mp, :, :, cols], us.at[n, k], vr.at[mp], at_place(p)), True)

    def finish(j):
        n, s = lax.rem(j, 2), lax.rem(j, slots)
        @pl.when(j >= 2)
        def _():
            onward(j - 2, "wait")
        for c in swaps(j):
            c.wait_recv()
        pd[n] = (kd[n] + rd[s].astype(F32)).astype(B16)
        pu[n] = (ku[n] + ru[s].astype(F32)).astype(B16).reshape(pu.shape[1:])
        onward(j, "start")
        @pl.when(j + slots < steps)
        def _():
            pl.semaphore_signal(free, inc=1, device_id=partner, device_id_type=MESH)

    @pl.when(step >= 2)
    def _():
        for c in swaps(step - 2):
            c.wait_send()
    split(wide, hw, sd.at[now], kd.at[now])
    split(tall, hf, su.at[now], ku.at[now])
    @pl.when(step >= slots)
    def _():
        pl.semaphore_wait(free, 1)
    for c in swaps(step):
        c.start()
    @pl.when(step >= 1)
    def _():
        finish(step - 1)

    @pl.when(step == steps - 1)
    def _():
        db_ref[...] = jnp.zeros_like(db_ref)
        def fn(f, rows):
            gf = g[rows, :].astype(F32)
            d = down[rows, :] + bd_ref[...]
            m = mixed[rows, :]
            ghf = gh[rows, :]
            inv = st[rows, 128:129]
            n = (m - st[rows, 0:1]) * inv
            t = ghf * (1.0 + mod_ref[f, 4:5, :])
            back = t - jnp.mean(t, axis=1, keepdims=True) - n * jnp.mean(t * n, axis=1, keepdims=True)
            gm = gf + inv * back
            gbr = (gm * mod_ref[f, 2:3, :]).astype(B16)
            s = lambda v: jnp.sum(v, axis=0, keepdims=True)
            sums_ref[f] = jnp.concatenate([s(gm * branch[rows, :]), s(ghf), s(ghf * n), s(gf * d)], axis=0)
            db_ref[...] += jnp.concatenate([s(gbr.astype(F32)), s(gd[rows, :].astype(F32))], axis=0)
            mixed[rows, :] = gm
            h[rows, :] = gbr
            gd[rows, :] = (m + mod_ref[f, 5:6, :] * d).astype(B16)
        group = plane.size
        per_call = clips // calls
        def go_copies():
            out = []
            for k in range(1, group):
                p, f, r = plane.peer(k)
                out.append(remote(gav.at[p], go_out.at[plane.f, plane.r], gs.at[k], gr.at[k], {"frame": f, "row": r}))
            return out, pltpu.make_async_copy(gav.at[plane.me], go_out.at[plane.f, plane.r], gl)
        def back_out(c):
            each(c * frames // clips, (c + 1) * frames // clips, fn)
            ga = dot(h[c * count:(c + 1) * count, :], wo_ref[...], NT).astype(B16)
            for i in range(hg):
                gav[c * hg + i] = ga[:, i * lw:(i + 1) * lw]
        for c in range(per_call):
            back_out(c)
        copies, own = go_copies()
        for c in copies:
            c.start()
        own.start()
        for c in range(per_call, clips):
            back_out(c)
        outs = [pltpu.make_async_copy(gd, y_out, oo.at[0]), pltpu.make_async_copy(mixed, gm_out, oo.at[1])]
        if calls > 1:
            outs.append(pltpu.make_async_copy(gav.at[pl.ds(group, (calls - 1) * group)], ga_out, oo.at[2]))
        for c in outs:
            c.start()
        finish(step)
        pl.semaphore_signal(done, inc=1, device_id=partner, device_id_type=MESH)
        wide_out = dot(an[:clips * count, :], h[...], TN)
        for b in range(2):
            @pl.when(bit == b)
            def _():
                an[:width, :hw] = wide_out[:, (1 - b) * hw:(2 - b) * hw].astype(B16)
                down[:width, :hw] = wide_out[:, b * hw:(b + 1) * hw]
        pl.semaphore_wait(done, 1)
        ro = g.at[pl.ds(0, width), pl.ds(0, hw)]
        last = remote(an.at[pl.ds(0, width), pl.ds(0, hw)], ro, pair.at[0, 2], pair.at[1, slots], partner)
        last.start()
        last.wait()
        an[:width, hw:] = (down[:width, :hw] + g[:width, :hw].astype(F32)).astype(B16)
        outs.append(pltpu.make_async_copy(an.at[pl.ds(0, width), pl.ds(hw, hw)], po_out, oo.at[3]))
        outs[-1].start()
        for c in copies:
            c.wait()
        own.wait()
        for c in swaps(step - 1) + swaps(step):
            c.wait_send()
        onward(step - 1, "wait")
        onward(step, "wait")
        for k in range(1, places):
            p = lax.rem(mp + k, places)
            remote(vgot.at[p], vgot.at[p], us.at[0, 0], vr.at[p], at_place(p)).wait_recv()
        for k in range(1, nc):
            c = lax.rem(mc + k, nc)
            remote(ugot.at[c], ugot.at[c], us.at[0, 0], ur.at[c], {"clip": c}).wait_recv()
        for c in outs:
            c.wait()


def mlp(attn, x, g, mods, w_out, b_out, w_up, b_up, w_down, b_down, calls, lead):
    clips, hg, count, lw = attn.shape
    rows, width = x.shape
    ff = w_up.shape[1]
    frames = mods.shape[0]
    fc = min(512, ff)
    hw, hf = width // 2, fc // 2
    nf, nr = lead[:2]
    group = nf * nr
    slots = 3
    nc = lax.axis_size("clip")
    places, steps = group // 2, ff // fc
    clip_first = max(1, steps // 4)
    two_u = width // (nc * places)
    tall = max(rows, width)
    whole = lambda *shape: pl.BlockSpec(shape, lambda j: (0,) * len(shape), pipeline_mode=pl.Buffered(1))
    keep = lambda *shape: pl.BlockSpec(shape, lambda j: (0,) * len(shape))
    hbm = pl.BlockSpec(memory_space=pl.ANY)
    s, v, dma = jax.ShapeDtypeStruct, pltpu.VMEM, pltpu.SemaphoreType.DMA
    return pl.pallas_call(
        functools.partial(mlp_kernel, calls=calls),
        grid=(ff // fc,),
        in_specs=[whole(clips, hg, count, lw), hbm, hbm, whole(frames, 6, width), whole(width, width), whole(1, width),
                  pl.BlockSpec((width, fc), lambda j: (0, j)), pl.BlockSpec((1, fc), lambda j: (0, j)),
                  pl.BlockSpec((fc, width), lambda j: (j, 0)), whole(1, width)],
        out_specs=[hbm] * 9 + [keep(frames, 4, width), pl.BlockSpec((1, fc), lambda j: (0, j)), keep(2, width)],
        out_shape=[s((rows, width), B16), s((rows, width), F32), s((max(1, calls - 1) * group, count, lw), B16),
                   s((nf, nr, count, lw), B16), s((ff, hw), B16), s((nc, places, two_u, clip_first * hf), B16), s((places, nc, two_u, (steps - clip_first - 2) * hf), B16), s((nc, places, two_u, 2 * hf), B16), s((width, hw), B16),
                   s((frames, 4, width), F32), s((1, ff), F32), s((2, width), F32)],
        scratch_shapes=[v((tall, width), B16), v((tall, width), B16), v((rows, width), F32), v((rows, width), F32),
                        v((rows, width), B16), v((rows, width), B16), v((tall, width), F32), v((rows, width), F32), v((rows, 256), F32),
                        v((clips * hg, count, lw), B16), v((2, fc, hw), B16), v((2, width, hf), B16), v((slots, fc, hw), B16),
                        v((slots, width, hf), B16), v((2, fc, hw), F32), v((2, width, hf), F32), v((2, fc, hw), B16), v((2, nc, places, two_u, hf), B16),
                        dma((2,)), dma((2, 2)), dma((4, slots + 1)), pltpu.SemaphoreType.REGULAR, pltpu.SemaphoreType.REGULAR,
                        dma((group,)), dma((group,)), dma, dma((4,)), dma((2, max(places, nc))), dma((nc,)), dma((places,))],
        compiler_params=pltpu.CompilerParams(vmem_limit_bytes=63 << 20, dimension_semantics=("arbitrary",), collective_id=3, has_side_effects=True),
        cost_estimate=pl.CostEstimate(flops=2 * rows * width * (3 * width + 6 * ff), bytes_accessed=8 * width * ff + 20 * rows * width, transcendentals=rows * ff),
        name="mlp",
    )(attn, x, g, mods, w_out, b_out, w_up, b_up, w_down, b_down)


def tail_kernel(gq_hbm, gkv_hbm, h_hbm, w_hbm, x_hbm, gm_hbm, y_hbm, mod_ref, clean_ref, sums2_ref, vec_ref,
                o_out, y_out, gw_ref, noise_ref, vec_out,
                gq, gkv, h, w, x, gm, yv, ob, yb, full, gh, send, got, part, s1s, dbq, nsend, nrecv, vsend, v1, vmid, v2, io, pair, nsem, vsem, oo, *scratch, jobs):
    plane = Plane()
    clips, hg, count, lw = gq_hbm.shape
    w3 = 3 * lw
    width = w.shape[0]
    frames = mod_ref.shape[0] // clips
    pt = count // frames
    nc, nf, nr = lax.axis_size("clip"), plane.nf, plane.nr
    group = plane.size
    bit = lax.rem(plane.r, 2)
    partner = {"row": plane.r + 1 - 2 * bit}
    packed = max(1, 128 * 3 // w3)
    blocks = hg // 2 // packed
    bw = packed * w3
    loads = [pltpu.make_async_copy(gq_hbm, gq, io.at[0]), pltpu.make_async_copy(gkv_hbm, gkv, io.at[5]), pltpu.make_async_copy(h_hbm, h, io.at[1]),
             pltpu.make_async_copy(w_hbm, w, io.at[2]), pltpu.make_async_copy(x_hbm, x, io.at[3]), pltpu.make_async_copy(gm_hbm, gm, io.at[4]), pltpu.make_async_copy(y_hbm, yv, io.at[6])]
    for c in loads:
        c.start()
    sums = make_sums(plane, jobs, [part], [gw_ref], scratch)
    greet(plane, True)
    for c in loads[:3]:
        c.wait()

    def outer(j):
        total = None
        for c in range(clips):
            b = jnp.concatenate([v[c, j * packed + i] for i in range(packed) for v in (gq, gkv)], axis=1)
            t = dot(h[c], b, TN)
            total = t if total is None else total + t
        return total

    def swap(j):
        return remote(send.at[j], got.at[j], pair.at[0, j], pair.at[1, j], partner)
    other = 1 - bit
    def block(n, _):
        @pl.when(n < blocks)
        def _():
            send[n] = outer(other * blocks + n).astype(B16)
            swap(n).start()
        @pl.when(n > 0)
        def _():
            j = n - 1
            total = outer(bit * blocks + j)
            swap(j).wait_recv()
            total = (total + got[j].astype(F32)).astype(B16)
            part[:, :, :, pl.ds(pl.multiple_of(j * bw, 128), bw)] = total.reshape(part.shape[:3] + (bw,))
            for k, s in enumerate(sums):
                @pl.when(j == k)
                def _():
                    s.start(1)
        return 0
    lax.fori_loop(0, blocks + 1, block, 0)

    for c in loads[3:]:
        c.wait()
    dbq[...] = jnp.zeros_like(dbq)
    def clip_back(c, _):
        for g in range(hg):
            full[:, g * lw:(g + 1) * lw] = gq[c, g]
            for j in range(2):
                full[:, (j + 1) * width + g * lw:(j + 1) * width + (g + 1) * lw] = gkv[c, g, :, j * lw:(j + 1) * lw]
        gh[...] = dot(full[...], w[...], NT)
        dbq[...] += jnp.sum(full[...].astype(F32), axis=0, keepdims=True)
        def one(f, _):
            rows = pl.ds(pl.multiple_of(f * pt, pt), pt)
            cf = c * frames + f
            n, inv = stats(x[c, rows, :].astype(F32))
            ghf = gh[rows, :]
            t = ghf * (1.0 + mod_ref[cf, 1:2, :])
            back = t - jnp.mean(t, axis=1, keepdims=True) - n * jnp.mean(t * n, axis=1, keepdims=True)
            new, out = gm[c, rows, :] + inv * back, yv[c, rows, :]
            for m in range(clips):
                @pl.when(c == m)
                def _():
                    ob[f, :, m, :] = new
                    yb[f, :, m, :] = out
            s = lambda v: jnp.sum(v, axis=0, keepdims=True)
            s1s[cf, 0:2, :] = jnp.concatenate([s(ghf), s(ghf * n)], axis=0)
            s1s[cf, 2:6, :] = sums2_ref[cf]
            return 0
        lax.fori_loop(0, frames, one, 0)
        for n in range(clips):
            @pl.when(c == n)
            def _():
                for s in (sums[1:2] if n < clips - 1 else sums[2 if clips > 1 else 1:3]):
                    s.wait(1)
                    s.middle()
        return 0
    lax.fori_loop(0, clips, clip_back, 0)

    results = [pltpu.make_async_copy(ob, o_out, oo.at[0]), pltpu.make_async_copy(yb, y_out, oo.at[1])]
    for c in results:
        c.start()

    quarter = width // nr
    vsend[...] = jnp.zeros_like(vsend)
    def gather(cf, total):
        both = s1s[cf, 0:6, :]
        keep = clean_ref[cf]
        noise = jnp.where(keep > 0.5, jnp.zeros_like(both), both)
        for q in range(nr):
            nsend[q, cf] = noise[:, q * quarter:(q + 1) * quarter].astype(B16)
        return total + (both - noise)
    clean_sum = lax.fori_loop(0, clips * frames, gather, jnp.zeros((6, width), F32))
    def ncopies():
        out = []
        for k in range(1, nr):
            q = lax.rem(plane.r + k, nr)
            out.append(remote(nsend.at[q], nrecv.at[plane.r], nsem.at[0, k], nsem.at[1, k], {"row": q}))
        return out
    for c in ncopies():
        c.start()
    vsend[:6, :] = clean_sum
    vsend[6:9, :] = jnp.concatenate([dbq[:, j * width:(j + 1) * width] for j in range(3)], axis=0)
    vsend[9:9 + vec_ref.shape[0], :] = vec_ref[...]
    def vcopies(stage):
        out = []
        if stage == 1:
            for k in range(1, group):
                p, f, r = plane.peer(k)
                out.append(remote(vsend, v1.at[plane.me], vsem.at[0, k], vsem.at[1, k], {"frame": f, "row": r}))
        else:
            c = lax.axis_index("clip")
            for k in range(1, nc):
                out.append(remote(vmid, v2.at[c], vsem.at[0, group + k], vsem.at[1, group + k], {"clip": lax.rem(c + k, nc)}))
        return out
    for c in vcopies(1):
        c.start()
    for s in sums[:1] + sums[3:]:
        s.wait(1)
        s.middle()
    for c in vcopies(1):
        c.wait()
    total = vsend[...]
    for k in range(1, group):
        p, _, _ = plane.peer(k)
        total = total + v1[p]
    vmid[...] = total
    for c in vcopies(2):
        c.start()
    for c in ncopies():
        c.wait()
    def add_noise(cf, _):
        total = nsend[plane.r, cf].astype(F32)
        for k in range(1, nr):
            total = total + nrecv[lax.rem(plane.r + k, nr), cf].astype(F32)
        noise_ref[lax.rem(cf, frames), cf // frames] = total
        return 0
    lax.fori_loop(0, clips * frames, add_noise, 0)
    for s in sums:
        s.wait(2)
        s.last()
    for c in vcopies(2):
        c.wait()
    total = vmid[...]
    for k in range(1, nc):
        total = total + v2[lax.rem(lax.axis_index("clip") + k, nc)]
    vec_out[...] = total
    for s in sums:
        s.close()
    for j in range(blocks):
        swap(j).wait_send()
    for c in results:
        c.wait()


def tail(gq, gkv, h1, w_qkv, x, gmixed, y, mods, clean, sums2, vec):
    clips, hg, count, lw = gq.shape
    w3 = 3 * lw
    width = x.shape[2]
    nc, nf, nr = (lax.axis_size(a) for a in ALL)
    group = nf * nr
    frames = mods.shape[0]
    fl, pt = frames // clips, count // (frames // clips)
    two = width // (nc * nf * nr // 2)
    packed = max(1, 128 * 3 // w3)
    blocks, bw = hg // 2 // packed, packed * w3
    vrows = -(-(9 + vec.shape[0]) // 8) * 8
    hbm, vmem = pl.BlockSpec(memory_space=pl.ANY), pl.BlockSpec(memory_space=pltpu.VMEM)
    s, v, dma = jax.ShapeDtypeStruct, pltpu.VMEM, pltpu.SemaphoreType.DMA
    shape = jax.ShapeDtypeStruct((nc, nf * nr // 2, two, blocks * bw), B16)
    order = [(False if j == 0 else True, j * bw, bw, j * bw) for j in range(blocks)]
    where = lambda b, u: u % 3 * width + (b * (hg // 2) + u // 3) * lw
    scratch, outs, jobs = sum_plan([shape], [(0, blocks * bw, False, order, lw, where)])
    return pl.pallas_call(
        functools.partial(tail_kernel, jobs=jobs),
        in_specs=[hbm] * 7 + [vmem] * 4,
        out_specs=[hbm, hbm, vmem, vmem, vmem],
        out_shape=[s((fl, pt, clips, width), F32), s((fl, pt, clips, width), B16)] + outs + [s((fl, clips, 6, width // nr), F32), s((vrows, width), F32)],
        scratch_shapes=[v((clips, hg, count, lw), B16), v((clips, hg, count, 2 * lw), B16), v((clips, count, width), B16), v((width, 3 * width), B16), v((clips, count, width), B16),
                        v((clips, count, width), F32), v((clips, count, width), B16), v((fl, pt, clips, width), F32), v((fl, pt, clips, width), B16), v((count, 3 * width), B16), v((count, width), F32), v((blocks, width, bw), B16),
                        v((blocks, width, bw), B16), v(shape.shape, B16), v((frames, 8, width), F32), v((1, 3 * width), F32),
                        v((nr, frames, 6, width // nr), B16), v((nr, frames, 6, width // nr), B16), v((vrows, width), F32), v((group, vrows, width), F32),
                        v((vrows, width), F32), v((nc, vrows, width), F32), dma((7,)), dma((2, blocks)), dma((2, nr)), dma((2, group + nc)), dma((2,))] + scratch,
        compiler_params=pltpu.CompilerParams(vmem_limit_bytes=62 << 20, collective_id=2, has_side_effects=True),
        cost_estimate=pl.CostEstimate(flops=12 * clips * count * width * width, bytes_accessed=40 * clips * count * width, transcendentals=0),
        name="tail",
    )(gq, gkv, h1, w_qkv, x, gmixed, y, mods, clean, sums2, vec)


def head_tables(frames, grid):
    pair = jnp.arange(32)[:, None]
    is_time = pair < 8
    is_height = (pair >= 8) & (pair < 20)
    exponent = jnp.where(is_time, pair / 8.0, jnp.where(is_height, (pair - 8) / 12.0, (pair - 20) / 12.0)).astype(F32)
    frequency = jnp.power(F32(10000.0), -exponent)
    count = max(frames, grid)
    angle = frequency * jnp.arange(count).astype(F32)[None, :]
    token = jnp.arange(frames * grid * grid)[None, :]
    position = jnp.where(is_time, token // (grid * grid), jnp.where(is_height, token // grid % grid, token % grid))
    def spread(table):
        out = jnp.broadcast_to(table[:, :1], position.shape)
        for n in range(1, count):
            out = jnp.where(position == n, table[:, n:n + 1], out)
        return out
    return spread(jnp.cos(angle)), spread(jnp.sin(angle))


def on_device(tokens, context, noise_mod, clean_mod, w_qkv, b_qkv, w_out, b_out, w_up, b_up, w_down, b_down, cotangent):
    frames, patches, clips, width = tokens.shape
    count = frames * patches
    heads = width // HD
    nf, nr = lax.axis_size("frame"), lax.axis_size("row")
    group = nf * nr
    nh = max(1, heads // group)
    lw = nh * HD
    hg = heads // nh
    cs = group // hg
    calls = clips // cs
    grid = round((patches * nr) ** 0.5)
    fi, ri = lax.axis_index("frame"), lax.axis_index("row")

    is_clean = (fi * frames + jnp.arange(frames))[None, :] < context[:, None]
    mods = jnp.where(is_clean[:, :, None, None], clean_mod[None, None], noise_mod.transpose(1, 0, 2, 3))
    inputs = tokens.transpose(2, 0, 1, 3).reshape(clips, count, width)
    cots = cotangent.transpose(2, 0, 1, 3).reshape(clips, count, width)

    tok = jnp.arange(count)
    cos, sin = rope_angles(fi * frames + tok // patches, ri * patches + tok % patches, grid)
    cos_l = jnp.tile(jnp.concatenate([cos, cos], axis=1), (1, nh))
    sin_l = jnp.tile(jnp.concatenate([-sin, sin], axis=1), (1, nh))
    cos_t, sin_t = head_tables(nf * frames, grid)
    row_of = lambda v: v.reshape(1, -1)

    lead = (nf, nr, frames, patches)
    sends, h1 = qkv_forward(inputs, mods, w_qkv, row_of(b_qkv), cos_l, sin_l, hg, lw)
    x, attn, ot, lse = attention_forward(sends.reshape(calls, group, frames, patches, 3 * lw), lead, lw)
    attn = attn.reshape(clips, hg, count, lw)

    rows = clips * count
    by_frame = mods.reshape(clips * frames, 6, width)
    y, gmixed, ga, go, part_down, got_up, got_up2, part_up, part_out, sums2, db_up, db_two = mlp(
        attn, inputs.reshape(rows, width), cots.reshape(rows, width), by_frame,
        w_out, row_of(b_out), w_up, row_of(b_up), w_down, row_of(b_down), calls, lead)
    go = go.reshape(lead + (lw,))
    go_sends = [v for v in ga.reshape((-1, group, frames, patches, lw))][:calls - 1]
    gmixed = gmixed.reshape(clips, count, width)

    nc = lax.axis_size("clip")
    places = group // 2
    first, second, hw = got_up.shape[3], got_up2.shape[3], width // 2
    as_blocks = lambda p: p.reshape(nc, places, p.shape[0] // (nc * places), p.shape[1])
    parts = [as_blocks(part_down), got_up, got_up2, part_up, as_blocks(part_out)]
    third, unit = part_up.shape[3], part_up.shape[3] // 2
    half_up = first + second + third
    by_half = lambda b, u: b * hw + u * (hw // 2)
    by_chunk = lambda b, u: (2 * u + b) * unit
    orders = [(0, hw, False, [(False, 0, hw // 2, 0), (True, hw // 2, hw // 2, hw // 2)], hw // 2, by_half),
              (1, half_up, True, [(False, 0, first, 0)], unit, by_chunk),
              (1, half_up, True, [(True, 0, second, first)], unit, by_chunk),
              (1, half_up, False, [(True, 0, third, first + second)], unit, by_chunk),
              (2, hw, False, [(False, 0, hw, 0)], hw // 2, by_half)]
    gq, gkv, gw_down, gw_up, gw_out = attention_backward(x, go, go_sends, ot, lse, cos_t, sin_t, parts, orders)
    gq, gkv = gq.reshape(clips, hg, count, lw), gkv.reshape(clips, hg, count, 2 * lw)
    clean = jnp.broadcast_to(is_clean.reshape(-1, 1, 1), (clips * frames, 1, width)).astype(F32)
    vec = jnp.concatenate([db_up.reshape(-1, width), db_two], axis=0)
    gtokens, output, gw_qkv, noise, vec = tail(gq, gkv, h1, w_qkv, inputs, gmixed, y.reshape(clips, count, width), by_frame, clean, sums2, vec)
    total = lax.axis_size(ALL)
    place = lax.axis_index(ALL)
    def own(at, size):
        return lax.dynamic_slice_in_dim(vec[at:at + size].reshape(-1), place * (size * width // total), size * width // total)
    grad_clean = lax.dynamic_slice_in_dim(vec[:6], place * (width // total), width // total, 1)
    ff = w_up.shape[1] // width
    gb_qkv, gb_up, gb_out, gb_down = own(6, 3), own(9, ff), own(9 + ff, 1), own(10 + ff, 1)
    return (output, gtokens, noise, grad_clean, gw_qkv, gb_qkv, gw_out, gb_out, gw_up, gb_up, gw_down, gb_down)


def solution(mesh):
    token = P("frame", "row", "clip", None)
    rows = P(ALL, None)
    return jax.shard_map(
        on_device,
        mesh=mesh,
        in_specs=(token, P("clip"), P("frame", "clip", None, None)) + (P(),) * 9 + (token,),
        out_specs=(token, token, P("frame", "clip", None, "row"), P(None, ALL), rows, P(ALL), rows, P(ALL), rows, P(ALL), rows, P(ALL)),
        check_vma=False,
    )
```
